256 devices in a mesh: gx: 32 (over x, z), gy: 8 (over y, core).
Axes of the slice: x: 4, y: 4, z: 8, core: 2. Of those that a mesh axis runs over, the one named last changes fastest.
Arguments:
- scalar: float32 [8, 4096, 2048], P(None, 'gx', 'gy'), may hold values from -6 to 6
- diffusivity: float32 [8, 4096, 2048], P(None, 'gx', 'gy'), may hold values from 0.1 to 1
Outputs:
- grad_x: float32 [8, 4096, 2048], P(None, 'gx', 'gy')
- grad_y: float32 [8, 4096, 2048], P(None, 'gx', 'gy')
- diffusion: float32 [8, 4096, 2048], P(None, 'gx', 'gy')
The draws below stay inside these ranges and needn't reach their ends.
All inputs are finite; a program needn't handle non-finite values.
Results may differ from the reference program's by a relative error of at most 0.000075.
Values sent between devices are 32-bit elements; how exact they have to be, the bound alone decides.
A program may use at most 128 MiB of HBM per device.

```python
import math
import jax
import jax.numpy as jnp
from jax import lax

P_SIZE = 8
NX = 4096
NY = 2048


def level_of(stream_key, shape, split, least, top_value):
    level = 1.0
    for dim, blocks in split:
        heights = jax.random.uniform(jax.random.fold_in(jax.random.fold_in(stream_key, 6), dim), (blocks,), jnp.float32, least / len(split), top_value / len(split))
        level = level * jnp.repeat(jnp.exp(heights), shape[dim] // blocks).reshape((-1,) + (1,) * (len(shape) - 1 - dim))
    return level


def centred(own_key, shape, width, reach, pieces=(), kind=jnp.bfloat16):
    drawn = jax.random.normal(own_key, shape, jnp.float32) * width
    if len(pieces) > 0:
        drawn = level_of(own_key, shape, pieces, -0.22, 0.18) * drawn
    return jnp.clip(drawn, min=-reach, max=reach).astype(kind)


def setup_inputs(seed: int = 0) -> dict:
    streams_of = jax.random.split(jax.random.key(seed), 3)
    return {
        "scalar": centred(streams_of[0], (P_SIZE, NX, NY), 1.0, 6.0, ((1, 32), (2, 8)), jnp.float32),
        "diffusivity": jnp.clip(jnp.exp(math.log(1.0) - 2.3025851 * jax.random.uniform(streams_of[1], (P_SIZE, NX, NY), jnp.float32) ** level_of(streams_of[1], (P_SIZE, NX, NY), ((1, 32), (2, 8)), -0.2, 0.2)), 0.1, 1.0),
    }


FIRST_ALPHA = 1.0 / 3.0
FIRST_A = 14.0 / 9.0
FIRST_B = 1.0 / 9.0
SECOND_ALPHA = 2.0 / 11.0
SECOND_A = 12.0 / 11.0
SECOND_B = 3.0 / 11.0


def symbols(cells, dtype):
    phase = (2.0 * jnp.pi / cells) * jnp.arange(cells // 2 + 1).astype(dtype)
    first = (FIRST_A * jnp.sin(phase) + 0.5 * FIRST_B * jnp.sin(2.0 * phase)) / (1.0 + 2.0 * FIRST_ALPHA * jnp.cos(phase))
    second = -(2.0 * SECOND_A * (1.0 - jnp.cos(phase)) + 0.5 * SECOND_B * (1.0 - jnp.cos(2.0 * phase))) / (1.0 + 2.0 * SECOND_ALPHA * jnp.cos(phase))
    return first, second


def along(field, axis_dim, multiplier, cells):
    spectrum = jnp.fft.rfft(field, axis=axis_dim) * multiplier
    return jnp.fft.irfft(spectrum, n=cells, axis=axis_dim).astype(field.dtype)


def reference(scalar, diffusivity):
    first_x, second_x = symbols(NX, scalar.dtype)
    first_y, second_y = symbols(NY, scalar.dtype)

    def one_plane(plane_pair):
        plane_field, plane_kappa = plane_pair
        grad_x = along(plane_field, 0, 1j * first_x[:, None], NX)
        kappa_x = along(plane_kappa, 0, 1j * first_x[:, None], NX)
        curv_x = along(plane_field, 0, second_x[:, None], NX)
        grad_y = along(plane_field, 1, 1j * first_y[None, :], NY)
        kappa_y = along(plane_kappa, 1, 1j * first_y[None, :], NY)
        curv_y = along(plane_field, 1, second_y[None, :], NY)
        result = plane_kappa * (curv_x + curv_y) + kappa_x * grad_x + kappa_y * grad_y
        return grad_x, grad_y, result

    grads_x, grads_y, diffusion = lax.map(one_plane, (scalar, diffusivity))
    return (grads_x, grads_y, diffusion)
```

```python
import functools

import jax
import jax.numpy as jnp
import numpy as np
from jax import lax
from jax.experimental import pallas as pl
from jax.experimental.pallas import tpu as pltpu
from jax.sharding import PartitionSpec as P

FIRST_ALPHA = 1.0 / 3.0
FIRST_A = 14.0 / 9.0
FIRST_B = 1.0 / 9.0
SECOND_ALPHA = 2.0 / 11.0
SECOND_A = 12.0 / 11.0
SECOND_B = 3.0 / 11.0
MESH = pl.DeviceIdType.MESH
STRIP = 24
REACH = 32
FULL = 128


class Line:
    def __init__(self, alpha, taps):
        root = np.sqrt(1.0 - 4.0 * alpha * alpha)
        self.rho = (root - 1.0) / (2.0 * alpha)
        self.root, self.taps = root, taps
        self.ahead = sum(c * self.rho**m for m, c in taps.items()) / root
        self.behind = sum(c * self.rho**-m for m, c in taps.items()) / root

    def weight(self, n):
        n = np.asarray(n)
        return sum(c * self.rho ** np.abs(n + m) for m, c in self.taps.items()) / self.root

    def local(self, cells):
        i = np.arange(cells)
        table = self.weight(i[:, None] - i[None, :])
        table[:, cells - 1] = 0.0
        return table

    def low_sum(self, reach):
        power = self.rho ** np.arange(reach - 1)
        weights = np.zeros(reach)
        weights[1:] += power
        weights[:-1] -= power
        return weights


FIRST = Line(
    FIRST_ALPHA,
    {
        1: 0.25 * FIRST_B,
        0: 0.5 * FIRST_A + 0.25 * FIRST_B,
        -1: 0.5 * FIRST_A + 0.25 * FIRST_B,
        -2: 0.25 * FIRST_B,
    },
)
SECOND = Line(
    SECOND_ALPHA,
    {
        1: 0.25 * SECOND_B,
        0: SECOND_A + 0.25 * SECOND_B,
        -1: -SECOND_A - 0.25 * SECOND_B,
        -2: -0.25 * SECOND_B,
    },
)


def halves(table):
    high = np.asarray(table, np.float32).astype(jnp.bfloat16)
    low = (table - high.astype(np.float64)).astype(np.float32).astype(jnp.bfloat16)
    return high, low


def sum_tables(reach):
    rows = [FIRST.low_sum(reach), SECOND.low_sum(reach)]
    rows += [-row[::-1] for row in rows]
    return np.repeat(np.stack(rows)[:, :, None], 128, axis=2).astype(np.float32)


def x_table(cells):
    rows = []
    for line in (FIRST, SECOND):
        for half in halves(line.local(cells)):
            rows.append(np.concatenate([half, half], axis=1))
    return np.concatenate(rows, axis=0)


def y_table(cells):
    columns = []
    for line in (FIRST, SECOND):
        high, low = halves(line.local(cells).T)
        columns.append(np.concatenate([high, high, low], axis=0))
    return np.concatenate(columns, axis=1)


def y_edge_table(cells):
    i = np.arange(cells)
    table = np.zeros((16, 3 * cells))
    for line, sum_row, edge_row, place in (
        (FIRST, 0, 2, 0),
        (SECOND, 1, 2, 1),
        (FIRST, 3, 4, 2),
    ):
        span = slice(place * cells, (place + 1) * cells)
        table[sum_row, span] = line.ahead * line.rho ** (i + 2)
        table[edge_row, span] = line.weight(i + 1)
        table[8 + sum_row, span] = line.behind * line.rho ** (cells - i)
        table[8 + edge_row, span] = line.weight(i - cells + 1)
    high, low = halves(table)
    blank = np.zeros((FULL - 48, 3 * cells), high.dtype)
    return np.concatenate([high, high, low, blank], axis=0)


def x_edge_table():
    r = np.arange(STRIP)
    table = np.zeros((2, 4, STRIP))
    for k, line in enumerate((FIRST, SECOND)):
        table[0, k] = line.ahead * line.rho ** (r + 1)
        table[0, 2 + k, 0] = line.weight(1) - line.ahead * line.rho
        table[1, k] = (line.behind * line.rho**r)[::-1]
        table[1, 2 + k, STRIP - 1] = line.weight(0) - line.behind
    return np.repeat(table[:, :, :, None], 128, axis=3).astype(np.float32)


def split(values):
    high = values.astype(jnp.bfloat16)
    low = (values - high.astype(jnp.float32)).astype(jnp.bfloat16)
    return high, low


def matmul(left, right):
    return jnp.dot(left, right, preferred_element_type=jnp.float32)


def twice(tile):
    return jnp.concatenate([tile, tile], axis=1)


def exchange_kernel(
    counts,
    f_hbm,
    k_hbm,
    tx_hbm,
    ty_hbm,
    hx_hbm,
    hy_hbm,
    wy_hbm,
    gx,
    gy,
    dif,
    kx,
    kap,
    xc,
    fld,
    tx,
    ty,
    hx,
    hy,
    wy,
    curv,
    ky,
    xs,
    xr,
    ys,
    yr,
    in_sem,
    send_sem,
    recv_sem,
):
    planes, cells_x, cells_y = fld.shape
    top = cells_x - STRIP
    ix, iy = lax.axis_index("gx"), lax.axis_index("gy")
    nx, ny = counts
    left = (lax.rem(ix + nx - 1, nx), iy)
    right = (lax.rem(ix + 1, nx), iy)
    below = (ix, lax.rem(iy + ny - 1, ny))
    above = (ix, lax.rem(iy + 1, ny))

    barrier = pltpu.get_barrier_semaphore()
    for neighbour in (left, right, below, above):
        pl.semaphore_signal(barrier, inc=1, device_id=neighbour, device_id_type=MESH)

    loads = []

    def load(source, target):
        copy = pltpu.make_async_copy(source, target, in_sem.at[len(loads)])
        copy.start()
        loads.append(copy)
        return copy

    first_loads = [load(tx_hbm, tx)]
    for rows in (pl.ds(0, STRIP), pl.ds(top, STRIP)):
        first_loads.append(load(f_hbm.at[:, rows, :], fld.at[:, rows, :]))
        first_loads.append(load(k_hbm.at[:, rows, :], kap.at[:, rows, :]))
    middle = pl.ds(STRIP, top - STRIP)
    next_loads = [
        load(ty_hbm, ty),
        load(f_hbm.at[:, middle, :], fld.at[:, middle, :]),
        load(k_hbm.at[:, middle, :], kap.at[:, middle, :]),
    ]
    last_loads = [load(hx_hbm, hx), load(hy_hbm, hy), load(wy_hbm, wy)]
    ys[:, :, 5:8, :] = jnp.zeros((2, planes, 3, 128), jnp.float32)

    for copy in first_loads:
        copy.wait()
    for side, start in ((0, 0), (1, top)):
        edge = 0 if side == 0 else cells_x - 1
        with_first, with_second = twice(tx[2 * side]), twice(tx[2 * side + 1])
        for p in range(planes):
            rows = fld[p, start : start + STRIP, :]
            krows = kap[p, start : start + STRIP, :]
            xs[side, 0, p : p + 1, :] = jnp.sum(rows * with_first, axis=0, keepdims=True)
            xs[side, 1, p : p + 1, :] = jnp.sum(rows * with_second, axis=0, keepdims=True)
            xs[side, 2, p : p + 1, :] = fld[p, edge : edge + 1, :]
            xs[side, 3, p : p + 1, :] = jnp.sum(krows * with_first, axis=0, keepdims=True)
            xs[side, 4, p : p + 1, :] = kap[p, edge : edge + 1, :]

    for copy in next_loads:
        copy.wait()
    lane = lax.broadcasted_iota(jnp.int32, (cells_x, 128), 1)
    for p in range(planes):
        f_low, f_high = fld[p, :, 0:128], fld[p, :, cells_y - 128 : cells_y]
        k_low, k_high = kap[p, :, 0:128], kap[p, :, cells_y - 128 : cells_y]
        packed = jnp.where(
            lane < REACH,
            f_low,
            jnp.where(
                lane < 2 * REACH,
                pltpu.roll(k_low, REACH, 1),
                jnp.where(lane < 3 * REACH, pltpu.roll(k_high, 128 - REACH, 1), f_high),
            ),
        )
        turned = packed.T
        for side, f_part, k_part, f_edge, k_edge in (
            (0, turned[0:32], turned[32:64], turned[0:1], turned[32:33]),
            (1, turned[96:128], turned[64:96], turned[127:128], turned[95:96]),
        ):
            with_first, with_second = ty[2 * side], ty[2 * side + 1]
            ys[side, p, 0:1, :] = jnp.sum(f_part * with_first, axis=0, keepdims=True)
            ys[side, p, 1:2, :] = jnp.sum(f_part * with_second, axis=0, keepdims=True)
            ys[side, p, 2:3, :] = f_edge
            ys[side, p, 3:4, :] = jnp.sum(k_part * with_first, axis=0, keepdims=True)
            ys[side, p, 4:5, :] = k_edge

    pl.semaphore_wait(barrier, 4)
    copies = []
    for place, (source, target, device) in enumerate(
        (
            (xs.at[0], xr.at[1], left),
            (xs.at[1], xr.at[0], right),
            (ys.at[0], yr.at[1], below),
            (ys.at[1], yr.at[0], above),
        )
    ):
        copy = pltpu.make_async_remote_copy(
            src_ref=source,
            dst_ref=target,
            send_sem=send_sem.at[place],
            recv_sem=recv_sem.at[place],
            device_id=device,
            device_id_type=MESH,
        )
        copy.start()
        copies.append(copy)

    for copy in last_loads:
        copy.wait()

    def local_pair(pair, carry):
        tall, ktall = [], []
        for q in range(2):
            p = 2 * pair + q
            f, k = fld[p], kap[p]
            high, low = split(pltpu.roll(f, cells_x - 1, 0) - f)
            along = matmul(hx[...], jnp.concatenate([high, low], axis=0))
            gx[p] = along[0:cells_x] + along[cells_x : 2 * cells_x]
            curv[p] = along[2 * cells_x : 3 * cells_x] + along[3 * cells_x : 4 * cells_x]
            high, low = split(pltpu.roll(k, cells_x - 1, 0) - k)
            along = matmul(hx[0 : 2 * cells_x, :], jnp.concatenate([high, low], axis=0))
            kx[p] = along[0:cells_x] + along[cells_x : 2 * cells_x]
            high, low = split(pltpu.roll(f, cells_y - 1, 1) - f)
            tall.append(jnp.concatenate([high, low, high], axis=1))
            high, low = split(pltpu.roll(k, cells_y - 1, 1) - k)
            ktall.append(jnp.concatenate([high, low, high], axis=1))
        across = matmul(jnp.concatenate(tall, axis=0), hy[...])
        kacross = matmul(jnp.concatenate(ktall, axis=0), hy[:, 0:cells_y])
        for q in range(2):
            p = 2 * pair + q
            rows = slice(q * cells_x, (q + 1) * cells_x)
            gy[p] = across[rows, 0:cells_y]
            curv[p] = curv[p] + across[rows, cells_y : 2 * cells_y]
            ky[p] = kacross[rows]
        return carry

    lax.fori_loop(0, planes // 2, local_pair, 0)

    copies[2].wait_recv()
    copies[3].wait_recv()
    row = lax.broadcasted_iota(jnp.int32, (8, 128), 0)
    is_edge = (row == 2) | (row == 4)

    def finish_plane(p, carry):
        from_below, from_above = yr[0, p], yr[1, p]
        from_below = jnp.where(is_edge, ys[0, p] - from_below, from_below)
        from_above = jnp.where(is_edge, from_above - ys[1, p], from_above)
        ends = jnp.concatenate([from_below, from_above], axis=0)
        high = ends.astype(jnp.bfloat16).astype(jnp.float32)
        stack = jnp.concatenate(
            [high, ends - high, high, jnp.zeros((FULL - 48, cells_x), jnp.float32)], axis=0
        )
        reach = matmul(stack.T.astype(jnp.bfloat16), wy[...])
        grad = gy[p] + reach[:, 0:cells_y]
        gy[p] = grad
        kappa = kap[p]
        part = kappa * (curv[p] + reach[:, cells_y : 2 * cells_y]) + (
            ky[p] + reach[:, 2 * cells_y :]
        ) * grad
        inner = slice(STRIP, top)
        dif[p, 0:STRIP, :] = part[0:STRIP]
        dif[p, inner, :] = part[inner] + kx[p, inner, :] * gx[p, inner, :]
        dif[p, top:, :] = part[top:]
        return carry

    lax.fori_loop(0, planes, finish_plane, 0)

    copies[0].wait_recv()
    copies[1].wait_recv()
    for side in range(2):
        sign = 1.0 if side == 0 else -1.0
        jump = sign * (xs[side, 2] - xr[side, 2])
        kjump = sign * (xs[side, 4] - xr[side, 4])
        xc[side, 0] = FIRST.rho * xr[side, 0] + jump
        xc[side, 1] = SECOND.rho * xr[side, 1] + jump
        xc[side, 2] = jump
        xc[side, 3] = FIRST.rho * xr[side, 3] + kjump
        xc[side, 4] = kjump
    for copy in copies:
        copy.wait_send()


def finish_kernel(gx, gy, dif, kx, kap, xc, wx, gx_out, gy_out, dif_out, gs, ds, sem):
    planes, cells_x, cells_y = gx.shape
    top = cells_x - STRIP
    middle = pl.ds(STRIP, top - STRIP)
    copies = []

    def store(source, target):
        copy = pltpu.make_async_copy(source, target, sem.at[len(copies)])
        copy.start()
        copies.append(copy)

    store(gy, gy_out)
    store(gx.at[:, middle, :], gx_out.at[:, middle, :])
    store(dif.at[:, middle, :], dif_out.at[:, middle, :])
    for side, start in ((0, 0), (1, top)):
        rows = slice(start, start + STRIP)
        decay, decay_second, end, end_second = (twice(wx[side, k]) for k in range(4))
        for p in range(planes):
            first, second, jump, kfirst, kjump = (xc[side, k, p : p + 1, :] for k in range(5))
            grad = gx[p, rows, :] + decay * first + end * jump
            bend = decay_second * second + end_second * jump
            kgrad = kx[p, rows, :] + decay * kfirst + end * kjump
            gs[side, p] = grad
            ds[side, p] = dif[p, rows, :] + kap[p, rows, :] * bend + kgrad * grad
        store(gs.at[side], gx_out.at[:, pl.ds(start, STRIP), :])
        store(ds.at[side], dif_out.at[:, pl.ds(start, STRIP), :])
    for copy in copies:
        copy.wait()


def local(counts, scalar, diffusivity):
    block = scalar.shape
    planes, cells_x, cells_y = block
    tables = (
        jnp.asarray(sum_tables(STRIP)),
        jnp.asarray(sum_tables(REACH)),
        jnp.asarray(x_table(cells_x)),
        jnp.asarray(y_table(cells_y)),
        jnp.asarray(y_edge_table(cells_y)),
    )
    vmem, hbm = pl.BlockSpec(memory_space=pltpu.VMEM), pl.BlockSpec(memory_space=pltpu.HBM)
    field = jax.ShapeDtypeStruct(block, jnp.float32)
    field_buffer = pltpu.VMEM(block, jnp.float32)
    parts = pl.pallas_call(
        functools.partial(exchange_kernel, counts),
        out_shape=(field,) * 5 + (jax.ShapeDtypeStruct((2, 5, planes, cells_y), jnp.float32),),
        in_specs=[hbm] * 7,
        out_specs=(vmem,) * 6,
        scratch_shapes=[field_buffer]
        + [pltpu.VMEM(table.shape, table.dtype) for table in tables]
        + [field_buffer, field_buffer]
        + [pltpu.VMEM((2, 5, planes, cells_y), jnp.float32)] * 2
        + [pltpu.VMEM((2, planes, 8, cells_x), jnp.float32)] * 2
        + [
            pltpu.SemaphoreType.DMA((11,)),
            pltpu.SemaphoreType.DMA((4,)),
            pltpu.SemaphoreType.DMA((4,)),
        ],
        compiler_params=pltpu.CompilerParams(
            collective_id=0, has_side_effects=True, vmem_limit_bytes=28 * 1024 * 1024
        ),
        name="exchange",
    )(*(pltpu.with_memory_space_constraint(array, pltpu.HBM) for array in (scalar, diffusivity) + tables))
    strip_buffer = pltpu.VMEM((2, planes, STRIP, cells_y), jnp.float32)
    return pl.pallas_call(
        finish_kernel,
        out_shape=(field,) * 3,
        in_specs=[vmem] * 7,
        out_specs=(hbm,) * 3,
        scratch_shapes=[strip_buffer, strip_buffer, pltpu.SemaphoreType.DMA((7,))],
        compiler_params=pltpu.CompilerParams(vmem_limit_bytes=28 * 1024 * 1024),
        name="finish",
    )(*parts, jnp.asarray(x_edge_table()))


def solution(mesh):
    placed = P(None, "gx", "gy")
    return jax.shard_map(
        functools.partial(local, (mesh.shape["gx"], mesh.shape["gy"])),
        mesh=mesh,
        in_specs=(placed, placed),
        out_specs=(placed,) * 3,
        check_vma=False,
    )
```

```python
import functools

import jax
import jax.numpy as jnp
import numpy as np
from jax import lax
from jax.experimental import pallas as pl
from jax.experimental.pallas import tpu as pltpu
from jax.sharding import PartitionSpec as P

FIRST_ALPHA = 1.0 / 3.0
FIRST_A = 14.0 / 9.0
FIRST_B = 1.0 / 9.0
SECOND_ALPHA = 2.0 / 11.0
SECOND_A = 12.0 / 11.0
SECOND_B = 3.0 / 11.0
MESH = pl.DeviceIdType.MESH
STRIP = 24
REACH = 32
FULL = 128


class Line:
    def __init__(self, alpha, taps):
        root = np.sqrt(1.0 - 4.0 * alpha * alpha)
        self.rho = (root - 1.0) / (2.0 * alpha)
        self.root, self.taps = root, taps
        self.ahead = sum(c * self.rho**m for m, c in taps.items()) / root
        self.behind = sum(c * self.rho**-m for m, c in taps.items()) / root

    def weight(self, n):
        n = np.asarray(n)
        return sum(c * self.rho ** np.abs(n + m) for m, c in self.taps.items()) / self.root

    def local(self, cells):
        i = np.arange(cells)
        table = self.weight(i[:, None] - i[None, :])
        table[:, cells - 1] = 0.0
        return table

    def low_sum(self, reach):
        power = self.rho ** np.arange(reach - 1)
        weights = np.zeros(reach)
        weights[1:] += power
        weights[:-1] -= power
        return weights


FIRST = Line(
    FIRST_ALPHA,
    {
        1: 0.25 * FIRST_B,
        0: 0.5 * FIRST_A + 0.25 * FIRST_B,
        -1: 0.5 * FIRST_A + 0.25 * FIRST_B,
        -2: 0.25 * FIRST_B,
    },
)
SECOND = Line(
    SECOND_ALPHA,
    {
        1: 0.25 * SECOND_B,
        0: SECOND_A + 0.25 * SECOND_B,
        -1: -SECOND_A - 0.25 * SECOND_B,
        -2: -0.25 * SECOND_B,
    },
)


def halves(table):
    high = np.asarray(table, np.float32).astype(jnp.bfloat16)
    low = (table - high.astype(np.float64)).astype(np.float32).astype(jnp.bfloat16)
    return high, low


def stacked(columns):
    table = np.zeros((len(columns), 32, 128), np.float32)
    for place, column in enumerate(columns):
        table[place, : len(column)] = column[:, None]
    return table


def sum_columns(reach):
    low = [FIRST.low_sum(reach), SECOND.low_sum(reach)]
    return [-row[::-1] for row in low] + low


def high_end_columns():
    r = np.arange(STRIP)[::-1]
    columns = [(line.behind * line.rho**r) for line in (FIRST, SECOND)]
    for line in (FIRST, SECOND):
        column = np.zeros(8)
        column[7] = line.weight(0) - line.behind
        columns.append(column)
    return columns


def low_end_columns():
    r = np.arange(STRIP)
    columns = [(line.ahead * line.rho ** (r + 1)) for line in (FIRST, SECOND)]
    for line in (FIRST, SECOND):
        column = np.zeros(8)
        column[0] = line.weight(1) - line.ahead * line.rho
        columns.append(column)
    return columns


def x_table(cells):
    rows = []
    for line in (FIRST, SECOND):
        for half in halves(line.local(cells)):
            rows.append(np.concatenate([half, half], axis=1))
    return np.concatenate(rows, axis=0)


def y_table(cells):
    rows = []
    for line in (FIRST, SECOND):
        high, low = halves(line.local(cells).T)
        rows += [high, high, low]
    return np.concatenate(rows, axis=0)


def y_end_table(cells):
    i = np.arange(cells)
    blocks = []
    for line, sum_row, edge_row in ((FIRST, 0, 2), (SECOND, 1, 2), (FIRST, 3, 4)):
        table = np.zeros((16, cells))
        table[sum_row] = line.ahead * line.rho ** (i + 2)
        table[edge_row] = line.weight(i + 1)
        table[8 + sum_row] = line.behind * line.rho ** (cells - i)
        table[8 + edge_row] = line.weight(i - cells + 1)
        high, low = halves(table)
        blank = np.zeros((FULL - 48, cells), high.dtype)
        blocks += [high, high, low, blank]
    return np.concatenate(blocks, axis=0)


def split(values):
    high = values.astype(jnp.bfloat16)
    low = (values - high.astype(jnp.float32)).astype(jnp.bfloat16)
    return high, low


def matmul(left, right):
    return jnp.dot(left, right, preferred_element_type=jnp.float32)


def twice(tile):
    return jnp.concatenate([tile, tile], axis=1)


def ends_applied(side, grad, kgrad, part, kappa, columns, values):
    decay, decay_second, end, end_second = columns
    first, second, jump, kfirst, kjump = values
    grads, parts = [], []
    for tile in range(STRIP // 8):
        r = slice(8 * tile, 8 * tile + 8)
        g = grad[r] + decay[r] * first
        k = kgrad[r] + decay[r] * kfirst
        distance = tile if side == 0 else STRIP // 8 - 1 - tile
        d = part[r]
        if distance < 2:
            bend = decay_second[r] * second
            if distance == 0:
                g = g + end * jump
                k = k + end * kjump
                bend = bend + end_second * jump
            d = d + kappa[r] * bend
        grads.append(g)
        parts.append(d + k * g)
    return jnp.concatenate(grads, axis=0), jnp.concatenate(parts, axis=0)


def exchange_kernel(
    counts,
    f_hbm,
    k_hbm,
    tab_hbm,
    mats_hbm,
    gx,
    gy,
    dif,
    kx,
    kap,
    xc,
    fld,
    tab,
    mats,
    curv,
    ky,
    xs,
    xr,
    ys,
    yr,
    xh,
    in_sem,
    send_sem,
    recv_sem,
    left_ready,
    above_ready,
):
    planes, cells_x, cells_y = fld.shape
    top = cells_x - STRIP
    loads = []

    def load(source, target):
        copy = pltpu.make_async_copy(source, target, in_sem.at[len(loads)])
        copy.start()
        loads.append(copy)
        return copy

    def load_rows(rows):
        return [
            load(f_hbm.at[:, rows, :], fld.at[:, rows, :]),
            load(k_hbm.at[:, rows, :], kap.at[:, rows, :]),
        ]

    high_loads = load_rows(pl.ds(top, STRIP)) + [load(tab_hbm, tab)]
    low_loads = load_rows(pl.ds(0, STRIP))
    middle_loads = load_rows(pl.ds(STRIP, top - STRIP))
    table_load = load(mats_hbm, mats)

    ix, iy = lax.axis_index("gx"), lax.axis_index("gy")
    nx, ny = counts
    left = (jnp.where(ix == 0, nx - 1, ix - 1), iy)
    right = (jnp.where(ix == nx - 1, 0, ix + 1), iy)
    below = (ix, jnp.where(iy == 0, ny - 1, iy - 1))
    above = (ix, jnp.where(iy == ny - 1, 0, iy + 1))
    barrier = pltpu.get_barrier_semaphore()
    for neighbour in (left, above):
        pl.semaphore_signal(barrier, inc=1, device_id=neighbour, device_id_type=MESH)

    def send(place, source, target, device):
        copy = pltpu.make_async_remote_copy(
            src_ref=source,
            dst_ref=target,
            send_sem=send_sem.at[place],
            recv_sem=recv_sem.at[place],
            device_id=device,
            device_id_type=MESH,
        )
        copy.start()
        return copy

    def sum_x_edge(side, start, edge, place):
        with_first, with_second = twice(tab[place, 0:STRIP]), twice(tab[place + 1, 0:STRIP])
        for p in range(planes):
            rows = fld[p, start : start + STRIP, :]
            krows = kap[p, start : start + STRIP, :]
            xs[side, 0, p : p + 1, :] = jnp.sum(rows * with_first, axis=0, keepdims=True)
            xs[side, 1, p : p + 1, :] = jnp.sum(rows * with_second, axis=0, keepdims=True)
            xs[side, 2, p : p + 1, :] = fld[p, edge : edge + 1, :]
            xs[side, 3, p : p + 1, :] = jnp.sum(krows * with_first, axis=0, keepdims=True)
            xs[side, 4, p : p + 1, :] = kap[p, edge : edge + 1, :]

    for copy in high_loads:
        copy.wait()
    sum_x_edge(1, top, cells_x - 1, 0)
    pl.semaphore_wait(barrier, 2)
    to_right = send(1, xs.at[1], xr.at[0], right)
    pl.semaphore_signal(left_ready, inc=1, device_id=right, device_id_type=MESH)
    pl.semaphore_signal(above_ready, inc=1, device_id=below, device_id_type=MESH)
    for copy in low_loads:
        copy.wait()
    sum_x_edge(0, 0, 0, 2)

    for copy in middle_loads:
        copy.wait()
    ys[:, :, 5:8, :] = jnp.zeros((2, planes, 3, 128), jnp.float32)
    lane = lax.broadcasted_iota(jnp.int32, (cells_x, 128), 1)
    for p in range(planes):
        f_low, f_high = fld[p, :, 0:128], fld[p, :, cells_y - 128 : cells_y]
        k_low, k_high = kap[p, :, 0:128], kap[p, :, cells_y - 128 : cells_y]
        packed = jnp.where(
            lane < REACH,
            f_low,
            jnp.where(
                lane < 2 * REACH,
                pltpu.roll(k_low, REACH, 1),
                jnp.where(lane < 3 * REACH, pltpu.roll(k_high, 128 - REACH, 1), f_high),
            ),
        )
        turned = packed.T
        for side, place, f_part, k_part, f_edge, k_edge in (
            (0, 6, turned[0:32], turned[32:64], turned[0:1], turned[32:33]),
            (1, 4, turned[96:128], turned[64:96], turned[127:128], turned[95:96]),
        ):
            with_first, with_second = tab[place], tab[place + 1]
            ys[side, p, 0:1, :] = jnp.sum(f_part * with_first, axis=0, keepdims=True)
            ys[side, p, 1:2, :] = jnp.sum(f_part * with_second, axis=0, keepdims=True)
            ys[side, p, 2:3, :] = f_edge
            ys[side, p, 3:4, :] = jnp.sum(k_part * with_first, axis=0, keepdims=True)
            ys[side, p, 4:5, :] = k_edge
    to_below = send(2, ys.at[0], yr.at[1], below)
    pl.semaphore_wait(above_ready, 1)
    to_above = send(3, ys.at[1], yr.at[0], above)

    table_load.wait()
    x_rows = 4 * cells_x
    y_first = slice(x_rows, x_rows + 3 * cells_y)
    y_second = slice(x_rows + 3 * cells_y, x_rows + 6 * cells_y)
    end_rows = x_rows + 6 * cells_y

    def local_pair(pair, carry):
        tall, ktall = [], []
        for q in range(2):
            p = 2 * pair + q
            f, k = fld[p], kap[p]
            high, low = split(pltpu.roll(f, cells_x - 1, 0) - f)
            along = matmul(mats[0:x_rows, :], jnp.concatenate([high, low], axis=0))
            gx[p] = along[0:cells_x] + along[cells_x : 2 * cells_x]
            curv[p] = along[2 * cells_x : 3 * cells_x] + along[3 * cells_x : 4 * cells_x]
            high, low = split(pltpu.roll(k, cells_x - 1, 0) - k)
            along = matmul(mats[0 : 2 * cells_x, :], jnp.concatenate([high, low], axis=0))
            kx[p] = along[0:cells_x] + along[cells_x : 2 * cells_x]
            high, low = split(pltpu.roll(f, cells_y - 1, 1) - f)
            tall.append(jnp.concatenate([high, low, high], axis=1))
            high, low = split(pltpu.roll(k, cells_y - 1, 1) - k)
            ktall.append(jnp.concatenate([high, low, high], axis=1))
        across = matmul(jnp.concatenate(tall + ktall, axis=0), mats[y_first, :])
        bend = matmul(jnp.concatenate(tall, axis=0), mats[y_second, :])
        for q in range(2):
            p = 2 * pair + q
            gy[p] = across[q * cells_x : (q + 1) * cells_x]
            ky[p] = across[(q + 2) * cells_x : (q + 3) * cells_x]
            curv[p] = curv[p] + bend[q * cells_x : (q + 1) * cells_x]
        return carry

    lax.fori_loop(0, planes // 2, local_pair, 0)

    pl.semaphore_wait(left_ready, 1)
    to_left = send(0, xs.at[0], xr.at[1], left)

    to_below.wait_recv()
    to_above.wait_recv()
    row = lax.broadcasted_iota(jnp.int32, (8, 128), 0)
    is_edge = (row == 2) | (row == 4)

    def finish_pair(pair, carry):
        stacks = []
        for q in range(2):
            p = 2 * pair + q
            from_below, from_above = yr[0, p], yr[1, p]
            from_below = jnp.where(is_edge, ys[0, p] - from_below, from_below)
            from_above = jnp.where(is_edge, from_above - ys[1, p], from_above)
            ends = jnp.concatenate([from_below, from_above], axis=0)
            high = ends.astype(jnp.bfloat16).astype(jnp.float32)
            blank = jnp.zeros((FULL - 48, cells_x), jnp.float32)
            stacks.append(jnp.concatenate([high, ends - high, high, blank], axis=0).T)
        turned = jnp.concatenate(stacks, axis=0).astype(jnp.bfloat16)
        reach = [
            matmul(turned, mats[end_rows + n * FULL : end_rows + (n + 1) * FULL, :]) for n in range(3)
        ]
        for q in range(2):
            p = 2 * pair + q
            rows = slice(q * cells_x, (q + 1) * cells_x)
            grad = gy[p] + reach[0][rows]
            gy[p] = grad
            part = kap[p] * (curv[p] + reach[1][rows]) + (ky[p] + reach[2][rows]) * grad
            inner = slice(STRIP, top)
            dif[p, 0:STRIP, :] = part[0:STRIP]
            dif[p, inner, :] = part[inner] + kx[p, inner, :] * gx[p, inner, :]
            dif[p, top:, :] = part[top:]
        return carry

    lax.fori_loop(0, planes // 2, finish_pair, 0)

    def combine(side, out):
        sign = 1.0 if side == 0 else -1.0
        jump = sign * (xs[side, 2] - xr[side, 2])
        kjump = sign * (xs[side, 4] - xr[side, 4])
        out[0] = FIRST.rho * xr[side, 0] + jump
        out[1] = SECOND.rho * xr[side, 1] + jump
        out[2] = jump
        out[3] = FIRST.rho * xr[side, 3] + kjump
        out[4] = kjump

    to_left.wait_recv()
    combine(1, xh)
    columns = [twice(tab[n, 0:STRIP]) for n in (8, 9)] + [twice(tab[n, 0:8]) for n in (10, 11)]
    for p in range(planes):
        gx[p, top:, :], dif[p, top:, :] = ends_applied(
            1,
            gx[p, top:, :],
            kx[p, top:, :],
            dif[p, top:, :],
            kap[p, top:, :],
            columns,
            [xh[n, p : p + 1, :] for n in range(5)],
        )
    for copy in (to_left, to_right, to_below, to_above):
        copy.wait_send()
    to_right.wait_recv()
    combine(0, xc)


def finish_kernel(gx, gy, dif, kx, kap, xc, tab, gx_out, gy_out, dif_out, gs, ds, sem):
    planes, cells_x, cells_y = gx.shape
    copies = []

    def store(source, target):
        copy = pltpu.make_async_copy(source, target, sem.at[len(copies)])
        copy.start()
        copies.append(copy)

    rest = pl.ds(STRIP, cells_x - STRIP)
    store(gy, gy_out)
    store(gx.at[:, rest, :], gx_out.at[:, rest, :])
    store(dif.at[:, rest, :], dif_out.at[:, rest, :])
    columns = [twice(tab[n, 0:STRIP]) for n in (0, 1)] + [twice(tab[n, 0:8]) for n in (2, 3)]
    for p in range(planes):
        gs[p], ds[p] = ends_applied(
            0,
            gx[p, 0:STRIP, :],
            kx[p, 0:STRIP, :],
            dif[p, 0:STRIP, :],
            kap[p, 0:STRIP, :],
            columns,
            [xc[n, p : p + 1, :] for n in range(5)],
        )
    store(gs, gx_out.at[:, pl.ds(0, STRIP), :])
    store(ds, dif_out.at[:, pl.ds(0, STRIP), :])
    for copy in copies:
        copy.wait()


def local(counts, scalar, diffusivity):
    block = scalar.shape
    planes, cells_x, cells_y = block
    columns = sum_columns(STRIP) + sum_columns(REACH) + high_end_columns()
    tables = (
        jnp.asarray(stacked(columns)),
        jnp.asarray(
            np.concatenate([x_table(cells_x), y_table(cells_y), y_end_table(cells_y)], axis=0)
        ),
    )
    vmem, hbm = pl.BlockSpec(memory_space=pltpu.VMEM), pl.BlockSpec(memory_space=pltpu.HBM)
    field = jax.ShapeDtypeStruct(block, jnp.float32)
    field_buffer = pltpu.VMEM(block, jnp.float32)
    ends_shape = (5, planes, cells_y)
    operands = [
        pltpu.with_memory_space_constraint(array, pltpu.HBM)
        for array in (scalar, diffusivity) + tables
    ]
    parts = pl.pallas_call(
        functools.partial(exchange_kernel, counts),
        out_shape=(field,) * 5 + (jax.ShapeDtypeStruct(ends_shape, jnp.float32),),
        in_specs=[hbm] * 4,
        out_specs=(vmem,) * 6,
        scratch_shapes=[field_buffer]
        + [pltpu.VMEM(table.shape, table.dtype) for table in tables]
        + [field_buffer, field_buffer]
        + [pltpu.VMEM((2,) + ends_shape, jnp.float32)] * 2
        + [pltpu.VMEM((2, planes, 8, cells_x), jnp.float32)] * 2
        + [
            pltpu.VMEM(ends_shape, jnp.float32),
            pltpu.SemaphoreType.DMA((8,)),
            pltpu.SemaphoreType.DMA((4,)),
            pltpu.SemaphoreType.DMA((4,)),
            pltpu.SemaphoreType.REGULAR,
            pltpu.SemaphoreType.REGULAR,
        ],
        compiler_params=pltpu.CompilerParams(
            collective_id=0, has_side_effects=True, vmem_limit_bytes=28 * 1024 * 1024
        ),
        name="exchange",
    )(*operands)
    strip_buffer = pltpu.VMEM((planes, STRIP, cells_y), jnp.float32)
    return pl.pallas_call(
        finish_kernel,
        out_shape=(field,) * 3,
        in_specs=[vmem] * 7,
        out_specs=(hbm,) * 3,
        scratch_shapes=[strip_buffer, strip_buffer, pltpu.SemaphoreType.DMA((5,))],
        compiler_params=pltpu.CompilerParams(vmem_limit_bytes=28 * 1024 * 1024),
        name="finish",
    )(*parts, jnp.asarray(stacked(low_end_columns())))


def solution(mesh):
    placed = P(None, "gx", "gy")
    return jax.shard_map(
        functools.partial(local, (mesh.shape["gx"], mesh.shape["gy"])),
        mesh=mesh,
        in_specs=(placed, placed),
        out_specs=(placed,) * 3,
        check_vma=False,
    )
```

```python
import functools

import jax
import jax.numpy as jnp
import numpy as np
from jax import lax
from jax.experimental import pallas as pl
from jax.experimental.pallas import tpu as pltpu
from jax.sharding import PartitionSpec as P

FIRST_ALPHA = 1.0 / 3.0
FIRST_A = 14.0 / 9.0
FIRST_B = 1.0 / 9.0
SECOND_ALPHA = 2.0 / 11.0
SECOND_A = 12.0 / 11.0
SECOND_B = 3.0 / 11.0
MESH = pl.DeviceIdType.MESH
STRIP = 24
REACH = 32
FULL = 128
RUN = 8


class Line:
    def __init__(self, alpha, taps):
        root = np.sqrt(1.0 - 4.0 * alpha * alpha)
        self.rho = (root - 1.0) / (2.0 * alpha)
        self.root, self.taps = root, taps
        self.ahead = sum(c * self.rho**m for m, c in taps.items()) / root
        self.behind = sum(c * self.rho**-m for m, c in taps.items()) / root

    def weight(self, n):
        n = np.asarray(n)
        return sum(c * self.rho ** np.abs(n + m) for m, c in self.taps.items()) / self.root

    def local(self, cells):
        i = np.arange(cells)
        table = self.weight(i[:, None] - i[None, :])
        table[:, cells - 1] = 0.0
        return table

    def low_sum(self, reach):
        power = self.rho ** np.arange(reach - 1)
        weights = np.zeros(reach)
        weights[1:] += power
        weights[:-1] -= power
        return weights


FIRST = Line(
    FIRST_ALPHA,
    {
        1: 0.25 * FIRST_B,
        0: 0.5 * FIRST_A + 0.25 * FIRST_B,
        -1: 0.5 * FIRST_A + 0.25 * FIRST_B,
        -2: 0.25 * FIRST_B,
    },
)
SECOND = Line(
    SECOND_ALPHA,
    {
        1: 0.25 * SECOND_B,
        0: SECOND_A + 0.25 * SECOND_B,
        -1: -SECOND_A - 0.25 * SECOND_B,
        -2: -0.25 * SECOND_B,
    },
)


def halves(table):
    high = np.asarray(table, np.float32).astype(jnp.bfloat16)
    low = (table - high.astype(np.float64)).astype(np.float32).astype(jnp.bfloat16)
    return high, low


def stacked(columns):
    table = np.zeros((len(columns), 32, 128), np.float32)
    for place, column in enumerate(columns):
        table[place, : len(column)] = column[:, None]
    return table


def sum_columns(reach):
    low = [FIRST.low_sum(reach), SECOND.low_sum(reach)]
    return [-row[::-1] for row in low] + low


def high_end_columns():
    r = np.arange(STRIP)[::-1]
    columns = [(line.behind * line.rho**r) for line in (FIRST, SECOND)]
    for line in (FIRST, SECOND):
        column = np.zeros(8)
        column[7] = line.weight(0) - line.behind
        columns.append(column)
    return columns


def low_end_columns():
    r = np.arange(STRIP)
    columns = [(line.ahead * line.rho ** (r + 1)) for line in (FIRST, SECOND)]
    for line in (FIRST, SECOND):
        column = np.zeros(8)
        column[0] = line.weight(1) - line.ahead * line.rho
        columns.append(column)
    return columns


def x_table(cells):
    rows = []
    for line in (FIRST, SECOND):
        for half in halves(line.local(cells)):
            rows.append(np.concatenate([half, half], axis=1))
    return np.concatenate(rows, axis=0)


def y_table(cells):
    rows = []
    for line in (FIRST, SECOND):
        high, low = halves(line.local(cells).T)
        rows += [high, high, low]
    return np.concatenate(rows, axis=0)


def y_end_table(cells):
    i = np.arange(cells)
    blocks = []
    for line, sum_row, edge_row in ((FIRST, 0, 2), (SECOND, 1, 2), (FIRST, 3, 4)):
        table = np.zeros((16, cells))
        table[sum_row] = line.ahead * line.rho ** (i + 2)
        table[edge_row] = line.weight(i + 1)
        table[8 + sum_row] = line.behind * line.rho ** (cells - i)
        table[8 + edge_row] = line.weight(i - cells + 1)
        high, low = halves(table)
        blank = np.zeros((FULL - 48, cells), high.dtype)
        blocks += [high, high, low, blank]
    return np.concatenate(blocks, axis=0)


def split(values):
    high = values.astype(jnp.bfloat16)
    low = (values - high.astype(jnp.float32)).astype(jnp.bfloat16)
    return high, low


def matmul(left, right):
    return jnp.dot(left, right, preferred_element_type=jnp.float32)


def twice(tile):
    return jnp.concatenate([tile, tile], axis=1)


def ends_applied(side, grad, kgrad, part, kappa, columns, values):
    decay, decay_second, end, end_second = columns
    first, second, jump, kfirst, kjump = values
    grads, parts = [], []
    for tile in range(STRIP // 8):
        r = slice(8 * tile, 8 * tile + 8)
        g = grad[r] + decay[r] * first
        k = kgrad[r] + decay[r] * kfirst
        distance = tile if side == 0 else STRIP // 8 - 1 - tile
        d = part[r]
        if distance < 2:
            bend = decay_second[r] * second
            if distance == 0:
                g = g + end * jump
                k = k + end * kjump
                bend = bend + end_second * jump
            d = d + kappa[r] * bend
        grads.append(g)
        parts.append(d + k * g)
    return jnp.concatenate(grads, axis=0), jnp.concatenate(parts, axis=0)


def exchange_kernel(
    counts,
    f_hbm,
    k_hbm,
    tab_hbm,
    mats_hbm,
    gx,
    gy,
    dif,
    kx,
    kap,
    xc,
    fld,
    tab,
    mats,
    curv,
    ky,
    xs,
    xr,
    ys,
    yr,
    xh,
    in_sem,
    send_sem,
    recv_sem,
    left_ready,
    above_ready,
):
    planes, cells_x, cells_y = fld.shape
    top = cells_x - STRIP
    loads = []

    def load(source, target):
        copy = pltpu.make_async_copy(source, target, in_sem.at[len(loads)])
        copy.start()
        loads.append(copy)
        return copy

    def load_rows(rows):
        return [
            load(f_hbm.at[:, rows, :], fld.at[:, rows, :]),
            load(k_hbm.at[:, rows, :], kap.at[:, rows, :]),
        ]

    high_loads = load_rows(pl.ds(top, STRIP)) + [load(tab_hbm, tab)]
    low_loads = load_rows(pl.ds(0, STRIP))
    middle_loads = load_rows(pl.ds(STRIP, top - STRIP))
    table_load = load(mats_hbm, mats)

    ix, iy = lax.axis_index("gx"), lax.axis_index("gy")
    nx, ny = counts
    left = (jnp.where(ix == 0, nx - 1, ix - 1), iy)
    right = (jnp.where(ix == nx - 1, 0, ix + 1), iy)
    below = (ix, jnp.where(iy == 0, ny - 1, iy - 1))
    above = (ix, jnp.where(iy == ny - 1, 0, iy + 1))
    barrier = pltpu.get_barrier_semaphore()
    for neighbour in (left, above):
        pl.semaphore_signal(barrier, inc=1, device_id=neighbour, device_id_type=MESH)

    def message(place, source, target, device):
        return pltpu.make_async_remote_copy(
            src_ref=source,
            dst_ref=target,
            send_sem=send_sem.at[place],
            recv_sem=recv_sem.at[place],
            device_id=device,
            device_id_type=MESH,
        )

    def send(*what):
        copy = message(*what)
        copy.start()
        return copy

    def take_x_edge(side, edge):
        for p in range(planes):
            xs[side, 0, p : p + 1, :] = fld[p, edge : edge + 1, :]
            xs[side, 1, p : p + 1, :] = kap[p, edge : edge + 1, :]

    def sum_x_edge(side, start, place):
        with_first, with_second = twice(tab[place, 0:STRIP]), twice(tab[place + 1, 0:STRIP])
        for p in range(planes):
            rows = fld[p, start : start + STRIP, :]
            krows = kap[p, start : start + STRIP, :]
            xs[side, 2, p : p + 1, :] = jnp.sum(rows * with_first, axis=0, keepdims=True)
            xs[side, 3, p : p + 1, :] = jnp.sum(rows * with_second, axis=0, keepdims=True)
            xs[side, 4, p : p + 1, :] = jnp.sum(krows * with_first, axis=0, keepdims=True)

    for copy in high_loads:
        copy.wait()
    take_x_edge(1, cells_x - 1)
    pl.semaphore_wait(barrier, 2)
    to_right = [send(1, xs.at[1, 0:2], xr.at[0, 0:2], right)]
    sum_x_edge(1, top, 0)
    to_right.append(send(2, xs.at[1, 2:5], xr.at[0, 2:5], right))
    pl.semaphore_signal(left_ready, inc=1, device_id=right, device_id_type=MESH)
    pl.semaphore_signal(above_ready, inc=1, device_id=below, device_id_type=MESH)
    for copy in low_loads:
        copy.wait()
    take_x_edge(0, 0)
    sum_x_edge(0, 0, 2)

    for copy in middle_loads:
        copy.wait()
    ys[:, :, 5:8, :] = jnp.zeros((2, planes, 3, 128), jnp.float32)
    lane = lax.broadcasted_iota(jnp.int32, (cells_x, 128), 1)
    for p in range(planes):
        f_low, f_high = fld[p, :, 0:128], fld[p, :, cells_y - 128 : cells_y]
        k_low, k_high = kap[p, :, 0:128], kap[p, :, cells_y - 128 : cells_y]
        packed = jnp.where(
            lane < REACH,
            f_low,
            jnp.where(
                lane < 2 * REACH,
                pltpu.roll(k_low, REACH, 1),
                jnp.where(lane < 3 * REACH, pltpu.roll(k_high, 128 - REACH, 1), f_high),
            ),
        )
        turned = packed.T
        for side, place, f_part, k_part, f_edge, k_edge in (
            (0, 6, turned[0:32], turned[32:64], turned[0:1], turned[32:33]),
            (1, 4, turned[96:128], turned[64:96], turned[127:128], turned[95:96]),
        ):
            with_first, with_second = tab[place], tab[place + 1]
            ys[side, p, 0:1, :] = jnp.sum(f_part * with_first, axis=0, keepdims=True)
            ys[side, p, 1:2, :] = jnp.sum(f_part * with_second, axis=0, keepdims=True)
            ys[side, p, 2:3, :] = f_edge
            ys[side, p, 3:4, :] = jnp.sum(k_part * with_first, axis=0, keepdims=True)
            ys[side, p, 4:5, :] = k_edge
    to_below = send(3, ys.at[0], yr.at[1], below)
    pl.semaphore_wait(above_ready, 1)
    to_above = send(4, ys.at[1], yr.at[0], above)

    to_left = message(0, xs.at[0], xr.at[1], left)
    run_begins = lax.rem(ix, RUN) == 0

    def send_left():
        pl.semaphore_wait(left_ready, 1)
        to_left.start()

    pl.when(jnp.logical_not(run_begins))(send_left)

    table_load.wait()
    x_rows = 4 * cells_x
    y_first = slice(x_rows, x_rows + 3 * cells_y)
    y_second = slice(x_rows + 3 * cells_y, x_rows + 6 * cells_y)
    end_rows = x_rows + 6 * cells_y

    def local_pair(pair, carry):
        tall, ktall = [], []
        for q in range(2):
            p = 2 * pair + q
            f, k = fld[p], kap[p]
            high, low = split(pltpu.roll(f, cells_x - 1, 0) - f)
            along = matmul(mats[0:x_rows, :], jnp.concatenate([high, low], axis=0))
            gx[p] = along[0:cells_x] + along[cells_x : 2 * cells_x]
            curv[p] = along[2 * cells_x : 3 * cells_x] + along[3 * cells_x : 4 * cells_x]
            high, low = split(pltpu.roll(k, cells_x - 1, 0) - k)
            along = matmul(mats[0 : 2 * cells_x, :], jnp.concatenate([high, low], axis=0))
            kx[p] = along[0:cells_x] + along[cells_x : 2 * cells_x]
            high, low = split(pltpu.roll(f, cells_y - 1, 1) - f)
            tall.append(jnp.concatenate([high, low, high], axis=1))
            high, low = split(pltpu.roll(k, cells_y - 1, 1) - k)
            ktall.append(jnp.concatenate([high, low, high], axis=1))
        across = matmul(jnp.concatenate(tall + ktall, axis=0), mats[y_first, :])
        bend = matmul(jnp.concatenate(tall, axis=0), mats[y_second, :])
        for q in range(2):
            p = 2 * pair + q
            gy[p] = across[q * cells_x : (q + 1) * cells_x]
            ky[p] = across[(q + 2) * cells_x : (q + 3) * cells_x]
            curv[p] = curv[p] + bend[q * cells_x : (q + 1) * cells_x]
        return carry

    lax.fori_loop(0, planes // 2, local_pair, 0)

    to_below.wait_recv()
    to_above.wait_recv()
    row = lax.broadcasted_iota(jnp.int32, (8, 128), 0)
    is_edge = (row == 2) | (row == 4)

    def finish_pair(pair, carry):
        stacks = []
        for q in range(2):
            p = 2 * pair + q
            from_below, from_above = yr[0, p], yr[1, p]
            from_below = jnp.where(is_edge, ys[0, p] - from_below, from_below)
            from_above = jnp.where(is_edge, from_above - ys[1, p], from_above)
            ends = jnp.concatenate([from_below, from_above], axis=0)
            high = ends.astype(jnp.bfloat16).astype(jnp.float32)
            blank = jnp.zeros((FULL - 48, cells_x), jnp.float32)
            stacks.append(jnp.concatenate([high, ends - high, high, blank], axis=0).T)
        turned = jnp.concatenate(stacks, axis=0).astype(jnp.bfloat16)
        reach = [
            matmul(turned, mats[end_rows + n * FULL : end_rows + (n + 1) * FULL, :]) for n in range(3)
        ]
        for q in range(2):
            p = 2 * pair + q
            rows = slice(q * cells_x, (q + 1) * cells_x)
            grad = gy[p] + reach[0][rows]
            gy[p] = grad
            part = kap[p] * (curv[p] + reach[1][rows]) + (ky[p] + reach[2][rows]) * grad
            inner = slice(STRIP, top)
            dif[p, 0:STRIP, :] = part[0:STRIP]
            dif[p, inner, :] = part[inner] + kx[p, inner, :] * gx[p, inner, :]
            dif[p, top:, :] = part[top:]
        return carry

    lax.fori_loop(0, planes // 2, finish_pair, 0)
    pl.when(run_begins)(send_left)

    def combine(side, out):
        sign = 1.0 if side == 0 else -1.0
        jump = sign * (xs[side, 0] - xr[side, 0])
        kjump = sign * (xs[side, 1] - xr[side, 1])
        out[0] = FIRST.rho * xr[side, 2] + jump
        out[1] = SECOND.rho * xr[side, 3] + jump
        out[2] = jump
        out[3] = FIRST.rho * xr[side, 4] + kjump
        out[4] = kjump

    to_left.wait_recv()
    combine(1, xh)
    columns = [twice(tab[n, 0:STRIP]) for n in (8, 9)] + [twice(tab[n, 0:8]) for n in (10, 11)]
    for p in range(planes):
        gx[p, top:, :], dif[p, top:, :] = ends_applied(
            1,
            gx[p, top:, :],
            kx[p, top:, :],
            dif[p, top:, :],
            kap[p, top:, :],
            columns,
            [xh[n, p : p + 1, :] for n in range(5)],
        )
    for copy in [to_left, to_below, to_above] + to_right:
        copy.wait_send()
    for copy in to_right:
        copy.wait_recv()
    combine(0, xc)


def finish_kernel(gx, gy, dif, kx, kap, xc, tab, gx_out, gy_out, dif_out, gs, ds, sem):
    planes, cells_x, cells_y = gx.shape
    copies = []

    def store(source, target):
        copy = pltpu.make_async_copy(source, target, sem.at[len(copies)])
        copy.start()
        copies.append(copy)

    rest = pl.ds(STRIP, cells_x - STRIP)
    store(gy, gy_out)
    store(gx.at[:, rest, :], gx_out.at[:, rest, :])
    store(dif.at[:, rest, :], dif_out.at[:, rest, :])
    columns = [twice(tab[n, 0:STRIP]) for n in (0, 1)] + [twice(tab[n, 0:8]) for n in (2, 3)]
    for p in range(planes):
        gs[p], ds[p] = ends_applied(
            0,
            gx[p, 0:STRIP, :],
            kx[p, 0:STRIP, :],
            dif[p, 0:STRIP, :],
            kap[p, 0:STRIP, :],
            columns,
            [xc[n, p : p + 1, :] for n in range(5)],
        )
    store(gs, gx_out.at[:, pl.ds(0, STRIP), :])
    store(ds, dif_out.at[:, pl.ds(0, STRIP), :])
    for copy in copies:
        copy.wait()


def local(counts, scalar, diffusivity):
    block = scalar.shape
    planes, cells_x, cells_y = block
    columns = sum_columns(STRIP) + sum_columns(REACH) + high_end_columns()
    tables = (
        jnp.asarray(stacked(columns)),
        jnp.asarray(
            np.concatenate([x_table(cells_x), y_table(cells_y), y_end_table(cells_y)], axis=0)
        ),
    )
    vmem, hbm = pl.BlockSpec(memory_space=pltpu.VMEM), pl.BlockSpec(memory_space=pltpu.HBM)
    field = jax.ShapeDtypeStruct(block, jnp.float32)
    field_buffer = pltpu.VMEM(block, jnp.float32)
    ends_shape = (5, planes, cells_y)
    operands = [
        pltpu.with_memory_space_constraint(array, pltpu.HBM)
        for array in (scalar, diffusivity) + tables
    ]
    parts = pl.pallas_call(
        functools.partial(exchange_kernel, counts),
        out_shape=(field,) * 5 + (jax.ShapeDtypeStruct(ends_shape, jnp.float32),),
        in_specs=[hbm] * 4,
        out_specs=(vmem,) * 6,
        scratch_shapes=[field_buffer]
        + [pltpu.VMEM(table.shape, table.dtype) for table in tables]
        + [field_buffer, field_buffer]
        + [pltpu.VMEM((2,) + ends_shape, jnp.float32)] * 2
        + [pltpu.VMEM((2, planes, 8, cells_x), jnp.float32)] * 2
        + [
            pltpu.VMEM(ends_shape, jnp.float32),
            pltpu.SemaphoreType.DMA((8,)),
            pltpu.SemaphoreType.DMA((5,)),
            pltpu.SemaphoreType.DMA((5,)),
            pltpu.SemaphoreType.REGULAR,
            pltpu.SemaphoreType.REGULAR,
        ],
        compiler_params=pltpu.CompilerParams(
            collective_id=0, has_side_effects=True, vmem_limit_bytes=28 * 1024 * 1024
        ),
        name="exchange",
    )(*operands)
    strip_buffer = pltpu.VMEM((planes, STRIP, cells_y), jnp.float32)
    return pl.pallas_call(
        finish_kernel,
        out_shape=(field,) * 3,
        in_specs=[vmem] * 7,
        out_specs=(hbm,) * 3,
        scratch_shapes=[strip_buffer, strip_buffer, pltpu.SemaphoreType.DMA((5,))],
        compiler_params=pltpu.CompilerParams(vmem_limit_bytes=28 * 1024 * 1024),
        name="finish",
    )(*parts, jnp.asarray(stacked(low_end_columns())))


def solution(mesh):
    placed = P(None, "gx", "gy")
    return jax.shard_map(
        functools.partial(local, (mesh.shape["gx"], mesh.shape["gy"])),
        mesh=mesh,
        in_specs=(placed, placed),
        out_specs=(placed,) * 3,
        check_vma=False,
    )
```

```python
import functools

import jax
import jax.numpy as jnp
import numpy as np
from jax import lax
from jax.experimental import pallas as pl
from jax.experimental.pallas import tpu as pltpu
from jax.sharding import PartitionSpec as P

FIRST_ALPHA = 1.0 / 3.0
FIRST_A = 14.0 / 9.0
FIRST_B = 1.0 / 9.0
SECOND_ALPHA = 2.0 / 11.0
SECOND_A = 12.0 / 11.0
SECOND_B = 3.0 / 11.0
MESH = pl.DeviceIdType.MESH
LIMIT = 28 * 1024 * 1024
STRIP = 24
REACH = 32
FULL = 128
RUN = 8


class Line:
    def __init__(self, alpha, taps):
        root = np.sqrt(1.0 - 4.0 * alpha * alpha)
        self.rho = (root - 1.0) / (2.0 * alpha)
        self.root, self.taps = root, taps
        self.ahead = sum(c * self.rho**m for m, c in taps.items()) / root
        self.behind = sum(c * self.rho**-m for m, c in taps.items()) / root

    def weight(self, n):
        n = np.asarray(n)
        return sum(c * self.rho ** np.abs(n + m) for m, c in self.taps.items()) / self.root

    def local(self, cells):
        i = np.arange(cells)
        table = self.weight(i[:, None] - i[None, :])
        table[:, cells - 1] = 0.0
        return table

    def low_sum(self, reach):
        power = self.rho ** np.arange(reach - 1)
        weights = np.zeros(reach)
        weights[1:] += power
        weights[:-1] -= power
        return weights


FIRST = Line(
    FIRST_ALPHA,
    {
        1: 0.25 * FIRST_B,
        0: 0.5 * FIRST_A + 0.25 * FIRST_B,
        -1: 0.5 * FIRST_A + 0.25 * FIRST_B,
        -2: 0.25 * FIRST_B,
    },
)
SECOND = Line(
    SECOND_ALPHA,
    {
        1: 0.25 * SECOND_B,
        0: SECOND_A + 0.25 * SECOND_B,
        -1: -SECOND_A - 0.25 * SECOND_B,
        -2: -0.25 * SECOND_B,
    },
)


def halves(table):
    high = np.asarray(table, np.float32).astype(jnp.bfloat16)
    low = (table - high.astype(np.float64)).astype(np.float32).astype(jnp.bfloat16)
    return high, low


def stacked(columns):
    table = np.zeros((len(columns), 32, 128), np.float32)
    for place, column in enumerate(columns):
        table[place, : len(column)] = column[:, None]
    return table


def sum_columns(reach):
    low = [FIRST.low_sum(reach), SECOND.low_sum(reach)]
    return [-row[::-1] for row in low] + low


def high_end_columns():
    r = np.arange(STRIP)[::-1]
    columns = [(line.behind * line.rho**r) for line in (FIRST, SECOND)]
    for line in (FIRST, SECOND):
        column = np.zeros(8)
        column[7] = line.weight(0) - line.behind
        columns.append(column)
    return columns


def low_end_columns():
    r = np.arange(STRIP)
    columns = [(line.ahead * line.rho ** (r + 1)) for line in (FIRST, SECOND)]
    for line in (FIRST, SECOND):
        column = np.zeros(8)
        column[0] = line.weight(1) - line.ahead * line.rho
        columns.append(column)
    return columns


def x_table(cells):
    rows = []
    for line in (FIRST, SECOND):
        for half in halves(line.local(cells)):
            rows.append(np.concatenate([half, half], axis=1))
    return np.concatenate(rows, axis=0)


def y_table(cells):
    rows = []
    for line in (FIRST, SECOND):
        high, low = halves(line.local(cells).T)
        rows += [high, high, low]
    return np.concatenate(rows, axis=0)


def y_end_table(cells):
    i = np.arange(cells)
    blocks = []
    for line, sum_row, edge_row in ((FIRST, 0, 2), (SECOND, 1, 2), (FIRST, 3, 4)):
        table = np.zeros((16, cells))
        table[sum_row] = line.ahead * line.rho ** (i + 2)
        table[edge_row] = line.weight(i + 1)
        table[8 + sum_row] = line.behind * line.rho ** (cells - i)
        table[8 + edge_row] = line.weight(i - cells + 1)
        high, low = halves(table)
        blank = np.zeros((FULL - 48, cells), high.dtype)
        blocks += [high, high, low, blank]
    return np.concatenate(blocks, axis=0)


def split(values):
    high = values.astype(jnp.bfloat16)
    low = (values - high.astype(jnp.float32)).astype(jnp.bfloat16)
    return high, low


def matmul(left, right):
    return jnp.dot(left, right, preferred_element_type=jnp.float32)


def twice(tile):
    return jnp.concatenate([tile, tile], axis=1)


def ends_applied(side, grad, kgrad, part, kappa, columns, values):
    decay, decay_second, end, end_second = columns
    first, second, jump, kfirst, kjump = values
    grads, parts = [], []
    for tile in range(STRIP // 8):
        r = slice(8 * tile, 8 * tile + 8)
        g = grad[r] + decay[r] * first
        k = kgrad[r] + decay[r] * kfirst
        distance = tile if side == 0 else STRIP // 8 - 1 - tile
        d = part[r]
        if distance < 2:
            bend = decay_second[r] * second
            if distance == 0:
                g = g + end * jump
                k = k + end * kjump
                bend = bend + end_second * jump
            d = d + kappa[r] * bend
        grads.append(g)
        parts.append(d + k * g)
    return jnp.concatenate(grads, axis=0), jnp.concatenate(parts, axis=0)


def exchange_kernel(
    counts,
    f_hbm,
    k_hbm,
    tab_hbm,
    mats_hbm,
    gx,
    gy,
    dif,
    kx,
    kap,
    xc,
    fld,
    tab,
    mats,
    curv,
    ky,
    xs,
    xr,
    ys,
    yr,
    xh,
    in_sem,
    send_sem,
    recv_sem,
    left_ready,
    above_ready,
    below_ready,
):
    planes, cells_x, cells_y = fld.shape
    top = cells_x - STRIP
    loads = []

    def load(source, target):
        copy = pltpu.make_async_copy(source, target, in_sem.at[len(loads)])
        copy.start()
        loads.append(copy)
        return copy

    def load_rows(rows):
        return [
            load(f_hbm.at[:, rows, :], fld.at[:, rows, :]),
            load(k_hbm.at[:, rows, :], kap.at[:, rows, :]),
        ]

    high_loads = load_rows(pl.ds(top, STRIP)) + [load(tab_hbm.at[0:4], tab.at[0:4])]
    low_loads = load_rows(pl.ds(0, STRIP)) + [load(tab_hbm.at[4:], tab.at[4:])]
    middle_loads = load_rows(pl.ds(STRIP, top - STRIP))
    table_load = load(mats_hbm, mats)

    ix, iy = lax.axis_index("gx"), lax.axis_index("gy")
    nx, ny = counts
    left = (jnp.where(ix == 0, nx - 1, ix - 1), iy)
    right = (jnp.where(ix == nx - 1, 0, ix + 1), iy)
    below = (ix, jnp.where(iy == 0, ny - 1, iy - 1))
    above = (ix, jnp.where(iy == ny - 1, 0, iy + 1))
    first_y, last_y = iy == 0, iy == ny - 1
    barrier = pltpu.get_barrier_semaphore()

    def tell(semaphore, neighbour, when=None):
        def signal():
            pl.semaphore_signal(semaphore, inc=1, device_id=neighbour, device_id_type=MESH)

        signal() if when is None else pl.when(when)(signal)

    tell(barrier, left)
    tell(barrier, above, jnp.logical_not(last_y))
    tell(barrier, below, first_y)
    heard = 1 + jnp.where(first_y, 0, 1) + jnp.where(last_y, 1, 0)

    def message(place, source, target, device):
        return pltpu.make_async_remote_copy(
            src_ref=source,
            dst_ref=target,
            send_sem=send_sem.at[place],
            recv_sem=recv_sem.at[place],
            device_id=device,
            device_id_type=MESH,
        )

    def send(*what):
        copy = message(*what)
        copy.start()
        return copy

    def take_x_edge(side, edge):
        for p in range(planes):
            xs[side, 0, p : p + 1, :] = fld[p, edge : edge + 1, :]
            xs[side, 1, p : p + 1, :] = kap[p, edge : edge + 1, :]

    def sum_x_edge(side, start, place):
        with_first, with_second = twice(tab[place, 0:STRIP]), twice(tab[place + 1, 0:STRIP])
        for p in range(planes):
            rows = fld[p, start : start + STRIP, :]
            krows = kap[p, start : start + STRIP, :]
            xs[side, 2, p : p + 1, :] = jnp.sum(rows * with_first, axis=0, keepdims=True)
            xs[side, 3, p : p + 1, :] = jnp.sum(rows * with_second, axis=0, keepdims=True)
            xs[side, 4, p : p + 1, :] = jnp.sum(krows * with_first, axis=0, keepdims=True)

    for copy in high_loads:
        copy.wait()
    take_x_edge(1, cells_x - 1)
    pl.semaphore_wait(barrier, heard)
    to_right = [send(1, xs.at[1, 0:2], xr.at[0, 0:2], right)]
    sum_x_edge(1, top, 0)
    to_right.append(send(2, xs.at[1, 2:5], xr.at[0, 2:5], right))
    tell(left_ready, right)
    tell(above_ready, below, jnp.logical_not(first_y))
    tell(below_ready, above, last_y)
    for copy in low_loads:
        copy.wait()
    take_x_edge(0, 0)
    sum_x_edge(0, 0, 2)

    for copy in middle_loads:
        copy.wait()
    ys[:, :, 5:8, :] = jnp.zeros((2, planes, 3, 128), jnp.float32)
    lane = lax.broadcasted_iota(jnp.int32, (cells_x, 128), 1)
    for p in range(planes):
        f_low, f_high = fld[p, :, 0:128], fld[p, :, cells_y - 128 : cells_y]
        k_low, k_high = kap[p, :, 0:128], kap[p, :, cells_y - 128 : cells_y]
        packed = jnp.where(
            lane < REACH,
            f_low,
            jnp.where(
                lane < 2 * REACH,
                pltpu.roll(k_low, REACH, 1),
                jnp.where(lane < 3 * REACH, pltpu.roll(k_high, 128 - REACH, 1), f_high),
            ),
        )
        turned = packed.T
        for side, place, f_part, k_part, f_edge, k_edge in (
            (0, 6, turned[0:32], turned[32:64], turned[0:1], turned[32:33]),
            (1, 4, turned[96:128], turned[64:96], turned[127:128], turned[95:96]),
        ):
            with_first, with_second = tab[place], tab[place + 1]
            ys[side, p, 0:1, :] = jnp.sum(f_part * with_first, axis=0, keepdims=True)
            ys[side, p, 1:2, :] = jnp.sum(f_part * with_second, axis=0, keepdims=True)
            ys[side, p, 2:3, :] = f_edge
            ys[side, p, 3:4, :] = jnp.sum(k_part * with_first, axis=0, keepdims=True)
            ys[side, p, 4:5, :] = k_edge
    pl.when(first_y)(lambda: pl.semaphore_wait(below_ready, 1))
    to_below = send(3, ys.at[0], yr.at[1], below)
    pl.when(jnp.logical_not(last_y))(lambda: pl.semaphore_wait(above_ready, 1))
    to_above = send(4, ys.at[1], yr.at[0], above)

    to_left = message(0, xs.at[0], xr.at[1], left)
    run_begins = lax.rem(ix, RUN) == 0

    def send_left():
        pl.semaphore_wait(left_ready, 1)
        to_left.start()

    pl.when(jnp.logical_not(run_begins))(send_left)

    table_load.wait()
    x_rows = 4 * cells_x
    y_first = slice(x_rows, x_rows + 3 * cells_y)
    y_second = slice(x_rows + 3 * cells_y, x_rows + 6 * cells_y)
    end_rows = x_rows + 6 * cells_y

    def local_pair(pair, carry):
        tall, ktall = [], []
        for q in range(2):
            p = 2 * pair + q
            f, k = fld[p], kap[p]
            high, low = split(pltpu.roll(f, cells_x - 1, 0) - f)
            along = matmul(mats[0:x_rows, :], jnp.concatenate([high, low], axis=0))
            gx[p] = along[0:cells_x] + along[cells_x : 2 * cells_x]
            curv[p] = along[2 * cells_x : 3 * cells_x] + along[3 * cells_x : 4 * cells_x]
            high, low = split(pltpu.roll(k, cells_x - 1, 0) - k)
            along = matmul(mats[0 : 2 * cells_x, :], jnp.concatenate([high, low], axis=0))
            kx[p] = along[0:cells_x] + along[cells_x : 2 * cells_x]
            high, low = split(pltpu.roll(f, cells_y - 1, 1) - f)
            tall.append(jnp.concatenate([high, low, high], axis=1))
            high, low = split(pltpu.roll(k, cells_y - 1, 1) - k)
            ktall.append(jnp.concatenate([high, low, high], axis=1))
        across = matmul(jnp.concatenate(tall + ktall, axis=0), mats[y_first, :])
        bend = matmul(jnp.concatenate(tall, axis=0), mats[y_second, :])
        for q in range(2):
            p = 2 * pair + q
            gy[p] = across[q * cells_x : (q + 1) * cells_x]
            ky[p] = across[(q + 2) * cells_x : (q + 3) * cells_x]
            curv[p] = curv[p] + bend[q * cells_x : (q + 1) * cells_x]
        return carry

    lax.fori_loop(0, planes // 2, local_pair, 0)

    to_below.wait_recv()
    to_above.wait_recv()
    row = lax.broadcasted_iota(jnp.int32, (8, 128), 0)
    is_edge = (row == 2) | (row == 4)

    def finish_pair(pair, carry):
        stacks = []
        for q in range(2):
            p = 2 * pair + q
            from_below, from_above = yr[0, p], yr[1, p]
            from_below = jnp.where(is_edge, ys[0, p] - from_below, from_below)
            from_above = jnp.where(is_edge, from_above - ys[1, p], from_above)
            ends = jnp.concatenate([from_below, from_above], axis=0)
            high = ends.astype(jnp.bfloat16).astype(jnp.float32)
            blank = jnp.zeros((FULL - 48, cells_x), jnp.float32)
            stacks.append(jnp.concatenate([high, ends - high, high, blank], axis=0).T)
        turned = jnp.concatenate(stacks, axis=0).astype(jnp.bfloat16)
        reach = [
            matmul(turned, mats[end_rows + n * FULL : end_rows + (n + 1) * FULL, :]) for n in range(3)
        ]
        for q in range(2):
            p = 2 * pair + q
            rows = slice(q * cells_x, (q + 1) * cells_x)
            grad = gy[p] + reach[0][rows]
            gy[p] = grad
            part = kap[p] * (curv[p] + reach[1][rows]) + (ky[p] + reach[2][rows]) * grad
            inner = slice(STRIP, top)
            dif[p, 0:STRIP, :] = part[0:STRIP]
            dif[p, inner, :] = part[inner] + kx[p, inner, :] * gx[p, inner, :]
            dif[p, top:, :] = part[top:]
        return carry

    lax.fori_loop(0, planes // 2, finish_pair, 0)
    pl.when(run_begins)(send_left)

    def combine(side, out):
        sign = 1.0 if side == 0 else -1.0
        jump = sign * (xs[side, 0] - xr[side, 0])
        kjump = sign * (xs[side, 1] - xr[side, 1])
        out[0] = FIRST.rho * xr[side, 2] + jump
        out[1] = SECOND.rho * xr[side, 3] + jump
        out[2] = jump
        out[3] = FIRST.rho * xr[side, 4] + kjump
        out[4] = kjump

    to_left.wait_recv()
    combine(1, xh)
    columns = [twice(tab[n, 0:STRIP]) for n in (8, 9)] + [twice(tab[n, 0:8]) for n in (10, 11)]
    for p in range(planes):
        gx[p, top:, :], dif[p, top:, :] = ends_applied(
            1,
            gx[p, top:, :],
            kx[p, top:, :],
            dif[p, top:, :],
            kap[p, top:, :],
            columns,
            [xh[n, p : p + 1, :] for n in range(5)],
        )
    for copy in [to_left, to_below, to_above] + to_right:
        copy.wait_send()
    for copy in to_right:
        copy.wait_recv()
    combine(0, xc)


def writes_early():
    return (lax.axis_index("gx") == 0) & (lax.axis_index("gy") != 0)


def early_kernel(f_hbm, mats_hbm, gx_out, fld, mats, gx, in_sem, out_sem):
    planes, cells_x, _ = fld.shape
    inner = pl.ds(STRIP, cells_x - 2 * STRIP)

    @pl.when(writes_early())
    def work():
        table_load = pltpu.make_async_copy(
            mats_hbm.at[pl.ds(0, 2 * cells_x), :], mats, in_sem.at[planes]
        )
        table_load.start()
        loads, stores = [], []
        for p in range(planes):
            loads.append(pltpu.make_async_copy(f_hbm.at[p], fld.at[p], in_sem.at[p]))
            loads[p].start()
        table_load.wait()
        for p in range(planes):
            loads[p].wait()
            high, low = split(pltpu.roll(fld[p], cells_x - 1, 0) - fld[p])
            along = matmul(mats[...], jnp.concatenate([high, low], axis=0))
            gx[p] = along[0:cells_x] + along[cells_x : 2 * cells_x]
            stores.append(
                pltpu.make_async_copy(gx.at[p, inner, :], gx_out.at[p, inner, :], out_sem.at[p])
            )
            stores[p].start()
        for copy in stores:
            copy.wait()


def finish_kernel(started, gx, gy, dif, kx, kap, xc, tab, gx_out, gy_out, dif_out, gs, ds, sem):
    planes, cells_x, cells_y = gx.shape
    top = cells_x - STRIP
    early = writes_early()

    def copy_of(place, source, target):
        return pltpu.make_async_copy(source, target, sem.at[place])

    rest, high, inner = pl.ds(STRIP, top), pl.ds(top, STRIP), pl.ds(STRIP, top - STRIP)
    copies = [
        copy_of(0, gy, gy_out),
        copy_of(1, dif.at[:, rest, :], dif_out.at[:, rest, :]),
        copy_of(2, gx.at[:, high, :], gx_out.at[:, high, :]),
    ]
    for copy in copies:
        copy.start()
    inner_copy = copy_of(3, gx.at[:, inner, :], gx_out.at[:, inner, :])
    pl.when(jnp.logical_not(early))(inner_copy.start)
    columns = [twice(tab[n, 0:STRIP]) for n in (0, 1)] + [twice(tab[n, 0:8]) for n in (2, 3)]
    for p in range(planes):
        gs[p], ds[p] = ends_applied(
            0,
            gx[p, 0:STRIP, :],
            kx[p, 0:STRIP, :],
            dif[p, 0:STRIP, :],
            kap[p, 0:STRIP, :],
            columns,
            [xc[n, p : p + 1, :] for n in range(5)],
        )
    low = pl.ds(0, STRIP)
    for place, source, target in ((4, gs, gx_out), (5, ds, dif_out)):
        copies.append(copy_of(place, source, target.at[:, low, :]))
        copies[-1].start()
    pl.when(jnp.logical_not(early))(inner_copy.wait)
    for copy in copies:
        copy.wait()


def local(counts, scalar, diffusivity):
    block = scalar.shape
    planes, cells_x, cells_y = block
    columns = sum_columns(STRIP) + sum_columns(REACH) + high_end_columns()
    tables = (
        jnp.asarray(stacked(columns)),
        jnp.asarray(
            np.concatenate([x_table(cells_x), y_table(cells_y), y_end_table(cells_y)], axis=0)
        ),
    )
    vmem, hbm = pl.BlockSpec(memory_space=pltpu.VMEM), pl.BlockSpec(memory_space=pltpu.HBM)
    field = jax.ShapeDtypeStruct(block, jnp.float32)
    field_buffer = pltpu.VMEM(block, jnp.float32)
    ends_shape = (5, planes, cells_y)
    operands = [
        pltpu.with_memory_space_constraint(array, pltpu.HBM)
        for array in (scalar, diffusivity) + tables
    ]
    started = pl.pallas_call(
        early_kernel,
        out_shape=field,
        in_specs=[hbm] * 2,
        out_specs=hbm,
        scratch_shapes=[
            field_buffer,
            pltpu.VMEM((2 * cells_x, tables[1].shape[1]), tables[1].dtype),
            field_buffer,
            pltpu.SemaphoreType.DMA((planes + 1,)),
            pltpu.SemaphoreType.DMA((planes,)),
        ],
        compiler_params=pltpu.CompilerParams(vmem_limit_bytes=LIMIT),
        name="early",
    )(operands[0], operands[3])
    parts = pl.pallas_call(
        functools.partial(exchange_kernel, counts),
        out_shape=(field,) * 5 + (jax.ShapeDtypeStruct(ends_shape, jnp.float32),),
        in_specs=[hbm] * 4,
        out_specs=(vmem,) * 6,
        scratch_shapes=[field_buffer]
        + [pltpu.VMEM(table.shape, table.dtype) for table in tables]
        + [field_buffer, field_buffer]
        + [pltpu.VMEM((2,) + ends_shape, jnp.float32)] * 2
        + [pltpu.VMEM((2, planes, 8, cells_x), jnp.float32)] * 2
        + [
            pltpu.VMEM(ends_shape, jnp.float32),
            pltpu.SemaphoreType.DMA((9,)),
            pltpu.SemaphoreType.DMA((5,)),
            pltpu.SemaphoreType.DMA((5,)),
            pltpu.SemaphoreType.REGULAR,
            pltpu.SemaphoreType.REGULAR,
            pltpu.SemaphoreType.REGULAR,
        ],
        compiler_params=pltpu.CompilerParams(
            collective_id=0, has_side_effects=True, vmem_limit_bytes=LIMIT
        ),
        name="exchange",
    )(*operands)
    strip_buffer = pltpu.VMEM((planes, STRIP, cells_y), jnp.float32)
    return pl.pallas_call(
        finish_kernel,
        out_shape=(field,) * 3,
        in_specs=[hbm] + [vmem] * 7,
        out_specs=(hbm,) * 3,
        scratch_shapes=[strip_buffer, strip_buffer, pltpu.SemaphoreType.DMA((6,))],
        input_output_aliases={0: 0},
        compiler_params=pltpu.CompilerParams(vmem_limit_bytes=LIMIT),
        name="finish",
    )(started, *parts, jnp.asarray(stacked(low_end_columns())))


def solution(mesh):
    placed = P(None, "gx", "gy")
    return jax.shard_map(
        functools.partial(local, (mesh.shape["gx"], mesh.shape["gy"])),
        mesh=mesh,
        in_specs=(placed, placed),
        out_specs=(placed,) * 3,
        check_vma=False,
    )
```

```python
import functools

import jax
import jax.numpy as jnp
import numpy as np
from jax import lax
from jax.experimental import pallas as pl
from jax.experimental.pallas import tpu as pltpu
from jax.sharding import PartitionSpec as P

FIRST_ALPHA = 1.0 / 3.0
FIRST_A = 14.0 / 9.0
FIRST_B = 1.0 / 9.0
SECOND_ALPHA = 2.0 / 11.0
SECOND_A = 12.0 / 11.0
SECOND_B = 3.0 / 11.0
MESH = pl.DeviceIdType.MESH
STRIP = 24
REACH = 32
FULL = 128
RUN = 8


class Line:
    def __init__(self, alpha, taps):
        root = np.sqrt(1.0 - 4.0 * alpha * alpha)
        self.rho = (root - 1.0) / (2.0 * alpha)
        self.root, self.taps = root, taps
        self.ahead = sum(c * self.rho**m for m, c in taps.items()) / root
        self.behind = sum(c * self.rho**-m for m, c in taps.items()) / root

    def weight(self, n):
        n = np.asarray(n)
        return sum(c * self.rho ** np.abs(n + m) for m, c in self.taps.items()) / self.root

    def local(self, cells):
        i = np.arange(cells)
        table = self.weight(i[:, None] - i[None, :])
        table[:, cells - 1] = 0.0
        return table

    def low_sum(self, reach):
        power = self.rho ** np.arange(reach - 1)
        weights = np.zeros(reach)
        weights[1:] += power
        weights[:-1] -= power
        return weights


FIRST = Line(
    FIRST_ALPHA,
    {
        1: 0.25 * FIRST_B,
        0: 0.5 * FIRST_A + 0.25 * FIRST_B,
        -1: 0.5 * FIRST_A + 0.25 * FIRST_B,
        -2: 0.25 * FIRST_B,
    },
)
SECOND = Line(
    SECOND_ALPHA,
    {
        1: 0.25 * SECOND_B,
        0: SECOND_A + 0.25 * SECOND_B,
        -1: -SECOND_A - 0.25 * SECOND_B,
        -2: -0.25 * SECOND_B,
    },
)


def halves(table):
    high = np.asarray(table, np.float32).astype(jnp.bfloat16)
    low = (table - high.astype(np.float64)).astype(np.float32).astype(jnp.bfloat16)
    return high, low


def stacked(columns):
    table = np.zeros((len(columns), 32, 128), np.float32)
    for place, column in enumerate(columns):
        table[place, : len(column)] = column[:, None]
    return table


def sum_columns(reach):
    low = [FIRST.low_sum(reach), SECOND.low_sum(reach)]
    return [-row[::-1] for row in low] + low


def high_end_columns():
    r = np.arange(STRIP)[::-1]
    columns = [(line.behind * line.rho**r) for line in (FIRST, SECOND)]
    for line in (FIRST, SECOND):
        column = np.zeros(8)
        column[7] = line.weight(0) - line.behind
        columns.append(column)
    return columns


def low_end_columns():
    r = np.arange(STRIP)
    columns = [(line.ahead * line.rho ** (r + 1)) for line in (FIRST, SECOND)]
    for line in (FIRST, SECOND):
        column = np.zeros(8)
        column[0] = line.weight(1) - line.ahead * line.rho
        columns.append(column)
    return columns


def x_table(cells):
    rows = []
    for line in (FIRST, SECOND):
        for half in halves(line.local(cells)):
            rows.append(np.concatenate([half, half], axis=1))
    return np.concatenate(rows, axis=0)


def y_table(cells):
    rows = []
    for line in (FIRST, SECOND):
        high, low = halves(line.local(cells).T)
        rows += [high, high, low]
    return np.concatenate(rows, axis=0)


def y_end_table(cells):
    i = np.arange(cells)
    blocks = []
    for line, sum_row, edge_row in ((FIRST, 0, 2), (SECOND, 1, 2), (FIRST, 3, 4)):
        table = np.zeros((16, cells))
        table[sum_row] = line.ahead * line.rho ** (i + 2)
        table[edge_row] = line.weight(i + 1)
        table[8 + sum_row] = line.behind * line.rho ** (cells - i)
        table[8 + edge_row] = line.weight(i - cells + 1)
        high, low = halves(table)
        blank = np.zeros((FULL - 48, cells), high.dtype)
        blocks += [high, high, low, blank]
    return np.concatenate(blocks, axis=0)


def split(values):
    high = values.astype(jnp.bfloat16)
    low = (values - high.astype(jnp.float32)).astype(jnp.bfloat16)
    return high, low


def matmul(left, right):
    return jnp.dot(left, right, preferred_element_type=jnp.float32)


def twice(tile):
    return jnp.concatenate([tile, tile], axis=1)


def ends_applied(side, grad, kgrad, part, kappa, columns, values):
    decay, decay_second, end, end_second = columns
    first, second, jump, kfirst, kjump = values
    grads, parts = [], []
    for tile in range(STRIP // 8):
        r = slice(8 * tile, 8 * tile + 8)
        g = grad[r] + decay[r] * first
        k = kgrad[r] + decay[r] * kfirst
        distance = tile if side == 0 else STRIP // 8 - 1 - tile
        d = part[r]
        if distance < 2:
            bend = decay_second[r] * second
            if distance == 0:
                g = g + end * jump
                k = k + end * kjump
                bend = bend + end_second * jump
            d = d + kappa[r] * bend
        grads.append(g)
        parts.append(d + k * g)
    return jnp.concatenate(grads, axis=0), jnp.concatenate(parts, axis=0)


def sums_kernel(f_hbm, k_hbm, tab_hbm, out, fst, kst, tab, sem):
    planes, cells_x = f_hbm.shape[0], f_hbm.shape[1]
    rows = pl.ds(cells_x - STRIP, STRIP)
    copies = [
        pltpu.make_async_copy(f_hbm.at[:, rows, :], fst, sem.at[0]),
        pltpu.make_async_copy(k_hbm.at[:, rows, :], kst, sem.at[1]),
        pltpu.make_async_copy(tab_hbm.at[0:2], tab, sem.at[2]),
    ]
    for copy in copies:
        copy.start()
    for copy in copies:
        copy.wait()
    with_first, with_second = twice(tab[0, 0:STRIP]), twice(tab[1, 0:STRIP])
    for p in range(planes):
        out[0, p : p + 1, :] = fst[p, STRIP - 1 : STRIP, :]
        out[1, p : p + 1, :] = kst[p, STRIP - 1 : STRIP, :]
        out[2, p : p + 1, :] = jnp.sum(fst[p] * with_first, axis=0, keepdims=True)
        out[3, p : p + 1, :] = jnp.sum(fst[p] * with_second, axis=0, keepdims=True)
        out[4, p : p + 1, :] = jnp.sum(kst[p] * with_first, axis=0, keepdims=True)


def exchange_kernel(
    counts,
    f_hbm,
    k_hbm,
    tab_hbm,
    mats_hbm,
    gx,
    gy,
    dif,
    kx,
    kap,
    xc,
    fld,
    tab,
    mats,
    curv,
    ky,
    xs,
    xr,
    ys,
    yr,
    xh,
    in_sem,
    send_sem,
    recv_sem,
    left_ready,
    above_ready,
):
    planes, cells_x, cells_y = fld.shape
    top = cells_x - STRIP
    loads = []

    def load(source, target):
        copy = pltpu.make_async_copy(source, target, in_sem.at[len(loads)])
        copy.start()
        loads.append(copy)
        return copy

    def load_rows(rows):
        return [
            load(f_hbm.at[:, rows, :], fld.at[:, rows, :]),
            load(k_hbm.at[:, rows, :], kap.at[:, rows, :]),
        ]

    high_loads = load_rows(pl.ds(top, STRIP)) + [load(tab_hbm, tab)]
    low_loads = load_rows(pl.ds(0, STRIP))
    middle_loads = load_rows(pl.ds(STRIP, top - STRIP))
    table_load = load(mats_hbm, mats)

    ix, iy = lax.axis_index("gx"), lax.axis_index("gy")
    nx, ny = counts
    left = (jnp.where(ix == 0, nx - 1, ix - 1), iy)
    right = (jnp.where(ix == nx - 1, 0, ix + 1), iy)
    below = (ix, jnp.where(iy == 0, ny - 1, iy - 1))
    above = (ix, jnp.where(iy == ny - 1, 0, iy + 1))
    barrier = pltpu.get_barrier_semaphore()
    for neighbour in (left, above):
        pl.semaphore_signal(barrier, inc=1, device_id=neighbour, device_id_type=MESH)

    def message(place, source, target, device):
        return pltpu.make_async_remote_copy(
            src_ref=source,
            dst_ref=target,
            send_sem=send_sem.at[place],
            recv_sem=recv_sem.at[place],
            device_id=device,
            device_id_type=MESH,
        )

    def send(*what):
        copy = message(*what)
        copy.start()
        return copy

    def take_x_edge(side, edge):
        for p in range(planes):
            xs[side, 0, p : p + 1, :] = fld[p, edge : edge + 1, :]
            xs[side, 1, p : p + 1, :] = kap[p, edge : edge + 1, :]

    def sum_x_edge(side, start, place):
        with_first, with_second = twice(tab[place, 0:STRIP]), twice(tab[place + 1, 0:STRIP])
        for p in range(planes):
            rows = fld[p, start : start + STRIP, :]
            krows = kap[p, start : start + STRIP, :]
            xs[side, 2, p : p + 1, :] = jnp.sum(rows * with_first, axis=0, keepdims=True)
            xs[side, 3, p : p + 1, :] = jnp.sum(rows * with_second, axis=0, keepdims=True)
            xs[side, 4, p : p + 1, :] = jnp.sum(krows * with_first, axis=0, keepdims=True)

    for copy in high_loads:
        copy.wait()
    take_x_edge(1, cells_x - 1)
    pl.semaphore_wait(barrier, 2)
    pl.semaphore_signal(left_ready, inc=1, device_id=right, device_id_type=MESH)
    pl.semaphore_signal(above_ready, inc=1, device_id=below, device_id_type=MESH)
    for copy in low_loads:
        copy.wait()
    take_x_edge(0, 0)
    sum_x_edge(0, 0, 2)

    for copy in middle_loads:
        copy.wait()
    ys[:, :, 5:8, :] = jnp.zeros((2, planes, 3, 128), jnp.float32)
    lane = lax.broadcasted_iota(jnp.int32, (cells_x, 128), 1)
    for p in range(planes):
        f_low, f_high = fld[p, :, 0:128], fld[p, :, cells_y - 128 : cells_y]
        k_low, k_high = kap[p, :, 0:128], kap[p, :, cells_y - 128 : cells_y]
        packed = jnp.where(
            lane < REACH,
            f_low,
            jnp.where(
                lane < 2 * REACH,
                pltpu.roll(k_low, REACH, 1),
                jnp.where(lane < 3 * REACH, pltpu.roll(k_high, 128 - REACH, 1), f_high),
            ),
        )
        turned = packed.T
        for side, place, f_part, k_part, f_edge, k_edge in (
            (0, 6, turned[0:32], turned[32:64], turned[0:1], turned[32:33]),
            (1, 4, turned[96:128], turned[64:96], turned[127:128], turned[95:96]),
        ):
            with_first, with_second = tab[place], tab[place + 1]
            ys[side, p, 0:1, :] = jnp.sum(f_part * with_first, axis=0, keepdims=True)
            ys[side, p, 1:2, :] = jnp.sum(f_part * with_second, axis=0, keepdims=True)
            ys[side, p, 2:3, :] = f_edge
            ys[side, p, 3:4, :] = jnp.sum(k_part * with_first, axis=0, keepdims=True)
            ys[side, p, 4:5, :] = k_edge
    to_below = send(3, ys.at[0], yr.at[1], below)
    pl.semaphore_wait(above_ready, 1)
    to_above = send(4, ys.at[1], yr.at[0], above)

    to_left = message(0, xs.at[0], xr.at[1], left)
    run_begins = lax.rem(ix, RUN) == 0

    def send_left():
        pl.semaphore_wait(left_ready, 1)
        to_left.start()

    pl.when(jnp.logical_not(run_begins))(send_left)

    table_load.wait()
    x_rows = 4 * cells_x
    y_first = slice(x_rows, x_rows + 3 * cells_y)
    y_second = slice(x_rows + 3 * cells_y, x_rows + 6 * cells_y)
    end_rows = x_rows + 6 * cells_y

    def local_pair(pair, carry):
        tall, ktall = [], []
        for q in range(2):
            p = 2 * pair + q
            f, k = fld[p], kap[p]
            high, low = split(pltpu.roll(f, cells_x - 1, 0) - f)
            along = matmul(mats[0:x_rows, :], jnp.concatenate([high, low], axis=0))
            gx[p] = along[0:cells_x] + along[cells_x : 2 * cells_x]
            curv[p] = along[2 * cells_x : 3 * cells_x] + along[3 * cells_x : 4 * cells_x]
            high, low = split(pltpu.roll(k, cells_x - 1, 0) - k)
            along = matmul(mats[0 : 2 * cells_x, :], jnp.concatenate([high, low], axis=0))
            kx[p] = along[0:cells_x] + along[cells_x : 2 * cells_x]
            high, low = split(pltpu.roll(f, cells_y - 1, 1) - f)
            tall.append(jnp.concatenate([high, low, high], axis=1))
            high, low = split(pltpu.roll(k, cells_y - 1, 1) - k)
            ktall.append(jnp.concatenate([high, low, high], axis=1))
        across = matmul(jnp.concatenate(tall + ktall, axis=0), mats[y_first, :])
        bend = matmul(jnp.concatenate(tall, axis=0), mats[y_second, :])
        for q in range(2):
            p = 2 * pair + q
            gy[p] = across[q * cells_x : (q + 1) * cells_x]
            ky[p] = across[(q + 2) * cells_x : (q + 3) * cells_x]
            curv[p] = curv[p] + bend[q * cells_x : (q + 1) * cells_x]
        return carry

    lax.fori_loop(0, planes // 2, local_pair, 0)

    to_below.wait_recv()
    to_above.wait_recv()
    row = lax.broadcasted_iota(jnp.int32, (8, 128), 0)
    is_edge = (row == 2) | (row == 4)

    def finish_pair(pair, carry):
        stacks = []
        for q in range(2):
            p = 2 * pair + q
            from_below, from_above = yr[0, p], yr[1, p]
            from_below = jnp.where(is_edge, ys[0, p] - from_below, from_below)
            from_above = jnp.where(is_edge, from_above - ys[1, p], from_above)
            ends = jnp.concatenate([from_below, from_above], axis=0)
            high = ends.astype(jnp.bfloat16).astype(jnp.float32)
            blank = jnp.zeros((FULL - 48, cells_x), jnp.float32)
            stacks.append(jnp.concatenate([high, ends - high, high, blank], axis=0).T)
        turned = jnp.concatenate(stacks, axis=0).astype(jnp.bfloat16)
        reach = [
            matmul(turned, mats[end_rows + n * FULL : end_rows + (n + 1) * FULL, :]) for n in range(3)
        ]
        for q in range(2):
            p = 2 * pair + q
            rows = slice(q * cells_x, (q + 1) * cells_x)
            grad = gy[p] + reach[0][rows]
            gy[p] = grad
            part = kap[p] * (curv[p] + reach[1][rows]) + (ky[p] + reach[2][rows]) * grad
            inner = slice(STRIP, top)
            dif[p, 0:STRIP, :] = part[0:STRIP]
            dif[p, inner, :] = part[inner] + kx[p, inner, :] * gx[p, inner, :]
            dif[p, top:, :] = part[top:]
        return carry

    lax.fori_loop(0, planes // 2, finish_pair, 0)
    pl.when(run_begins)(send_left)

    def combine(side, out):
        sign = 1.0 if side == 0 else -1.0
        jump = sign * (xs[side, 0] - xr[side, 0])
        kjump = sign * (xs[side, 1] - xr[side, 1])
        out[0] = FIRST.rho * xr[side, 2] + jump
        out[1] = SECOND.rho * xr[side, 3] + jump
        out[2] = jump
        out[3] = FIRST.rho * xr[side, 4] + kjump
        out[4] = kjump

    to_left.wait_recv()
    combine(1, xh)
    columns = [twice(tab[n, 0:STRIP]) for n in (8, 9)] + [twice(tab[n, 0:8]) for n in (10, 11)]
    for p in range(planes):
        gx[p, top:, :], dif[p, top:, :] = ends_applied(
            1,
            gx[p, top:, :],
            kx[p, top:, :],
            dif[p, top:, :],
            kap[p, top:, :],
            columns,
            [xh[n, p : p + 1, :] for n in range(5)],
        )
    xc[0] = xs[0, 0]
    xc[1] = xs[0, 1]
    for copy in (to_left, to_below, to_above):
        copy.wait_send()


def bulk_kernel(gx, gy, dif, gx_out, gy_out, dif_out, sem):
    rest = pl.ds(STRIP, gx.shape[1] - STRIP)
    copies = [
        pltpu.make_async_copy(gy, gy_out, sem.at[0]),
        pltpu.make_async_copy(gx.at[:, rest, :], gx_out.at[:, rest, :], sem.at[1]),
        pltpu.make_async_copy(dif.at[:, rest, :], dif_out.at[:, rest, :], sem.at[2]),
    ]
    for copy in copies:
        copy.start()
    for copy in copies:
        copy.wait()


def finish_kernel(gx_in, dif_in, gx, dif, kx, kap, edges, came, tab, gx_out, dif_out, gs, ds, xc, sem):
    planes = gx.shape[0]
    jump, kjump = edges[0] - came[0], edges[1] - came[1]
    xc[0] = FIRST.rho * came[2] + jump
    xc[1] = SECOND.rho * came[3] + jump
    xc[2] = jump
    xc[3] = FIRST.rho * came[4] + kjump
    xc[4] = kjump
    columns = [twice(tab[n, 0:STRIP]) for n in (0, 1)] + [twice(tab[n, 0:8]) for n in (2, 3)]
    low = pl.ds(0, STRIP)
    copies = []
    for p in range(planes):
        gs[p], ds[p] = ends_applied(
            0,
            gx[p, 0:STRIP, :],
            kx[p, 0:STRIP, :],
            dif[p, 0:STRIP, :],
            kap[p, 0:STRIP, :],
            columns,
            [xc[n, p : p + 1, :] for n in range(5)],
        )
        if p % 4 == 3:
            some = pl.ds(p - 3, 4)
            for source, target in ((gs, gx_out), (ds, dif_out)):
                copies.append(
                    pltpu.make_async_copy(
                        source.at[some], target.at[some, low, :], sem.at[len(copies)]
                    )
                )
                copies[-1].start()
    for copy in copies:
        copy.wait()


def local(counts, scalar, diffusivity):
    block = scalar.shape
    planes, cells_x, cells_y = block
    columns = sum_columns(STRIP) + sum_columns(REACH) + high_end_columns()
    tables = (
        jnp.asarray(stacked(columns)),
        jnp.asarray(
            np.concatenate([x_table(cells_x), y_table(cells_y), y_end_table(cells_y)], axis=0)
        ),
    )
    vmem, hbm = pl.BlockSpec(memory_space=pltpu.VMEM), pl.BlockSpec(memory_space=pltpu.HBM)
    field = jax.ShapeDtypeStruct(block, jnp.float32)
    field_buffer = pltpu.VMEM(block, jnp.float32)
    ends_shape = (5, planes, cells_y)
    operands = [
        pltpu.with_memory_space_constraint(array, pltpu.HBM)
        for array in (scalar, diffusivity) + tables
    ]
    strip_shape = (planes, STRIP, cells_y)
    message = pl.pallas_call(
        sums_kernel,
        out_shape=jax.ShapeDtypeStruct(ends_shape, jnp.float32),
        in_specs=[hbm] * 3,
        out_specs=vmem,
        scratch_shapes=[
            pltpu.VMEM(strip_shape, jnp.float32),
            pltpu.VMEM(strip_shape, jnp.float32),
            pltpu.VMEM((2, 32, 128), jnp.float32),
            pltpu.SemaphoreType.DMA((3,)),
        ],
        compiler_params=pltpu.CompilerParams(vmem_limit_bytes=28 * 1024 * 1024),
        name="sums",
    )(*operands[:3])
    came = lax.ppermute(message, "gx", [(i, (i + 1) % counts[0]) for i in range(counts[0])])
    parts = pl.pallas_call(
        functools.partial(exchange_kernel, counts),
        out_shape=(field,) * 5 + (jax.ShapeDtypeStruct((2,) + ends_shape[1:], jnp.float32),),
        in_specs=[hbm] * 4,
        out_specs=(vmem,) * 6,
        scratch_shapes=[field_buffer]
        + [pltpu.VMEM(table.shape, table.dtype) for table in tables]
        + [field_buffer, field_buffer]
        + [pltpu.VMEM((2,) + ends_shape, jnp.float32)] * 2
        + [pltpu.VMEM((2, planes, 8, cells_x), jnp.float32)] * 2
        + [
            pltpu.VMEM(ends_shape, jnp.float32),
            pltpu.SemaphoreType.DMA((8,)),
            pltpu.SemaphoreType.DMA((5,)),
            pltpu.SemaphoreType.DMA((5,)),
            pltpu.SemaphoreType.REGULAR,
            pltpu.SemaphoreType.REGULAR,
        ],
        compiler_params=pltpu.CompilerParams(
            collective_id=0, has_side_effects=True, vmem_limit_bytes=28 * 1024 * 1024
        ),
        cost_estimate=pl.CostEstimate(flops=2 * 10**9, bytes_accessed=8 * 2**20, transcendentals=0),
        name="exchange",
    )(*operands)
    strip_buffer = pltpu.VMEM((planes, STRIP, cells_y), jnp.float32)
    grad_x, grad_y, dif, kx, kap, edges = parts
    gx_out, gy_out, dif_out = pl.pallas_call(
        bulk_kernel,
        out_shape=(field,) * 3,
        in_specs=[vmem] * 3,
        out_specs=(hbm,) * 3,
        scratch_shapes=[pltpu.SemaphoreType.DMA((3,))],
        compiler_params=pltpu.CompilerParams(vmem_limit_bytes=28 * 1024 * 1024),
        cost_estimate=pl.CostEstimate(flops=0, bytes_accessed=3 * 2**20, transcendentals=0),
        name="bulk",
    )(grad_x, grad_y, dif)
    gx_out, dif_out = pl.pallas_call(
        finish_kernel,
        out_shape=(field,) * 2,
        in_specs=[hbm] * 2 + [vmem] * 7,
        out_specs=(hbm,) * 2,
        scratch_shapes=[
            strip_buffer,
            strip_buffer,
            pltpu.VMEM(ends_shape, jnp.float32),
            pltpu.SemaphoreType.DMA((4,)),
        ],
        input_output_aliases={0: 0, 1: 1},
        compiler_params=pltpu.CompilerParams(vmem_limit_bytes=28 * 1024 * 1024),
        name="finish",
    )(gx_out, dif_out, grad_x, dif, kx, kap, edges, came, jnp.asarray(stacked(low_end_columns())))
    return gx_out, gy_out, dif_out


def solution(mesh):
    placed = P(None, "gx", "gy")
    return jax.shard_map(
        functools.partial(local, (mesh.shape["gx"], mesh.shape["gy"])),
        mesh=mesh,
        in_specs=(placed, placed),
        out_specs=(placed,) * 3,
        check_vma=False,
    )
```

```python
import functools

import jax
import jax.numpy as jnp
import numpy as np
from jax import lax
from jax.experimental import pallas as pl
from jax.experimental.pallas import tpu as pltpu
from jax.sharding import PartitionSpec as P

FIRST_ALPHA = 1.0 / 3.0
FIRST_A = 14.0 / 9.0
FIRST_B = 1.0 / 9.0
SECOND_ALPHA = 2.0 / 11.0
SECOND_A = 12.0 / 11.0
SECOND_B = 3.0 / 11.0
MESH = pl.DeviceIdType.MESH
LIMIT = 28 * 1024 * 1024
STRIP = 24
REACH = 32
FULL = 128
RUN = 8


class Line:
    def __init__(self, alpha, taps):
        root = np.sqrt(1.0 - 4.0 * alpha * alpha)
        self.rho = (root - 1.0) / (2.0 * alpha)
        self.root, self.taps = root, taps
        self.ahead = sum(c * self.rho**m for m, c in taps.items()) / root
        self.behind = sum(c * self.rho**-m for m, c in taps.items()) / root

    def weight(self, n):
        n = np.asarray(n)
        return sum(c * self.rho ** np.abs(n + m) for m, c in self.taps.items()) / self.root

    def local(self, cells):
        i = np.arange(cells)
        table = self.weight(i[:, None] - i[None, :])
        table[:, cells - 1] = 0.0
        return table

    def low_sum(self, reach):
        power = self.rho ** np.arange(reach - 1)
        weights = np.zeros(reach)
        weights[1:] += power
        weights[:-1] -= power
        return weights


FIRST = Line(
    FIRST_ALPHA,
    {
        1: 0.25 * FIRST_B,
        0: 0.5 * FIRST_A + 0.25 * FIRST_B,
        -1: 0.5 * FIRST_A + 0.25 * FIRST_B,
        -2: 0.25 * FIRST_B,
    },
)
SECOND = Line(
    SECOND_ALPHA,
    {
        1: 0.25 * SECOND_B,
        0: SECOND_A + 0.25 * SECOND_B,
        -1: -SECOND_A - 0.25 * SECOND_B,
        -2: -0.25 * SECOND_B,
    },
)


def halves(table):
    high = np.asarray(table, np.float32).astype(jnp.bfloat16)
    low = (table - high.astype(np.float64)).astype(np.float32).astype(jnp.bfloat16)
    return high, low


def stacked(columns):
    table = np.zeros((len(columns), 32, 128), np.float32)
    for place, column in enumerate(columns):
        table[place, : len(column)] = column[:, None]
    return table


def sum_columns(reach):
    low = [FIRST.low_sum(reach), SECOND.low_sum(reach)]
    return [-row[::-1] for row in low] + low


def high_end_columns():
    r = np.arange(STRIP)[::-1]
    columns = [(line.behind * line.rho**r) for line in (FIRST, SECOND)]
    for line in (FIRST, SECOND):
        column = np.zeros(8)
        column[7] = line.weight(0) - line.behind
        columns.append(column)
    return columns


def low_end_columns():
    r = np.arange(STRIP)
    columns = [(line.ahead * line.rho ** (r + 1)) for line in (FIRST, SECOND)]
    for line in (FIRST, SECOND):
        column = np.zeros(8)
        column[0] = line.weight(1) - line.ahead * line.rho
        columns.append(column)
    return columns


def x_table(cells):
    rows = []
    for line in (FIRST, SECOND):
        for half in halves(line.local(cells)):
            rows.append(np.concatenate([half, half], axis=1))
    return np.concatenate(rows, axis=0)


def y_table(cells):
    rows = []
    for line in (FIRST, SECOND):
        high, low = halves(line.local(cells).T)
        rows += [high, high, low]
    return np.concatenate(rows, axis=0)


def y_end_table(cells):
    i = np.arange(cells)
    blocks = []
    for line, sum_row, edge_row in ((FIRST, 0, 2), (SECOND, 1, 2), (FIRST, 3, 4)):
        table = np.zeros((16, cells))
        table[sum_row] = line.ahead * line.rho ** (i + 2)
        table[edge_row] = line.weight(i + 1)
        table[8 + sum_row] = line.behind * line.rho ** (cells - i)
        table[8 + edge_row] = line.weight(i - cells + 1)
        high, low = halves(table)
        blank = np.zeros((FULL - 48, cells), high.dtype)
        blocks += [high, high, low, blank]
    return np.concatenate(blocks, axis=0)


def split(values):
    high = values.astype(jnp.bfloat16)
    low = (values - high.astype(jnp.float32)).astype(jnp.bfloat16)
    return high, low


def matmul(left, right):
    return jnp.dot(left, right, preferred_element_type=jnp.float32)


def twice(tile):
    return jnp.concatenate([tile, tile], axis=1)


def ends_applied(side, grad, kgrad, part, kappa, columns, values):
    decay, decay_second, end, end_second = columns
    first, second, jump, kfirst, kjump = values
    grads, parts = [], []
    for tile in range(STRIP // 8):
        r = slice(8 * tile, 8 * tile + 8)
        g = grad[r] + decay[r] * first
        k = kgrad[r] + decay[r] * kfirst
        distance = tile if side == 0 else STRIP // 8 - 1 - tile
        d = part[r]
        if distance < 2:
            bend = decay_second[r] * second
            if distance == 0:
                g = g + end * jump
                k = k + end * kjump
                bend = bend + end_second * jump
            d = d + kappa[r] * bend
        grads.append(g)
        parts.append(d + k * g)
    return jnp.concatenate(grads, axis=0), jnp.concatenate(parts, axis=0)


def sums_kernel(f_hbm, k_hbm, tab_hbm, out, fst, kst, tab, sem):
    planes, cells_x = f_hbm.shape[0], f_hbm.shape[1]
    rows = pl.ds(cells_x - STRIP, STRIP)
    copies = [
        pltpu.make_async_copy(f_hbm.at[:, rows, :], fst, sem.at[0]),
        pltpu.make_async_copy(k_hbm.at[:, rows, :], kst, sem.at[1]),
        pltpu.make_async_copy(tab_hbm.at[0:2], tab, sem.at[2]),
    ]
    for copy in copies:
        copy.start()
    for copy in copies:
        copy.wait()
    with_first, with_second = twice(tab[0, 0:STRIP]), twice(tab[1, 0:STRIP])
    for p in range(planes):
        out[0, p : p + 1, :] = fst[p, STRIP - 1 : STRIP, :]
        out[1, p : p + 1, :] = kst[p, STRIP - 1 : STRIP, :]
        out[2, p : p + 1, :] = jnp.sum(fst[p] * with_first, axis=0, keepdims=True)
        out[3, p : p + 1, :] = jnp.sum(fst[p] * with_second, axis=0, keepdims=True)
        out[4, p : p + 1, :] = jnp.sum(kst[p] * with_first, axis=0, keepdims=True)


def exchange_kernel(
    counts,
    f_hbm,
    k_hbm,
    tab_hbm,
    mats_hbm,
    gx,
    kx,
    kap,
    curv,
    gy,
    ky,
    yends,
    xh,
    edges,
    fld,
    tab,
    mats,
    xs,
    xr,
    ys,
    yr,
    in_sem,
    send_sem,
    recv_sem,
    left_ready,
    above_ready,
):
    planes, cells_x, cells_y = fld.shape
    half = planes // 2
    loads = []

    def load(source, target):
        copy = pltpu.make_async_copy(source, target, in_sem.at[len(loads)])
        copy.start()
        loads.append(copy)
        return copy

    table_load = load(tab_hbm, tab)
    field_loads = []
    for part in (pl.ds(0, half), pl.ds(half, half)):
        field_loads.append(
            [load(f_hbm.at[part], fld.at[part]), load(k_hbm.at[part], kap.at[part])]
        )
    mats_load = load(mats_hbm, mats)

    ix, iy = lax.axis_index("gx"), lax.axis_index("gy")
    nx, ny = counts
    left = (jnp.where(ix == 0, nx - 1, ix - 1), iy)
    right = (jnp.where(ix == nx - 1, 0, ix + 1), iy)
    below = (ix, jnp.where(iy == 0, ny - 1, iy - 1))
    above = (ix, jnp.where(iy == ny - 1, 0, iy + 1))
    run_begins, run_ends = lax.rem(ix, RUN) == 0, lax.rem(ix, RUN) == RUN - 1
    run_goes_on = jnp.logical_not(run_ends)
    barrier = pltpu.get_barrier_semaphore()

    def tell(semaphore, neighbour):
        pl.semaphore_signal(semaphore, inc=1, device_id=neighbour, device_id_type=MESH)

    tell(barrier, left)
    tell(barrier, above)
    pl.when(run_goes_on)(lambda: tell(barrier, below))

    def meet():
        pl.semaphore_wait(barrier, jnp.where(run_ends, 2, 3))
        tell(left_ready, right)
        pl.when(run_ends)(lambda: tell(above_ready, below))

    pl.when(run_ends)(meet)

    def message(place, source, target, device):
        return pltpu.make_async_remote_copy(
            src_ref=source,
            dst_ref=target,
            send_sem=send_sem.at[place],
            recv_sem=recv_sem.at[place],
            device_id=device,
            device_id_type=MESH,
        )

    to_left = message(0, xs, xr, left)
    to_below = message(1, ys.at[0], yr.at[1], below)
    to_above = message(2, ys.at[1], yr.at[0], above)

    def send_left():
        pl.semaphore_wait(left_ready, 1)
        to_left.start()

    ys[:, :, 5:8, :] = jnp.zeros((2, planes, 3, 128), jnp.float32)
    lane = lax.broadcasted_iota(jnp.int32, (cells_x, 128), 1)
    table_load.wait()
    for p in range(planes):
        if p % half == 0:
            for copy in field_loads[p // half]:
                copy.wait()
        f_low, f_high = fld[p, :, 0:128], fld[p, :, cells_y - 128 : cells_y]
        k_low, k_high = kap[p, :, 0:128], kap[p, :, cells_y - 128 : cells_y]
        packed = jnp.where(
            lane < REACH,
            f_low,
            jnp.where(
                lane < 2 * REACH,
                pltpu.roll(k_low, REACH, 1),
                jnp.where(lane < 3 * REACH, pltpu.roll(k_high, 128 - REACH, 1), f_high),
            ),
        )
        turned = packed.T
        for side, place, f_part, k_part, f_edge, k_edge in (
            (0, 6, turned[0:32], turned[32:64], turned[0:1], turned[32:33]),
            (1, 4, turned[96:128], turned[64:96], turned[127:128], turned[95:96]),
        ):
            with_first, with_second = tab[place], tab[place + 1]
            ys[side, p, 0:1, :] = jnp.sum(f_part * with_first, axis=0, keepdims=True)
            ys[side, p, 1:2, :] = jnp.sum(f_part * with_second, axis=0, keepdims=True)
            ys[side, p, 2:3, :] = f_edge
            ys[side, p, 3:4, :] = jnp.sum(k_part * with_first, axis=0, keepdims=True)
            ys[side, p, 4:5, :] = k_edge
    with_first, with_second = twice(tab[2, 0:STRIP]), twice(tab[3, 0:STRIP])
    for p in range(planes):
        rows, krows = fld[p, 0:STRIP, :], kap[p, 0:STRIP, :]
        xs[0, p : p + 1, :] = fld[p, 0:1, :]
        xs[1, p : p + 1, :] = kap[p, 0:1, :]
        xs[2, p : p + 1, :] = jnp.sum(rows * with_first, axis=0, keepdims=True)
        xs[3, p : p + 1, :] = jnp.sum(rows * with_second, axis=0, keepdims=True)
        xs[4, p : p + 1, :] = jnp.sum(krows * with_first, axis=0, keepdims=True)
        edges[0, p : p + 1, :] = fld[p, 0:1, :]
        edges[1, p : p + 1, :] = kap[p, 0:1, :]
        edges[2, p : p + 1, :] = fld[p, cells_x - 1 : cells_x, :]
        edges[3, p : p + 1, :] = kap[p, cells_x - 1 : cells_x, :]

    mats_load.wait()
    x_rows = 4 * cells_x
    y_first = slice(x_rows, x_rows + 3 * cells_y)
    y_second = slice(x_rows + 3 * cells_y, x_rows + 6 * cells_y)

    def local_pair(pair, carry):
        tall, ktall = [], []
        for q in range(2):
            p = 2 * pair + q
            f, k = fld[p], kap[p]
            high, low = split(pltpu.roll(f, cells_x - 1, 0) - f)
            along = matmul(mats[0:x_rows, :], jnp.concatenate([high, low], axis=0))
            gx[p] = along[0:cells_x] + along[cells_x : 2 * cells_x]
            curv[p] = along[2 * cells_x : 3 * cells_x] + along[3 * cells_x : 4 * cells_x]
            high, low = split(pltpu.roll(k, cells_x - 1, 0) - k)
            along = matmul(mats[0 : 2 * cells_x, :], jnp.concatenate([high, low], axis=0))
            kx[p] = along[0:cells_x] + along[cells_x : 2 * cells_x]
            high, low = split(pltpu.roll(f, cells_y - 1, 1) - f)
            tall.append(jnp.concatenate([high, low, high], axis=1))
            high, low = split(pltpu.roll(k, cells_y - 1, 1) - k)
            ktall.append(jnp.concatenate([high, low, high], axis=1))
        across = matmul(jnp.concatenate(tall + ktall, axis=0), mats[y_first, :])
        bend = matmul(jnp.concatenate(tall, axis=0), mats[y_second, :])
        for q in range(2):
            p = 2 * pair + q
            gy[p] = across[q * cells_x : (q + 1) * cells_x]
            ky[p] = across[(q + 2) * cells_x : (q + 3) * cells_x]
            curv[p] = curv[p] + bend[q * cells_x : (q + 1) * cells_x]
        return carry

    pairs = planes // 2
    lax.fori_loop(0, pairs // 2, local_pair, 0)

    pl.when(run_goes_on)(meet)
    to_below.start()
    pl.when(run_ends)(lambda: pl.semaphore_wait(above_ready, 1))
    to_above.start()
    pl.when(jnp.logical_not(run_begins))(send_left)

    lax.fori_loop(pairs // 2, pairs, local_pair, 0)

    to_below.wait_recv()
    to_above.wait_recv()
    row = lax.broadcasted_iota(jnp.int32, (8, 128), 0)
    is_edge = (row == 2) | (row == 4)
    for p in range(planes):
        from_below, from_above = yr[0, p], yr[1, p]
        yends[p, 0:8] = jnp.where(is_edge, ys[0, p] - from_below, from_below)
        yends[p, 8:16] = jnp.where(is_edge, from_above - ys[1, p], from_above)
    to_below.wait_send()
    to_above.wait_send()

    pl.when(run_begins)(send_left)
    to_left.wait_recv()
    jump, kjump = xr[0] - edges[2], xr[1] - edges[3]
    xh[0] = FIRST.rho * xr[2] + jump
    xh[1] = SECOND.rho * xr[3] + jump
    xh[2] = jump
    xh[3] = FIRST.rho * xr[4] + kjump
    xh[4] = kjump
    to_left.wait_send()


def bulk_kernel(
    gx, kx, kap, curv, gy, ky, yends, xh, tab, ends, dif_low, gx_out, gy_out, dif_out, gyf, dif, gh, sem
):
    planes, cells_x, cells_y = gx.shape
    top = cells_x - STRIP
    rest, high_rows = pl.ds(STRIP, top), pl.ds(top, STRIP)
    inner_rows, inner = pl.ds(STRIP, top - STRIP), slice(STRIP, top)
    copies = []

    def store(source, target):
        copy = pltpu.make_async_copy(source, target, sem.at[len(copies)])
        copy.start()
        copies.append(copy)

    store(gx.at[:, inner_rows, :], gx_out.at[:, inner_rows, :])
    columns = [twice(tab[n, 0:STRIP]) for n in (0, 1)] + [twice(tab[n, 0:8]) for n in (2, 3)]
    for pair in range(planes // 2):
        stacks = []
        for q in range(2):
            values = yends[2 * pair + q]
            high = values.astype(jnp.bfloat16).astype(jnp.float32)
            blank = jnp.zeros((FULL - 48, cells_x), jnp.float32)
            stacks.append(jnp.concatenate([high, values - high, high, blank], axis=0).T)
        turned = jnp.concatenate(stacks, axis=0).astype(jnp.bfloat16)
        reach = [matmul(turned, ends[n * FULL : (n + 1) * FULL, :]) for n in range(3)]
        for q in range(2):
            p = 2 * pair + q
            rows = slice(q * cells_x, (q + 1) * cells_x)
            grad = gy[p] + reach[0][rows]
            gyf[p] = grad
            part = kap[p] * (curv[p] + reach[1][rows]) + (ky[p] + reach[2][rows]) * grad
            dif_low[p] = part[0:STRIP]
            dif[p, inner, :] = part[inner] + kx[p, inner, :] * gx[p, inner, :]
            gh[p], dif[p, top:, :] = ends_applied(
                1,
                gx[p, top:, :],
                kx[p, top:, :],
                part[top:],
                kap[p, top:, :],
                columns,
                [xh[n, p : p + 1, :] for n in range(5)],
            )
        both = pl.ds(2 * pair, 2)
        store(gyf.at[both], gy_out.at[both])
        store(dif.at[both, rest, :], dif_out.at[both, rest, :])
        store(gh.at[both], gx_out.at[both, high_rows, :])
    for copy in copies:
        copy.wait()


def finish_kernel(gx_in, dif_in, gx, dif_low, kx, kap, edges, came, tab, gx_out, dif_out, gs, ds, xc, sem):
    planes = gx.shape[0]
    jump, kjump = edges[0] - came[0], edges[1] - came[1]
    xc[0] = FIRST.rho * came[2] + jump
    xc[1] = SECOND.rho * came[3] + jump
    xc[2] = jump
    xc[3] = FIRST.rho * came[4] + kjump
    xc[4] = kjump
    columns = [twice(tab[n, 0:STRIP]) for n in (0, 1)] + [twice(tab[n, 0:8]) for n in (2, 3)]
    low = pl.ds(0, STRIP)
    copies = []
    for p in range(planes):
        gs[p], ds[p] = ends_applied(
            0,
            gx[p, 0:STRIP, :],
            kx[p, 0:STRIP, :],
            dif_low[p],
            kap[p, 0:STRIP, :],
            columns,
            [xc[n, p : p + 1, :] for n in range(5)],
        )
        if p % 4 == 3:
            some = pl.ds(p - 3, 4)
            for source, target in ((gs, gx_out), (ds, dif_out)):
                copies.append(
                    pltpu.make_async_copy(
                        source.at[some], target.at[some, low, :], sem.at[len(copies)]
                    )
                )
                copies[-1].start()
    for copy in copies:
        copy.wait()


def local(counts, scalar, diffusivity):
    block = scalar.shape
    planes, cells_x, cells_y = block
    tables = (
        jnp.asarray(stacked(sum_columns(STRIP) + sum_columns(REACH))),
        jnp.asarray(np.concatenate([x_table(cells_x), y_table(cells_y)], axis=0)),
    )
    vmem, hbm = pl.BlockSpec(memory_space=pltpu.VMEM), pl.BlockSpec(memory_space=pltpu.HBM)
    field = jax.ShapeDtypeStruct(block, jnp.float32)
    field_buffer = pltpu.VMEM(block, jnp.float32)
    ends_shape, strip_shape = (5, planes, cells_y), (planes, STRIP, cells_y)
    strip_buffer = pltpu.VMEM(strip_shape, jnp.float32)
    y_shape = (2, planes, 8, cells_x)
    operands = [
        pltpu.with_memory_space_constraint(array, pltpu.HBM)
        for array in (scalar, diffusivity) + tables
    ]
    message = pl.pallas_call(
        sums_kernel,
        out_shape=jax.ShapeDtypeStruct(ends_shape, jnp.float32),
        in_specs=[hbm] * 3,
        out_specs=vmem,
        scratch_shapes=[
            strip_buffer,
            strip_buffer,
            pltpu.VMEM((2, 32, 128), jnp.float32),
            pltpu.SemaphoreType.DMA((3,)),
        ],
        compiler_params=pltpu.CompilerParams(vmem_limit_bytes=LIMIT),
        name="sums",
    )(*operands[:3])
    came = lax.ppermute(message, "gx", [(i, (i + 1) % counts[0]) for i in range(counts[0])])
    gx, kx, kap, curv, gy, ky, yends, xh, edges = pl.pallas_call(
        functools.partial(exchange_kernel, counts),
        out_shape=(field,) * 6
        + (
            jax.ShapeDtypeStruct((planes, 16, cells_x), jnp.float32),
            jax.ShapeDtypeStruct(ends_shape, jnp.float32),
            jax.ShapeDtypeStruct((4, planes, cells_y), jnp.float32),
        ),
        in_specs=[hbm] * 4,
        out_specs=(vmem,) * 9,
        scratch_shapes=[field_buffer]
        + [pltpu.VMEM(table.shape, table.dtype) for table in tables]
        + [pltpu.VMEM(ends_shape, jnp.float32)] * 2
        + [pltpu.VMEM(y_shape, jnp.float32)] * 2
        + [
            pltpu.SemaphoreType.DMA((6,)),
            pltpu.SemaphoreType.DMA((3,)),
            pltpu.SemaphoreType.DMA((3,)),
            pltpu.SemaphoreType.REGULAR,
            pltpu.SemaphoreType.REGULAR,
        ],
        compiler_params=pltpu.CompilerParams(
            collective_id=0, has_side_effects=True, vmem_limit_bytes=LIMIT
        ),
        cost_estimate=pl.CostEstimate(flops=2 * 10**9, bytes_accessed=8 * 2**20, transcendentals=0),
        name="exchange",
    )(*operands)
    dif_low, gx_out, gy_out, dif_out = pl.pallas_call(
        bulk_kernel,
        out_shape=(jax.ShapeDtypeStruct(strip_shape, jnp.float32),) + (field,) * 3,
        in_specs=[vmem] * 10,
        out_specs=(vmem,) + (hbm,) * 3,
        scratch_shapes=[
            field_buffer,
            field_buffer,
            strip_buffer,
            pltpu.SemaphoreType.DMA((1 + 3 * (planes // 2),)),
        ],
        compiler_params=pltpu.CompilerParams(vmem_limit_bytes=LIMIT),
        cost_estimate=pl.CostEstimate(flops=2 * 10**8, bytes_accessed=3 * 2**20, transcendentals=0),
        name="bulk",
    )(
        *(gx, kx, kap, curv, gy, ky, yends, xh),
        jnp.asarray(stacked(high_end_columns())),
        jnp.asarray(y_end_table(cells_y)),
    )
    gx_out, dif_out = pl.pallas_call(
        finish_kernel,
        out_shape=(field,) * 2,
        in_specs=[hbm] * 2 + [vmem] * 7,
        out_specs=(hbm,) * 2,
        scratch_shapes=[
            strip_buffer,
            strip_buffer,
            pltpu.VMEM(ends_shape, jnp.float32),
            pltpu.SemaphoreType.DMA((4,)),
        ],
        input_output_aliases={0: 0, 1: 1},
        compiler_params=pltpu.CompilerParams(vmem_limit_bytes=LIMIT),
        name="finish",
    )(
        *(gx_out, dif_out, gx, dif_low, kx, kap, edges, came),
        jnp.asarray(stacked(low_end_columns())),
    )
    return gx_out, gy_out, dif_out


def solution(mesh):
    placed = P(None, "gx", "gy")
    return jax.shard_map(
        functools.partial(local, (mesh.shape["gx"], mesh.shape["gy"])),
        mesh=mesh,
        in_specs=(placed, placed),
        out_specs=(placed,) * 3,
        check_vma=False,
    )
```

```python
import functools

import jax
import jax.numpy as jnp
import numpy as np
from jax import lax
from jax.experimental import pallas as pl
from jax.experimental.pallas import tpu as pltpu
from jax.sharding import PartitionSpec as P

FIRST_ALPHA = 1.0 / 3.0
FIRST_A = 14.0 / 9.0
FIRST_B = 1.0 / 9.0
SECOND_ALPHA = 2.0 / 11.0
SECOND_A = 12.0 / 11.0
SECOND_B = 3.0 / 11.0
MESH = pl.DeviceIdType.MESH
LIMIT = 28 * 1024 * 1024
STRIP = 24
REACH = 32
FULL = 128
RUN = 8


class Line:
    def __init__(self, alpha, taps):
        root = np.sqrt(1.0 - 4.0 * alpha * alpha)
        self.rho = (root - 1.0) / (2.0 * alpha)
        self.root, self.taps = root, taps
        self.ahead = sum(c * self.rho**m for m, c in taps.items()) / root
        self.behind = sum(c * self.rho**-m for m, c in taps.items()) / root

    def weight(self, n):
        n = np.asarray(n)
        return sum(c * self.rho ** np.abs(n + m) for m, c in self.taps.items()) / self.root

    def local(self, cells):
        i = np.arange(cells)
        table = self.weight(i[:, None] - i[None, :])
        table[:, cells - 1] = 0.0
        return table

    def low_sum(self, reach):
        power = self.rho ** np.arange(reach - 1)
        weights = np.zeros(reach)
        weights[1:] += power
        weights[:-1] -= power
        return weights


FIRST = Line(
    FIRST_ALPHA,
    {
        1: 0.25 * FIRST_B,
        0: 0.5 * FIRST_A + 0.25 * FIRST_B,
        -1: 0.5 * FIRST_A + 0.25 * FIRST_B,
        -2: 0.25 * FIRST_B,
    },
)
SECOND = Line(
    SECOND_ALPHA,
    {
        1: 0.25 * SECOND_B,
        0: SECOND_A + 0.25 * SECOND_B,
        -1: -SECOND_A - 0.25 * SECOND_B,
        -2: -0.25 * SECOND_B,
    },
)


def halves(table):
    high = np.asarray(table, np.float32).astype(jnp.bfloat16)
    low = (table - high.astype(np.float64)).astype(np.float32).astype(jnp.bfloat16)
    return high, low


def stacked(columns):
    table = np.zeros((len(columns), 32, 128), np.float32)
    for place, column in enumerate(columns):
        table[place, : len(column)] = column[:, None]
    return table


def sum_columns(reach):
    low = [FIRST.low_sum(reach), SECOND.low_sum(reach)]
    return [-row[::-1] for row in low] + low


def high_end_columns():
    r = np.arange(STRIP)[::-1]
    columns = [(line.behind * line.rho**r) for line in (FIRST, SECOND)]
    for line in (FIRST, SECOND):
        column = np.zeros(8)
        column[7] = line.weight(0) - line.behind
        columns.append(column)
    return columns


def low_end_columns():
    r = np.arange(STRIP)
    columns = [(line.ahead * line.rho ** (r + 1)) for line in (FIRST, SECOND)]
    for line in (FIRST, SECOND):
        column = np.zeros(8)
        column[0] = line.weight(1) - line.ahead * line.rho
        columns.append(column)
    return columns


def x_table(cells):
    rows = []
    for line in (FIRST, SECOND):
        for half in halves(line.local(cells)):
            rows.append(np.concatenate([half, half], axis=1))
    return np.concatenate(rows, axis=0)


def y_table(cells):
    rows = []
    for line in (FIRST, SECOND):
        high, low = halves(line.local(cells).T)
        rows += [high, high, low]
    return np.concatenate(rows, axis=0)


def y_end_table(cells):
    i = np.arange(cells)
    blocks = []
    for line, sum_row, edge_row in ((FIRST, 0, 2), (SECOND, 1, 2), (FIRST, 3, 4)):
        table = np.zeros((16, cells))
        table[sum_row] = line.ahead * line.rho ** (i + 2)
        table[edge_row] = line.weight(i + 1)
        table[8 + sum_row] = line.behind * line.rho ** (cells - i)
        table[8 + edge_row] = line.weight(i - cells + 1)
        high, low = halves(table)
        blank = np.zeros((FULL - 48, cells), high.dtype)
        blocks += [high, high, low, blank]
    return np.concatenate(blocks, axis=0)


def split(values):
    high = values.astype(jnp.bfloat16)
    low = (values - high.astype(jnp.float32)).astype(jnp.bfloat16)
    return high, low


def matmul(left, right):
    return jnp.dot(left, right, preferred_element_type=jnp.float32)


def twice(tile):
    return jnp.concatenate([tile, tile], axis=1)


def ends_applied(side, grad, kgrad, part, kappa, columns, values):
    decay, decay_second, end, end_second = columns
    first, second, jump, kfirst, kjump = values
    grads, parts = [], []
    for tile in range(STRIP // 8):
        r = slice(8 * tile, 8 * tile + 8)
        g = grad[r] + decay[r] * first
        k = kgrad[r] + decay[r] * kfirst
        distance = tile if side == 0 else STRIP // 8 - 1 - tile
        d = part[r]
        if distance < 2:
            bend = decay_second[r] * second
            if distance == 0:
                g = g + end * jump
                k = k + end * kjump
                bend = bend + end_second * jump
            d = d + kappa[r] * bend
        grads.append(g)
        parts.append(d + k * g)
    return jnp.concatenate(grads, axis=0), jnp.concatenate(parts, axis=0)


def sums_kernel(last, f_hbm, k_hbm, tab_hbm, out, fst, kst, tab, sem):
    planes, cells_x = f_hbm.shape[0], f_hbm.shape[1]
    rows = pl.ds(cells_x - STRIP, STRIP)
    copies = [
        pltpu.make_async_copy(f_hbm.at[:, rows, :], fst, sem.at[0]),
        pltpu.make_async_copy(k_hbm.at[:, rows, :], kst, sem.at[1]),
        pltpu.make_async_copy(tab_hbm.at[0:2], tab, sem.at[2]),
    ]

    @pl.when(lax.axis_index("gx") == last)
    def work():
        for copy in copies:
            copy.start()
        for copy in copies:
            copy.wait()
        with_first, with_second = twice(tab[0, 0:STRIP]), twice(tab[1, 0:STRIP])
        for p in range(planes):
            out[0, p : p + 1, :] = fst[p, STRIP - 1 : STRIP, :]
            out[1, p : p + 1, :] = kst[p, STRIP - 1 : STRIP, :]
            out[2, p : p + 1, :] = jnp.sum(fst[p] * with_first, axis=0, keepdims=True)
            out[3, p : p + 1, :] = jnp.sum(fst[p] * with_second, axis=0, keepdims=True)
            out[4, p : p + 1, :] = jnp.sum(kst[p] * with_first, axis=0, keepdims=True)


def exchange_kernel(
    counts,
    f_hbm,
    k_hbm,
    tab_hbm,
    mats_hbm,
    gx,
    gy,
    dif,
    kx,
    kap,
    xc,
    edges,
    fld,
    tab,
    mats,
    curv,
    ky,
    xs,
    xr,
    ys,
    yr,
    xh,
    in_sem,
    send_sem,
    recv_sem,
    left_ready,
    above_ready,
):
    planes, cells_x, cells_y = fld.shape
    top = cells_x - STRIP
    loads = []

    def load(source, target):
        copy = pltpu.make_async_copy(source, target, in_sem.at[len(loads)])
        copy.start()
        loads.append(copy)
        return copy

    def load_rows(rows):
        return [
            load(f_hbm.at[:, rows, :], fld.at[:, rows, :]),
            load(k_hbm.at[:, rows, :], kap.at[:, rows, :]),
        ]

    high_loads = load_rows(pl.ds(top, STRIP)) + [load(tab_hbm, tab)]
    low_loads = load_rows(pl.ds(0, STRIP))
    middle_loads = load_rows(pl.ds(STRIP, top - STRIP))
    table_load = load(mats_hbm, mats)

    ix, iy = lax.axis_index("gx"), lax.axis_index("gy")
    nx, ny = counts
    left = (jnp.where(ix == 0, nx - 1, ix - 1), iy)
    right = (jnp.where(ix == nx - 1, 0, ix + 1), iy)
    below = (ix, jnp.where(iy == 0, ny - 1, iy - 1))
    above = (ix, jnp.where(iy == ny - 1, 0, iy + 1))
    barrier = pltpu.get_barrier_semaphore()
    for neighbour in (left, above):
        pl.semaphore_signal(barrier, inc=1, device_id=neighbour, device_id_type=MESH)

    def message(place, source, target, device):
        return pltpu.make_async_remote_copy(
            src_ref=source,
            dst_ref=target,
            send_sem=send_sem.at[place],
            recv_sem=recv_sem.at[place],
            device_id=device,
            device_id_type=MESH,
        )

    def send(*what):
        copy = message(*what)
        copy.start()
        return copy

    def take_x_edge(side, edge):
        for p in range(planes):
            xs[side, 0, p : p + 1, :] = fld[p, edge : edge + 1, :]
            xs[side, 1, p : p + 1, :] = kap[p, edge : edge + 1, :]

    def sum_x_edge(side, start, place):
        with_first, with_second = twice(tab[place, 0:STRIP]), twice(tab[place + 1, 0:STRIP])
        for p in range(planes):
            rows = fld[p, start : start + STRIP, :]
            krows = kap[p, start : start + STRIP, :]
            xs[side, 2, p : p + 1, :] = jnp.sum(rows * with_first, axis=0, keepdims=True)
            xs[side, 3, p : p + 1, :] = jnp.sum(rows * with_second, axis=0, keepdims=True)
            xs[side, 4, p : p + 1, :] = jnp.sum(krows * with_first, axis=0, keepdims=True)

    for copy in high_loads:
        copy.wait()
    take_x_edge(1, cells_x - 1)
    pl.semaphore_wait(barrier, 2)
    sends_right, hears_left = ix != nx - 1, ix != 0
    to_right = [
        message(1, xs.at[1, 0:2], xr.at[0, 0:2], right),
        message(2, xs.at[1, 2:5], xr.at[0, 2:5], right),
    ]
    pl.when(sends_right)(to_right[0].start)
    sum_x_edge(1, top, 0)
    pl.when(sends_right)(to_right[1].start)
    pl.semaphore_signal(left_ready, inc=1, device_id=right, device_id_type=MESH)
    pl.semaphore_signal(above_ready, inc=1, device_id=below, device_id_type=MESH)
    for copy in low_loads:
        copy.wait()
    take_x_edge(0, 0)
    sum_x_edge(0, 0, 2)

    for copy in middle_loads:
        copy.wait()
    ys[:, :, 5:8, :] = jnp.zeros((2, planes, 3, 128), jnp.float32)
    lane = lax.broadcasted_iota(jnp.int32, (cells_x, 128), 1)
    for p in range(planes):
        f_low, f_high = fld[p, :, 0:128], fld[p, :, cells_y - 128 : cells_y]
        k_low, k_high = kap[p, :, 0:128], kap[p, :, cells_y - 128 : cells_y]
        packed = jnp.where(
            lane < REACH,
            f_low,
            jnp.where(
                lane < 2 * REACH,
                pltpu.roll(k_low, REACH, 1),
                jnp.where(lane < 3 * REACH, pltpu.roll(k_high, 128 - REACH, 1), f_high),
            ),
        )
        turned = packed.T
        for side, place, f_part, k_part, f_edge, k_edge in (
            (0, 6, turned[0:32], turned[32:64], turned[0:1], turned[32:33]),
            (1, 4, turned[96:128], turned[64:96], turned[127:128], turned[95:96]),
        ):
            with_first, with_second = tab[place], tab[place + 1]
            ys[side, p, 0:1, :] = jnp.sum(f_part * with_first, axis=0, keepdims=True)
            ys[side, p, 1:2, :] = jnp.sum(f_part * with_second, axis=0, keepdims=True)
            ys[side, p, 2:3, :] = f_edge
            ys[side, p, 3:4, :] = jnp.sum(k_part * with_first, axis=0, keepdims=True)
            ys[side, p, 4:5, :] = k_edge
    to_below = send(3, ys.at[0], yr.at[1], below)
    pl.semaphore_wait(above_ready, 1)
    to_above = send(4, ys.at[1], yr.at[0], above)

    to_left = message(0, xs.at[0], xr.at[1], left)
    run_begins = lax.rem(ix, RUN) == 0

    def send_left():
        pl.semaphore_wait(left_ready, 1)
        to_left.start()

    pl.when(jnp.logical_not(run_begins))(send_left)

    table_load.wait()
    x_rows = 4 * cells_x
    y_first = slice(x_rows, x_rows + 3 * cells_y)
    y_second = slice(x_rows + 3 * cells_y, x_rows + 6 * cells_y)
    end_rows = x_rows + 6 * cells_y

    def local_pair(pair, carry):
        tall, ktall = [], []
        for q in range(2):
            p = 2 * pair + q
            f, k = fld[p], kap[p]
            high, low = split(pltpu.roll(f, cells_x - 1, 0) - f)
            along = matmul(mats[0:x_rows, :], jnp.concatenate([high, low], axis=0))
            gx[p] = along[0:cells_x] + along[cells_x : 2 * cells_x]
            curv[p] = along[2 * cells_x : 3 * cells_x] + along[3 * cells_x : 4 * cells_x]
            high, low = split(pltpu.roll(k, cells_x - 1, 0) - k)
            along = matmul(mats[0 : 2 * cells_x, :], jnp.concatenate([high, low], axis=0))
            kx[p] = along[0:cells_x] + along[cells_x : 2 * cells_x]
            high, low = split(pltpu.roll(f, cells_y - 1, 1) - f)
            tall.append(jnp.concatenate([high, low, high], axis=1))
            high, low = split(pltpu.roll(k, cells_y - 1, 1) - k)
            ktall.append(jnp.concatenate([high, low, high], axis=1))
        across = matmul(jnp.concatenate(tall + ktall, axis=0), mats[y_first, :])
        bend = matmul(jnp.concatenate(tall, axis=0), mats[y_second, :])
        for q in range(2):
            p = 2 * pair + q
            gy[p] = across[q * cells_x : (q + 1) * cells_x]
            ky[p] = across[(q + 2) * cells_x : (q + 3) * cells_x]
            curv[p] = curv[p] + bend[q * cells_x : (q + 1) * cells_x]
        return carry

    lax.fori_loop(0, planes // 2, local_pair, 0)

    to_below.wait_recv()
    to_above.wait_recv()
    row = lax.broadcasted_iota(jnp.int32, (8, 128), 0)
    is_edge = (row == 2) | (row == 4)

    def finish_pair(pair, carry):
        stacks = []
        for q in range(2):
            p = 2 * pair + q
            from_below, from_above = yr[0, p], yr[1, p]
            from_below = jnp.where(is_edge, ys[0, p] - from_below, from_below)
            from_above = jnp.where(is_edge, from_above - ys[1, p], from_above)
            ends = jnp.concatenate([from_below, from_above], axis=0)
            high = ends.astype(jnp.bfloat16).astype(jnp.float32)
            blank = jnp.zeros((FULL - 48, cells_x), jnp.float32)
            stacks.append(jnp.concatenate([high, ends - high, high, blank], axis=0).T)
        turned = jnp.concatenate(stacks, axis=0).astype(jnp.bfloat16)
        reach = [
            matmul(turned, mats[end_rows + n * FULL : end_rows + (n + 1) * FULL, :]) for n in range(3)
        ]
        for q in range(2):
            p = 2 * pair + q
            rows = slice(q * cells_x, (q + 1) * cells_x)
            grad = gy[p] + reach[0][rows]
            gy[p] = grad
            part = kap[p] * (curv[p] + reach[1][rows]) + (ky[p] + reach[2][rows]) * grad
            inner = slice(STRIP, top)
            dif[p, 0:STRIP, :] = part[0:STRIP]
            dif[p, inner, :] = part[inner] + kx[p, inner, :] * gx[p, inner, :]
            dif[p, top:, :] = part[top:]
        return carry

    lax.fori_loop(0, planes // 2, finish_pair, 0)
    pl.when(run_begins)(send_left)

    def combine(side, out):
        sign = 1.0 if side == 0 else -1.0
        jump = sign * (xs[side, 0] - xr[side, 0])
        kjump = sign * (xs[side, 1] - xr[side, 1])
        out[0] = FIRST.rho * xr[side, 2] + jump
        out[1] = SECOND.rho * xr[side, 3] + jump
        out[2] = jump
        out[3] = FIRST.rho * xr[side, 4] + kjump
        out[4] = kjump

    to_left.wait_recv()
    combine(1, xh)
    columns = [twice(tab[n, 0:STRIP]) for n in (8, 9)] + [twice(tab[n, 0:8]) for n in (10, 11)]
    for p in range(planes):
        gx[p, top:, :], dif[p, top:, :] = ends_applied(
            1,
            gx[p, top:, :],
            kx[p, top:, :],
            dif[p, top:, :],
            kap[p, top:, :],
            columns,
            [xh[n, p : p + 1, :] for n in range(5)],
        )
    edges[...] = xs[0, 0:2]
    for copy in (to_left, to_below, to_above):
        copy.wait_send()

    @pl.when(sends_right)
    def sent():
        for copy in to_right:
            copy.wait_send()

    @pl.when(hears_left)
    def hear():
        for copy in to_right:
            copy.wait_recv()
        combine(0, xc)


def low_rows(gx, dif, kx, kap, values, tab, gs, ds):
    columns = [twice(tab[n, 0:STRIP]) for n in (0, 1)] + [twice(tab[n, 0:8]) for n in (2, 3)]
    for p in range(gx.shape[0]):
        gs[p], ds[p] = ends_applied(
            0,
            gx[p, 0:STRIP, :],
            kx[p, 0:STRIP, :],
            dif[p, 0:STRIP, :],
            kap[p, 0:STRIP, :],
            columns,
            [values[n, p : p + 1, :] for n in range(5)],
        )


def low_copies(gs, ds, gx_out, dif_out, sem):
    low = pl.ds(0, STRIP)
    return [
        pltpu.make_async_copy(gs, gx_out.at[:, low, :], sem.at[0]),
        pltpu.make_async_copy(ds, dif_out.at[:, low, :], sem.at[1]),
    ]


def bulk_kernel(gx, gy, dif, kx, kap, xc, tab, gx_out, gy_out, dif_out, gs, ds, sem, low_sem):
    rest = pl.ds(STRIP, gx.shape[1] - STRIP)
    copies = [
        pltpu.make_async_copy(gy, gy_out, sem.at[0]),
        pltpu.make_async_copy(gx.at[:, rest, :], gx_out.at[:, rest, :], sem.at[1]),
        pltpu.make_async_copy(dif.at[:, rest, :], dif_out.at[:, rest, :], sem.at[2]),
    ]
    for copy in copies:
        copy.start()

    @pl.when(lax.axis_index("gx") != 0)
    def low():
        low_rows(gx, dif, kx, kap, xc, tab, gs, ds)
        for copy in low_copies(gs, ds, gx_out, dif_out, low_sem):
            copy.start()
        for copy in low_copies(gs, ds, gx_out, dif_out, low_sem):
            copy.wait()

    for copy in copies:
        copy.wait()


def finish_kernel(
    gx_in, dif_in, gx, dif, kx, kap, edges, came, tab, gx_out, dif_out, gs, ds, values, low_sem
):
    @pl.when(lax.axis_index("gx") == 0)
    def low():
        jump, kjump = edges[0] - came[0], edges[1] - came[1]
        values[0] = FIRST.rho * came[2] + jump
        values[1] = SECOND.rho * came[3] + jump
        values[2] = jump
        values[3] = FIRST.rho * came[4] + kjump
        values[4] = kjump
        low_rows(gx, dif, kx, kap, values, tab, gs, ds)
        for copy in low_copies(gs, ds, gx_out, dif_out, low_sem):
            copy.start()
        for copy in low_copies(gs, ds, gx_out, dif_out, low_sem):
            copy.wait()


def local(counts, scalar, diffusivity):
    block = scalar.shape
    planes, cells_x, cells_y = block
    columns = sum_columns(STRIP) + sum_columns(REACH) + high_end_columns()
    tables = (
        jnp.asarray(stacked(columns)),
        jnp.asarray(
            np.concatenate([x_table(cells_x), y_table(cells_y), y_end_table(cells_y)], axis=0)
        ),
    )
    vmem, hbm = pl.BlockSpec(memory_space=pltpu.VMEM), pl.BlockSpec(memory_space=pltpu.HBM)
    field = jax.ShapeDtypeStruct(block, jnp.float32)
    field_buffer = pltpu.VMEM(block, jnp.float32)
    ends_shape = (5, planes, cells_y)
    operands = [
        pltpu.with_memory_space_constraint(array, pltpu.HBM)
        for array in (scalar, diffusivity) + tables
    ]
    strip_shape = (planes, STRIP, cells_y)
    strip_buffer = pltpu.VMEM(strip_shape, jnp.float32)
    last = counts[0] - 1
    message = pl.pallas_call(
        functools.partial(sums_kernel, last),
        out_shape=jax.ShapeDtypeStruct(ends_shape, jnp.float32),
        in_specs=[hbm] * 3,
        out_specs=vmem,
        scratch_shapes=[
            strip_buffer,
            strip_buffer,
            pltpu.VMEM((2, 32, 128), jnp.float32),
            pltpu.SemaphoreType.DMA((3,)),
        ],
        compiler_params=pltpu.CompilerParams(vmem_limit_bytes=LIMIT),
        name="sums",
    )(*operands[:3])
    came = lax.ppermute(message, "gx", [(last, 0)])
    parts = pl.pallas_call(
        functools.partial(exchange_kernel, counts),
        out_shape=(field,) * 5 + (jax.ShapeDtypeStruct(ends_shape, jnp.float32), jax.ShapeDtypeStruct((2,) + ends_shape[1:], jnp.float32)),
        in_specs=[hbm] * 4,
        out_specs=(vmem,) * 7,
        scratch_shapes=[field_buffer]
        + [pltpu.VMEM(table.shape, table.dtype) for table in tables]
        + [field_buffer, field_buffer]
        + [pltpu.VMEM((2,) + ends_shape, jnp.float32)] * 2
        + [pltpu.VMEM((2, planes, 8, cells_x), jnp.float32)] * 2
        + [
            pltpu.VMEM(ends_shape, jnp.float32),
            pltpu.SemaphoreType.DMA((8,)),
            pltpu.SemaphoreType.DMA((5,)),
            pltpu.SemaphoreType.DMA((5,)),
            pltpu.SemaphoreType.REGULAR,
            pltpu.SemaphoreType.REGULAR,
        ],
        compiler_params=pltpu.CompilerParams(
            collective_id=0, has_side_effects=True, vmem_limit_bytes=LIMIT
        ),
        cost_estimate=pl.CostEstimate(flops=2 * 10**9, bytes_accessed=8 * 2**20, transcendentals=0),
        name="exchange",
    )(*operands)
    grad_x, grad_y, dif, kx, kap, xc, edges = parts
    tab = jnp.asarray(stacked(low_end_columns()))
    low_scratch = [strip_buffer, strip_buffer]
    gx_out, gy_out, dif_out = pl.pallas_call(
        bulk_kernel,
        out_shape=(field,) * 3,
        in_specs=[vmem] * 7,
        out_specs=(hbm,) * 3,
        scratch_shapes=low_scratch
        + [pltpu.SemaphoreType.DMA((3,)), pltpu.SemaphoreType.DMA((2,))],
        compiler_params=pltpu.CompilerParams(vmem_limit_bytes=LIMIT),
        cost_estimate=pl.CostEstimate(flops=0, bytes_accessed=3 * 2**20, transcendentals=0),
        name="bulk",
    )(grad_x, grad_y, dif, kx, kap, xc, tab)
    gx_out, dif_out = pl.pallas_call(
        finish_kernel,
        out_shape=(field,) * 2,
        in_specs=[hbm] * 2 + [vmem] * 7,
        out_specs=(hbm,) * 2,
        scratch_shapes=low_scratch
        + [pltpu.VMEM(ends_shape, jnp.float32), pltpu.SemaphoreType.DMA((2,))],
        input_output_aliases={0: 0, 1: 1},
        compiler_params=pltpu.CompilerParams(vmem_limit_bytes=LIMIT),
        name="finish",
    )(gx_out, dif_out, grad_x, dif, kx, kap, edges, came, tab)
    return gx_out, gy_out, dif_out


def solution(mesh):
    placed = P(None, "gx", "gy")
    return jax.shard_map(
        functools.partial(local, (mesh.shape["gx"], mesh.shape["gy"])),
        mesh=mesh,
        in_specs=(placed, placed),
        out_specs=(placed,) * 3,
        check_vma=False,
    )
```

```python
import functools

import jax
import jax.numpy as jnp
import numpy as np
from jax import lax
from jax.experimental import pallas as pl
from jax.experimental.pallas import tpu as pltpu
from jax.sharding import PartitionSpec as P

FIRST_ALPHA = 1.0 / 3.0
FIRST_A = 14.0 / 9.0
FIRST_B = 1.0 / 9.0
SECOND_ALPHA = 2.0 / 11.0
SECOND_A = 12.0 / 11.0
SECOND_B = 3.0 / 11.0
MESH = pl.DeviceIdType.MESH
LIMIT = 28 * 1024 * 1024
STRIP = 24
SHORT = 16
REACH = 32
FULL = 128
RUN = 8


class Line:
    def __init__(self, alpha, taps):
        root = np.sqrt(1.0 - 4.0 * alpha * alpha)
        self.rho = (root - 1.0) / (2.0 * alpha)
        self.root, self.taps = root, taps
        self.ahead = sum(c * self.rho**m for m, c in taps.items()) / root
        self.behind = sum(c * self.rho**-m for m, c in taps.items()) / root

    def weight(self, n):
        n = np.asarray(n)
        return sum(c * self.rho ** np.abs(n + m) for m, c in self.taps.items()) / self.root

    def local(self, cells):
        i = np.arange(cells)
        table = self.weight(i[:, None] - i[None, :])
        table[:, cells - 1] = 0.0
        return table

    def low_sum(self, reach):
        power = self.rho ** np.arange(reach - 1)
        weights = np.zeros(reach)
        weights[1:] += power
        weights[:-1] -= power
        return weights


FIRST = Line(
    FIRST_ALPHA,
    {
        1: 0.25 * FIRST_B,
        0: 0.5 * FIRST_A + 0.25 * FIRST_B,
        -1: 0.5 * FIRST_A + 0.25 * FIRST_B,
        -2: 0.25 * FIRST_B,
    },
)
SECOND = Line(
    SECOND_ALPHA,
    {
        1: 0.25 * SECOND_B,
        0: SECOND_A + 0.25 * SECOND_B,
        -1: -SECOND_A - 0.25 * SECOND_B,
        -2: -0.25 * SECOND_B,
    },
)


def halves(table):
    high = np.asarray(table, np.float32).astype(jnp.bfloat16)
    low = (table - high.astype(np.float64)).astype(np.float32).astype(jnp.bfloat16)
    return high, low


def stacked(columns):
    table = np.zeros((len(columns), 32, 128), np.float32)
    for place, column in enumerate(columns):
        table[place, : len(column)] = column[:, None]
    return table


def sum_columns(reach, short):
    low = [FIRST.low_sum(reach), SECOND.low_sum(short)]
    return [-row[::-1] for row in low] + low


def high_end_columns():
    r = np.arange(STRIP)[::-1]
    columns = [(line.behind * line.rho**r) for line in (FIRST, SECOND)]
    for line in (FIRST, SECOND):
        column = np.zeros(8)
        column[7] = line.weight(0) - line.behind
        columns.append(column)
    return columns


def low_end_columns():
    r = np.arange(STRIP)
    columns = [(line.ahead * line.rho ** (r + 1)) for line in (FIRST, SECOND)]
    for line in (FIRST, SECOND):
        column = np.zeros(8)
        column[0] = line.weight(1) - line.ahead * line.rho
        columns.append(column)
    return columns


def x_table(cells):
    rows = []
    for line in (FIRST, SECOND):
        for half in halves(line.local(cells)):
            rows.append(np.concatenate([half, half], axis=1))
    return np.concatenate(rows, axis=0)


def y_table(cells):
    rows = []
    for line in (FIRST, SECOND):
        high, low = halves(line.local(cells).T)
        rows += [high, high, low]
    return np.concatenate(rows, axis=0)


def y_end_table(cells):
    i = np.arange(cells)
    blocks = []
    for line, sum_row, edge_row in ((FIRST, 0, 2), (SECOND, 1, 2), (FIRST, 3, 4)):
        table = np.zeros((16, cells))
        table[sum_row] = line.ahead * line.rho ** (i + 2)
        table[edge_row] = line.weight(i + 1)
        table[8 + sum_row] = line.behind * line.rho ** (cells - i)
        table[8 + edge_row] = line.weight(i - cells + 1)
        high, low = halves(table)
        blank = np.zeros((FULL - 48, cells), high.dtype)
        blocks += [high, high, low, blank]
    return np.concatenate(blocks, axis=0)


def split(values):
    high = values.astype(jnp.bfloat16)
    low = (values - high.astype(jnp.float32)).astype(jnp.bfloat16)
    return high, low


def matmul(left, right):
    return jnp.dot(left, right, preferred_element_type=jnp.float32)


def twice(tile):
    return jnp.concatenate([tile, tile], axis=1)


def ends_applied(side, grad, kgrad, part, kappa, columns, values):
    decay, decay_second, end, end_second = columns
    first, second, jump, kfirst, kjump = values
    grads, parts = [], []
    for tile in range(STRIP // 8):
        r = slice(8 * tile, 8 * tile + 8)
        g = grad[r] + decay[r] * first
        k = kgrad[r] + decay[r] * kfirst
        distance = tile if side == 0 else STRIP // 8 - 1 - tile
        d = part[r]
        if distance < 2:
            bend = decay_second[r] * second
            if distance == 0:
                g = g + end * jump
                k = k + end * kjump
                bend = bend + end_second * jump
            d = d + kappa[r] * bend
        grads.append(g)
        parts.append(d + k * g)
    return jnp.concatenate(grads, axis=0), jnp.concatenate(parts, axis=0)


def exchange_kernel(
    counts,
    f_hbm,
    k_hbm,
    tab_hbm,
    mats_hbm,
    gx,
    gy,
    dif,
    kx,
    kap,
    xc,
    fld,
    tab,
    mats,
    curv,
    ky,
    xs,
    xr,
    ys,
    yr,
    xh,
    in_sem,
    send_sem,
    recv_sem,
    left_ready,
    above_ready,
):
    planes, cells_x, cells_y = fld.shape
    top = cells_x - STRIP
    loads = []

    def load(source, target):
        copy = pltpu.make_async_copy(source, target, in_sem.at[len(loads)])
        copy.start()
        loads.append(copy)
        return copy

    def load_rows(rows):
        return [
            load(f_hbm.at[:, rows, :], fld.at[:, rows, :]),
            load(k_hbm.at[:, rows, :], kap.at[:, rows, :]),
        ]

    top_rows, other_rows = pl.ds(top, STRIP), pl.ds(0, top)
    weights_load = load(tab_hbm.at[0:2], tab.at[0:2])
    f_high_load, k_high_load = load_rows(top_rows)
    other_loads = [load(tab_hbm.at[2:], tab.at[2:])] + load_rows(other_rows)
    table_load = load(mats_hbm, mats)

    ix, iy = lax.axis_index("gx"), lax.axis_index("gy")
    nx, ny = counts
    left = (jnp.where(ix == 0, nx - 1, ix - 1), iy)
    right = (jnp.where(ix == nx - 1, 0, ix + 1), iy)
    below = (ix, jnp.where(iy == 0, ny - 1, iy - 1))
    above = (ix, jnp.where(iy == ny - 1, 0, iy + 1))
    barrier = pltpu.get_barrier_semaphore()
    for neighbour in (left, above):
        pl.semaphore_signal(barrier, inc=1, device_id=neighbour, device_id_type=MESH)

    def tell(semaphore, neighbour):
        pl.semaphore_signal(semaphore, inc=1, device_id=neighbour, device_id_type=MESH)

    def message(place, source, target, device):
        return pltpu.make_async_remote_copy(
            src_ref=source,
            dst_ref=target,
            send_sem=send_sem.at[place],
            recv_sem=recv_sem.at[place],
            device_id=device,
            device_id_type=MESH,
        )

    def send(*what):
        copy = message(*what)
        copy.start()
        return copy

    def f_sums(side, start, place):
        with_first, with_second = twice(tab[place, 0:STRIP]), twice(tab[place + 1, 0:SHORT])
        near = start if side == 0 else start + STRIP - SHORT
        for p in range(planes):
            rows = fld[p, start : start + STRIP, :]
            few = fld[p, near : near + SHORT, :]
            xs[side, 2, p : p + 1, :] = jnp.sum(rows * with_first, axis=0, keepdims=True)
            xs[side, 3, p : p + 1, :] = jnp.sum(few * with_second, axis=0, keepdims=True)

    def k_sums(side, start, place):
        with_first = twice(tab[place, 0:STRIP])
        for p in range(planes):
            rows = kap[p, start : start + STRIP, :]
            xs[side, 4, p : p + 1, :] = jnp.sum(rows * with_first, axis=0, keepdims=True)

    def take_edge(side, place, field, edge):
        for p in range(planes):
            xs[side, place, p : p + 1, :] = field[p, edge : edge + 1, :]

    f_high_load.wait()
    take_edge(1, 0, fld, cells_x - 1)
    pl.semaphore_wait(barrier, 2)
    send(1, xs.at[1, 0:1], xr.at[0, 0:1], right)
    weights_load.wait()
    f_sums(1, top, 0)
    k_high_load.wait()
    take_edge(1, 1, kap, cells_x - 1)
    send(1, xs.at[1, 1:4], xr.at[0, 1:4], right)
    k_sums(1, top, 0)
    send(1, xs.at[1, 4:5], xr.at[0, 4:5], right)
    to_right = message(1, xs.at[1], xr.at[0], right)
    tell(left_ready, right)
    tell(above_ready, below)
    for copy in other_loads:
        copy.wait()
    take_edge(0, 0, fld, 0)
    take_edge(0, 1, kap, 0)
    f_sums(0, 0, 2)
    k_sums(0, 0, 2)

    ys[:, :, 5:8, :] = jnp.zeros((2, planes, 3, 128), jnp.float32)
    lane = lax.broadcasted_iota(jnp.int32, (cells_x, 128), 1)
    for p in range(planes):
        f_low, f_high = fld[p, :, 0:128], fld[p, :, cells_y - 128 : cells_y]
        k_low, k_high = kap[p, :, 0:128], kap[p, :, cells_y - 128 : cells_y]
        packed = jnp.where(
            lane < REACH,
            f_low,
            jnp.where(
                lane < 2 * REACH,
                pltpu.roll(k_low, REACH, 1),
                jnp.where(lane < 3 * REACH, pltpu.roll(k_high, 128 - REACH, 1), f_high),
            ),
        )
        turned = packed.T
        for side, place, f_part, k_part, f_edge, k_edge in (
            (0, 6, turned[0:32], turned[32:64], turned[0:1], turned[32:33]),
            (1, 4, turned[96:128], turned[64:96], turned[127:128], turned[95:96]),
        ):
            with_first, with_second = tab[place], tab[place + 1]
            ys[side, p, 0:1, :] = jnp.sum(f_part * with_first, axis=0, keepdims=True)
            ys[side, p, 1:2, :] = jnp.sum(f_part * with_second, axis=0, keepdims=True)
            ys[side, p, 2:3, :] = f_edge
            ys[side, p, 3:4, :] = jnp.sum(k_part * with_first, axis=0, keepdims=True)
            ys[side, p, 4:5, :] = k_edge
    to_below = send(2, ys.at[0], yr.at[1], below)
    pl.semaphore_wait(above_ready, 1)
    to_above = send(3, ys.at[1], yr.at[0], above)

    to_left = message(0, xs.at[0], xr.at[1], left)
    run_begins = lax.rem(ix, RUN) == 0

    def send_left():
        pl.semaphore_wait(left_ready, 1)
        to_left.start()

    pl.when(jnp.logical_not(run_begins))(send_left)

    table_load.wait()
    x_rows = 4 * cells_x
    y_first = slice(x_rows, x_rows + 3 * cells_y)
    y_second = slice(x_rows + 3 * cells_y, x_rows + 6 * cells_y)
    end_rows = x_rows + 6 * cells_y

    def local_pair(pair, carry):
        tall, ktall = [], []
        for q in range(2):
            p = 2 * pair + q
            f, k = fld[p], kap[p]
            high, low = split(pltpu.roll(f, cells_x - 1, 0) - f)
            along = matmul(mats[0:x_rows, :], jnp.concatenate([high, low], axis=0))
            gx[p] = along[0:cells_x] + along[cells_x : 2 * cells_x]
            curv[p] = along[2 * cells_x : 3 * cells_x] + along[3 * cells_x : 4 * cells_x]
            high, low = split(pltpu.roll(k, cells_x - 1, 0) - k)
            along = matmul(mats[0 : 2 * cells_x, :], jnp.concatenate([high, low], axis=0))
            kx[p] = along[0:cells_x] + along[cells_x : 2 * cells_x]
            high, low = split(pltpu.roll(f, cells_y - 1, 1) - f)
            tall.append(jnp.concatenate([high, low, high], axis=1))
            high, low = split(pltpu.roll(k, cells_y - 1, 1) - k)
            ktall.append(jnp.concatenate([high, low, high], axis=1))
        across = matmul(jnp.concatenate(tall + ktall, axis=0), mats[y_first, :])
        bend = matmul(jnp.concatenate(tall, axis=0), mats[y_second, :])
        for q in range(2):
            p = 2 * pair + q
            gy[p] = across[q * cells_x : (q + 1) * cells_x]
            ky[p] = across[(q + 2) * cells_x : (q + 3) * cells_x]
            curv[p] = curv[p] + bend[q * cells_x : (q + 1) * cells_x]
        return carry

    lax.fori_loop(0, planes // 2, local_pair, 0)

    to_below.wait_recv()
    to_above.wait_recv()
    row = lax.broadcasted_iota(jnp.int32, (8, 128), 0)
    is_edge = (row == 2) | (row == 4)

    def finish_pair(pair, carry):
        stacks = []
        for q in range(2):
            p = 2 * pair + q
            from_below, from_above = yr[0, p], yr[1, p]
            from_below = jnp.where(is_edge, ys[0, p] - from_below, from_below)
            from_above = jnp.where(is_edge, from_above - ys[1, p], from_above)
            ends = jnp.concatenate([from_below, from_above], axis=0)
            high = ends.astype(jnp.bfloat16).astype(jnp.float32)
            blank = jnp.zeros((FULL - 48, cells_x), jnp.float32)
            stacks.append(jnp.concatenate([high, ends - high, high, blank], axis=0).T)
        turned = jnp.concatenate(stacks, axis=0).astype(jnp.bfloat16)
        reach = [
            matmul(turned, mats[end_rows + n * FULL : end_rows + (n + 1) * FULL, :]) for n in range(3)
        ]
        for q in range(2):
            p = 2 * pair + q
            rows = slice(q * cells_x, (q + 1) * cells_x)
            grad = gy[p] + reach[0][rows]
            gy[p] = grad
            part = kap[p] * (curv[p] + reach[1][rows]) + (ky[p] + reach[2][rows]) * grad
            inner = slice(STRIP, top)
            dif[p, 0:STRIP, :] = part[0:STRIP]
            dif[p, inner, :] = part[inner] + kx[p, inner, :] * gx[p, inner, :]
            dif[p, top:, :] = part[top:]
        return carry

    lax.fori_loop(0, planes // 2, finish_pair, 0)
    pl.when(run_begins)(send_left)

    def combine(side, out):
        sign = 1.0 if side == 0 else -1.0
        jump = sign * (xs[side, 0] - xr[side, 0])
        kjump = sign * (xs[side, 1] - xr[side, 1])
        out[0] = FIRST.rho * xr[side, 2] + jump
        out[1] = SECOND.rho * xr[side, 3] + jump
        out[2] = jump
        out[3] = FIRST.rho * xr[side, 4] + kjump
        out[4] = kjump

    to_left.wait_recv()
    combine(1, xh)
    columns = [twice(tab[n, 0:STRIP]) for n in (8, 9)] + [twice(tab[n, 0:8]) for n in (10, 11)]
    for p in range(planes):
        gx[p, top:, :], dif[p, top:, :] = ends_applied(
            1,
            gx[p, top:, :],
            kx[p, top:, :],
            dif[p, top:, :],
            kap[p, top:, :],
            columns,
            [xh[n, p : p + 1, :] for n in range(5)],
        )
    for copy in (to_left, to_below, to_above, to_right):
        copy.wait_send()
    to_right.wait_recv()
    combine(0, xc)


def finish_kernel(gx, gy, dif, kx, kap, xc, tab, gx_out, gy_out, dif_out, gs, ds, sem):
    planes, cells_x, cells_y = gx.shape
    copies = []

    def store(source, target):
        copy = pltpu.make_async_copy(source, target, sem.at[len(copies)])
        copy.start()
        copies.append(copy)

    rest = pl.ds(STRIP, cells_x - STRIP)
    store(gy, gy_out)
    store(gx.at[:, rest, :], gx_out.at[:, rest, :])
    store(dif.at[:, rest, :], dif_out.at[:, rest, :])
    columns = [twice(tab[n, 0:STRIP]) for n in (0, 1)] + [twice(tab[n, 0:8]) for n in (2, 3)]
    for p in range(planes):
        gs[p], ds[p] = ends_applied(
            0,
            gx[p, 0:STRIP, :],
            kx[p, 0:STRIP, :],
            dif[p, 0:STRIP, :],
            kap[p, 0:STRIP, :],
            columns,
            [xc[n, p : p + 1, :] for n in range(5)],
        )
    store(gs, gx_out.at[:, pl.ds(0, STRIP), :])
    store(ds, dif_out.at[:, pl.ds(0, STRIP), :])
    for copy in copies:
        copy.wait()


def local(counts, scalar, diffusivity):
    block = scalar.shape
    planes, cells_x, cells_y = block
    columns = sum_columns(STRIP, SHORT) + sum_columns(REACH, REACH) + high_end_columns()
    tables = (
        jnp.asarray(stacked(columns)),
        jnp.asarray(
            np.concatenate([x_table(cells_x), y_table(cells_y), y_end_table(cells_y)], axis=0)
        ),
    )
    vmem, hbm = pl.BlockSpec(memory_space=pltpu.VMEM), pl.BlockSpec(memory_space=pltpu.HBM)
    field = jax.ShapeDtypeStruct(block, jnp.float32)
    field_buffer = pltpu.VMEM(block, jnp.float32)
    ends_shape = (5, planes, cells_y)
    operands = [
        pltpu.with_memory_space_constraint(array, pltpu.HBM)
        for array in (scalar, diffusivity) + tables
    ]
    parts = pl.pallas_call(
        functools.partial(exchange_kernel, counts),
        out_shape=(field,) * 5 + (jax.ShapeDtypeStruct(ends_shape, jnp.float32),),
        in_specs=[hbm] * 4,
        out_specs=(vmem,) * 6,
        scratch_shapes=[field_buffer]
        + [pltpu.VMEM(table.shape, table.dtype) for table in tables]
        + [field_buffer, field_buffer]
        + [pltpu.VMEM((2,) + ends_shape, jnp.float32)] * 2
        + [pltpu.VMEM((2, planes, 8, cells_x), jnp.float32)] * 2
        + [
            pltpu.VMEM(ends_shape, jnp.float32),
            pltpu.SemaphoreType.DMA((8,)),
            pltpu.SemaphoreType.DMA((4,)),
            pltpu.SemaphoreType.DMA((4,)),
            pltpu.SemaphoreType.REGULAR,
            pltpu.SemaphoreType.REGULAR,
        ],
        compiler_params=pltpu.CompilerParams(
            collective_id=0, has_side_effects=True, vmem_limit_bytes=LIMIT
        ),
        name="exchange",
    )(*operands)
    strip_buffer = pltpu.VMEM((planes, STRIP, cells_y), jnp.float32)
    return pl.pallas_call(
        finish_kernel,
        out_shape=(field,) * 3,
        in_specs=[vmem] * 7,
        out_specs=(hbm,) * 3,
        scratch_shapes=[strip_buffer, strip_buffer, pltpu.SemaphoreType.DMA((5,))],
        compiler_params=pltpu.CompilerParams(vmem_limit_bytes=LIMIT),
        name="finish",
    )(*parts, jnp.asarray(stacked(low_end_columns())))


def solution(mesh):
    placed = P(None, "gx", "gy")
    return jax.shard_map(
        functools.partial(local, (mesh.shape["gx"], mesh.shape["gy"])),
        mesh=mesh,
        in_specs=(placed, placed),
        out_specs=(placed,) * 3,
        check_vma=False,
    )
```

```python
import functools

import jax
import jax.numpy as jnp
import numpy as np
from jax import lax
from jax.experimental import pallas as pl
from jax.experimental.pallas import tpu as pltpu
from jax.sharding import PartitionSpec as P

FIRST_ALPHA = 1.0 / 3.0
FIRST_A = 14.0 / 9.0
FIRST_B = 1.0 / 9.0
SECOND_ALPHA = 2.0 / 11.0
SECOND_A = 12.0 / 11.0
SECOND_B = 3.0 / 11.0
MESH = pl.DeviceIdType.MESH
LIMIT = 28 * 1024 * 1024
STRIP = 24
SHORT = 16
REACH = 32
FULL = 128
RUN = 8


class Line:
    def __init__(self, alpha, taps):
        root = np.sqrt(1.0 - 4.0 * alpha * alpha)
        self.rho = (root - 1.0) / (2.0 * alpha)
        self.root, self.taps = root, taps
        self.ahead = sum(c * self.rho**m for m, c in taps.items()) / root
        self.behind = sum(c * self.rho**-m for m, c in taps.items()) / root

    def weight(self, n):
        n = np.asarray(n)
        return sum(c * self.rho ** np.abs(n + m) for m, c in self.taps.items()) / self.root

    def local(self, cells):
        i = np.arange(cells)
        table = self.weight(i[:, None] - i[None, :])
        table[:, cells - 1] = 0.0
        return table

    def low_sum(self, reach):
        power = self.rho ** np.arange(reach - 1)
        weights = np.zeros(reach)
        weights[1:] += power
        weights[:-1] -= power
        return weights


FIRST = Line(
    FIRST_ALPHA,
    {
        1: 0.25 * FIRST_B,
        0: 0.5 * FIRST_A + 0.25 * FIRST_B,
        -1: 0.5 * FIRST_A + 0.25 * FIRST_B,
        -2: 0.25 * FIRST_B,
    },
)
SECOND = Line(
    SECOND_ALPHA,
    {
        1: 0.25 * SECOND_B,
        0: SECOND_A + 0.25 * SECOND_B,
        -1: -SECOND_A - 0.25 * SECOND_B,
        -2: -0.25 * SECOND_B,
    },
)


def halves(table):
    high = np.asarray(table, np.float32).astype(jnp.bfloat16)
    low = (table - high.astype(np.float64)).astype(np.float32).astype(jnp.bfloat16)
    return high, low


def stacked(columns):
    table = np.zeros((len(columns), 32, 128), np.float32)
    for place, column in enumerate(columns):
        table[place, : len(column)] = column[:, None]
    return table


def sum_columns(reach, short):
    low = [FIRST.low_sum(reach), SECOND.low_sum(short)]
    return [-row[::-1] for row in low] + low


def high_end_columns():
    r = np.arange(STRIP)[::-1]
    columns = [(line.behind * line.rho**r) for line in (FIRST, SECOND)]
    for line in (FIRST, SECOND):
        column = np.zeros(8)
        column[7] = line.weight(0) - line.behind
        columns.append(column)
    return columns


def low_end_columns():
    r = np.arange(STRIP)
    columns = [(line.ahead * line.rho ** (r + 1)) for line in (FIRST, SECOND)]
    for line in (FIRST, SECOND):
        column = np.zeros(8)
        column[0] = line.weight(1) - line.ahead * line.rho
        columns.append(column)
    return columns


def x_table(cells):
    rows = []
    for line in (FIRST, SECOND):
        for half in halves(line.local(cells)):
            rows.append(np.concatenate([half, half], axis=1))
    return np.concatenate(rows, axis=0)


def y_table(cells):
    rows = []
    for line in (FIRST, SECOND):
        high, low = halves(line.local(cells).T)
        rows += [high, high, low]
    return np.concatenate(rows, axis=0)


def y_end_table(cells):
    i = np.arange(cells)
    blocks = []
    for line, sum_row, edge_row in ((FIRST, 0, 2), (SECOND, 1, 2), (FIRST, 3, 4)):
        table = np.zeros((16, cells))
        table[sum_row] = line.ahead * line.rho ** (i + 2)
        table[edge_row] = line.weight(i + 1)
        table[8 + sum_row] = line.behind * line.rho ** (cells - i)
        table[8 + edge_row] = line.weight(i - cells + 1)
        high, low = halves(table)
        blank = np.zeros((FULL - 48, cells), high.dtype)
        blocks += [high, high, low, blank]
    return np.concatenate(blocks, axis=0)


def split(values):
    high = values.astype(jnp.bfloat16)
    low = (values - high.astype(jnp.float32)).astype(jnp.bfloat16)
    return high, low


def matmul(left, right):
    return jnp.dot(left, right, preferred_element_type=jnp.float32)


def twice(tile):
    return jnp.concatenate([tile, tile], axis=1)


def ends_applied(side, grad, kgrad, part, kappa, columns, values):
    decay, decay_second, end, end_second = columns
    first, second, jump, kfirst, kjump = values
    grads, parts = [], []
    for tile in range(STRIP // 8):
        r = slice(8 * tile, 8 * tile + 8)
        g = grad[r] + decay[r] * first
        k = kgrad[r] + decay[r] * kfirst
        distance = tile if side == 0 else STRIP // 8 - 1 - tile
        d = part[r]
        if distance < 2:
            bend = decay_second[r] * second
            if distance == 0:
                g = g + end * jump
                k = k + end * kjump
                bend = bend + end_second * jump
            d = d + kappa[r] * bend
        grads.append(g)
        parts.append(d + k * g)
    return jnp.concatenate(grads, axis=0), jnp.concatenate(parts, axis=0)


def exchange_kernel(
    counts,
    f_hbm,
    k_hbm,
    tab_hbm,
    mats_hbm,
    gx,
    gy,
    dif,
    kx,
    kap,
    xc,
    low_tab,
    fld,
    tab,
    mats,
    curv,
    ky,
    xs,
    xr,
    ys,
    yr,
    xh,
    in_sem,
    send_sem,
    recv_sem,
    left_ready,
    above_ready,
):
    planes, cells_x, cells_y = fld.shape
    top = cells_x - STRIP
    other_rows = pl.ds(0, top)
    end_rows, next_rows = pl.ds(cells_x - 8, 8), pl.ds(top, STRIP - 8)

    def load(place, source, target):
        copy = pltpu.make_async_copy(source, target, in_sem.at[place])
        copy.start()
        return copy

    f_end_load = load(0, f_hbm.at[:, end_rows, :], fld.at[:, end_rows, :])
    k_end_load = load(3, k_hbm.at[:, end_rows, :], kap.at[:, end_rows, :])
    weights_load = load(2, tab_hbm.at[0:2], tab.at[0:2])
    f_high_load = load(1, f_hbm.at[:, next_rows, :], fld.at[:, next_rows, :])
    k_high_load = load(6, k_hbm.at[:, next_rows, :], kap.at[:, next_rows, :])
    other_loads = [
        load(4, f_hbm.at[:, other_rows, :], fld.at[:, other_rows, :]),
        load(5, k_hbm.at[:, other_rows, :], kap.at[:, other_rows, :]),
    ]

    ix, iy = lax.axis_index("gx"), lax.axis_index("gy")
    nx, ny = counts
    left = (jnp.where(ix == 0, nx - 1, ix - 1), iy)
    right = (jnp.where(ix == nx - 1, 0, ix + 1), iy)
    below = (ix, jnp.where(iy == 0, ny - 1, iy - 1))
    above = (ix, jnp.where(iy == ny - 1, 0, iy + 1))
    barrier = pltpu.get_barrier_semaphore()
    for neighbour in (left, above):
        pl.semaphore_signal(barrier, inc=1, device_id=neighbour, device_id_type=MESH)

    def tell(semaphore, neighbour):
        pl.semaphore_signal(semaphore, inc=1, device_id=neighbour, device_id_type=MESH)

    def message(place, source, target, device):
        return pltpu.make_async_remote_copy(
            src_ref=source,
            dst_ref=target,
            send_sem=send_sem.at[place],
            recv_sem=recv_sem.at[place],
            device_id=device,
            device_id_type=MESH,
        )

    def send(*what):
        copy = message(*what)
        copy.start()
        return copy

    def sums(side, place, field, start, reach, weights):
        with_weights = twice(tab[weights, 0:reach])
        for p in range(planes):
            rows = field[p, start : start + reach, :]
            xs[side, place, p : p + 1, :] = jnp.sum(rows * with_weights, axis=0, keepdims=True)

    def take_edge(side, place, field, edge):
        for p in range(planes):
            xs[side, place, p : p + 1, :] = field[p, edge : edge + 1, :]

    def send_right(place):
        send(1, xs.at[1, place : place + 1], xr.at[0, place : place + 1], right)

    f_end_load.wait()
    take_edge(1, 0, fld, cells_x - 1)
    pl.semaphore_wait(barrier, 2)
    send_right(0)
    k_end_load.wait()
    take_edge(1, 1, kap, cells_x - 1)
    send_right(1)
    table_load = load(0, mats_hbm, mats)
    weights_load.wait()
    other_loads.append(load(2, tab_hbm.at[2:12], tab.at[2:12]))
    f_high_load.wait()
    sums(1, 2, fld, top, STRIP, 0)
    send_right(2)
    low_load = load(1, tab_hbm.at[12:16], low_tab)
    sums(1, 3, fld, cells_x - SHORT, SHORT, 1)
    send_right(3)
    k_high_load.wait()
    sums(1, 4, kap, top, STRIP, 0)
    send_right(4)
    to_right = message(1, xs.at[1], xr.at[0], right)
    tell(left_ready, right)
    tell(above_ready, below)
    for copy in other_loads:
        copy.wait()
    take_edge(0, 0, fld, 0)
    take_edge(0, 1, kap, 0)
    sums(0, 2, fld, 0, STRIP, 2)
    sums(0, 3, fld, 0, SHORT, 3)
    sums(0, 4, kap, 0, STRIP, 2)

    ys[:, :, 5:8, :] = jnp.zeros((2, planes, 3, 128), jnp.float32)
    lane = lax.broadcasted_iota(jnp.int32, (cells_x, 128), 1)
    for p in range(planes):
        f_low, f_high = fld[p, :, 0:128], fld[p, :, cells_y - 128 : cells_y]
        k_low, k_high = kap[p, :, 0:128], kap[p, :, cells_y - 128 : cells_y]
        packed = jnp.where(
            lane < REACH,
            f_low,
            jnp.where(
                lane < 2 * REACH,
                pltpu.roll(k_low, REACH, 1),
                jnp.where(lane < 3 * REACH, pltpu.roll(k_high, 128 - REACH, 1), f_high),
            ),
        )
        turned = packed.T
        for side, place, f_part, k_part, f_edge, k_edge in (
            (0, 6, turned[0:32], turned[32:64], turned[0:1], turned[32:33]),
            (1, 4, turned[96:128], turned[64:96], turned[127:128], turned[95:96]),
        ):
            with_first, with_second = tab[place], tab[place + 1]
            ys[side, p, 0:1, :] = jnp.sum(f_part * with_first, axis=0, keepdims=True)
            ys[side, p, 1:2, :] = jnp.sum(f_part * with_second, axis=0, keepdims=True)
            ys[side, p, 2:3, :] = f_edge
            ys[side, p, 3:4, :] = jnp.sum(k_part * with_first, axis=0, keepdims=True)
            ys[side, p, 4:5, :] = k_edge
    to_below = send(2, ys.at[0], yr.at[1], below)
    pl.semaphore_wait(above_ready, 1)
    to_above = send(3, ys.at[1], yr.at[0], above)

    to_left = message(0, xs.at[0], xr.at[1], left)
    run_begins = lax.rem(ix, RUN) == 0

    def send_left():
        pl.semaphore_wait(left_ready, 1)
        to_left.start()

    pl.when(jnp.logical_not(run_begins))(send_left)

    table_load.wait()
    low_load.wait()
    x_rows = 4 * cells_x
    y_first = slice(x_rows, x_rows + 3 * cells_y)
    y_second = slice(x_rows + 3 * cells_y, x_rows + 6 * cells_y)
    ends_from = x_rows + 6 * cells_y

    def local_pair(pair, carry):
        tall, ktall = [], []
        for q in range(2):
            p = 2 * pair + q
            f, k = fld[p], kap[p]
            high, low = split(pltpu.roll(f, cells_x - 1, 0) - f)
            along = matmul(mats[0:x_rows, :], jnp.concatenate([high, low], axis=0))
            gx[p] = along[0:cells_x] + along[cells_x : 2 * cells_x]
            curv[p] = along[2 * cells_x : 3 * cells_x] + along[3 * cells_x : 4 * cells_x]
            high, low = split(pltpu.roll(k, cells_x - 1, 0) - k)
            along = matmul(mats[0 : 2 * cells_x, :], jnp.concatenate([high, low], axis=0))
            kx[p] = along[0:cells_x] + along[cells_x : 2 * cells_x]
            high, low = split(pltpu.roll(f, cells_y - 1, 1) - f)
            tall.append(jnp.concatenate([high, low, high], axis=1))
            high, low = split(pltpu.roll(k, cells_y - 1, 1) - k)
            ktall.append(jnp.concatenate([high, low, high], axis=1))
        across = matmul(jnp.concatenate(tall + ktall, axis=0), mats[y_first, :])
        bend = matmul(jnp.concatenate(tall, axis=0), mats[y_second, :])
        for q in range(2):
            p = 2 * pair + q
            gy[p] = across[q * cells_x : (q + 1) * cells_x]
            ky[p] = across[(q + 2) * cells_x : (q + 3) * cells_x]
            curv[p] = curv[p] + bend[q * cells_x : (q + 1) * cells_x]
        return carry

    lax.fori_loop(0, planes // 2, local_pair, 0)

    to_below.wait_recv()
    to_above.wait_recv()
    row = lax.broadcasted_iota(jnp.int32, (8, 128), 0)
    is_edge = (row == 2) | (row == 4)

    def finish_pair(pair, carry):
        stacks = []
        for q in range(2):
            p = 2 * pair + q
            from_below, from_above = yr[0, p], yr[1, p]
            from_below = jnp.where(is_edge, ys[0, p] - from_below, from_below)
            from_above = jnp.where(is_edge, from_above - ys[1, p], from_above)
            ends = jnp.concatenate([from_below, from_above], axis=0)
            high = ends.astype(jnp.bfloat16).astype(jnp.float32)
            blank = jnp.zeros((FULL - 48, cells_x), jnp.float32)
            stacks.append(jnp.concatenate([high, ends - high, high, blank], axis=0).T)
        turned = jnp.concatenate(stacks, axis=0).astype(jnp.bfloat16)
        reach = [
            matmul(turned, mats[ends_from + n * FULL : ends_from + (n + 1) * FULL, :]) for n in range(3)
        ]
        for q in range(2):
            p = 2 * pair + q
            rows = slice(q * cells_x, (q + 1) * cells_x)
            grad = gy[p] + reach[0][rows]
            gy[p] = grad
            part = kap[p] * (curv[p] + reach[1][rows]) + (ky[p] + reach[2][rows]) * grad
            inner = slice(STRIP, top)
            dif[p, 0:STRIP, :] = part[0:STRIP]
            dif[p, inner, :] = part[inner] + kx[p, inner, :] * gx[p, inner, :]
            dif[p, top:, :] = part[top:]
        return carry

    lax.fori_loop(0, planes // 2, finish_pair, 0)
    pl.when(run_begins)(send_left)

    def combine(side, out):
        sign = 1.0 if side == 0 else -1.0
        jump = sign * (xs[side, 0] - xr[side, 0])
        kjump = sign * (xs[side, 1] - xr[side, 1])
        out[0] = FIRST.rho * xr[side, 2] + jump
        out[1] = SECOND.rho * xr[side, 3] + jump
        out[2] = jump
        out[3] = FIRST.rho * xr[side, 4] + kjump
        out[4] = kjump

    to_left.wait_recv()
    combine(1, xh)
    columns = [twice(tab[n, 0:STRIP]) for n in (8, 9)] + [twice(tab[n, 0:8]) for n in (10, 11)]
    for p in range(planes):
        gx[p, top:, :], dif[p, top:, :] = ends_applied(
            1,
            gx[p, top:, :],
            kx[p, top:, :],
            dif[p, top:, :],
            kap[p, top:, :],
            columns,
            [xh[n, p : p + 1, :] for n in range(5)],
        )
    for copy in (to_left, to_below, to_above, to_right):
        copy.wait_send()
    to_right.wait_recv()
    combine(0, xc)


def finish_kernel(gx, gy, dif, kx, kap, xc, tab, gx_out, gy_out, dif_out, gs, ds, sem):
    planes, cells_x, cells_y = gx.shape
    copies = []

    def store(source, target):
        copy = pltpu.make_async_copy(source, target, sem.at[len(copies)])
        copy.start()
        copies.append(copy)

    rest = pl.ds(STRIP, cells_x - STRIP)
    store(gy, gy_out)
    store(gx.at[:, rest, :], gx_out.at[:, rest, :])
    store(dif.at[:, rest, :], dif_out.at[:, rest, :])
    columns = [twice(tab[n, 0:STRIP]) for n in (0, 1)] + [twice(tab[n, 0:8]) for n in (2, 3)]
    for p in range(planes):
        gs[p], ds[p] = ends_applied(
            0,
            gx[p, 0:STRIP, :],
            kx[p, 0:STRIP, :],
            dif[p, 0:STRIP, :],
            kap[p, 0:STRIP, :],
            columns,
            [xc[n, p : p + 1, :] for n in range(5)],
        )
    store(gs, gx_out.at[:, pl.ds(0, STRIP), :])
    store(ds, dif_out.at[:, pl.ds(0, STRIP), :])
    for copy in copies:
        copy.wait()


def local(counts, scalar, diffusivity):
    block = scalar.shape
    planes, cells_x, cells_y = block
    columns = sum_columns(STRIP, SHORT) + sum_columns(REACH, REACH)
    columns += high_end_columns() + low_end_columns()
    tables = (
        jnp.asarray(stacked(columns)),
        jnp.asarray(
            np.concatenate([x_table(cells_x), y_table(cells_y), y_end_table(cells_y)], axis=0)
        ),
    )
    vmem, hbm = pl.BlockSpec(memory_space=pltpu.VMEM), pl.BlockSpec(memory_space=pltpu.HBM)
    field = jax.ShapeDtypeStruct(block, jnp.float32)
    field_buffer = pltpu.VMEM(block, jnp.float32)
    ends_shape = (5, planes, cells_y)
    operands = [
        pltpu.with_memory_space_constraint(array, pltpu.HBM)
        for array in (scalar, diffusivity) + tables
    ]
    parts = pl.pallas_call(
        functools.partial(exchange_kernel, counts),
        out_shape=(field,) * 5 + (jax.ShapeDtypeStruct(ends_shape, jnp.float32), jax.ShapeDtypeStruct((4, 32, 128), jnp.float32)),
        in_specs=[hbm] * 4,
        out_specs=(vmem,) * 7,
        scratch_shapes=[field_buffer]
        + [pltpu.VMEM(table.shape, table.dtype) for table in tables]
        + [field_buffer, field_buffer]
        + [pltpu.VMEM((2,) + ends_shape, jnp.float32)] * 2
        + [pltpu.VMEM((2, planes, 8, cells_x), jnp.float32)] * 2
        + [
            pltpu.VMEM(ends_shape, jnp.float32),
            pltpu.SemaphoreType.DMA((7,)),
            pltpu.SemaphoreType.DMA((4,)),
            pltpu.SemaphoreType.DMA((4,)),
            pltpu.SemaphoreType.REGULAR,
            pltpu.SemaphoreType.REGULAR,
        ],
        compiler_params=pltpu.CompilerParams(
            collective_id=0, has_side_effects=True, vmem_limit_bytes=LIMIT
        ),
        name="exchange",
    )(*operands)
    strip_buffer = pltpu.VMEM((planes, STRIP, cells_y), jnp.float32)
    return pl.pallas_call(
        finish_kernel,
        out_shape=(field,) * 3,
        in_specs=[vmem] * 7,
        out_specs=(hbm,) * 3,
        scratch_shapes=[strip_buffer, strip_buffer, pltpu.SemaphoreType.DMA((5,))],
        compiler_params=pltpu.CompilerParams(vmem_limit_bytes=LIMIT),
        name="finish",
    )(*parts)


def solution(mesh):
    placed = P(None, "gx", "gy")
    return jax.shard_map(
        functools.partial(local, (mesh.shape["gx"], mesh.shape["gy"])),
        mesh=mesh,
        in_specs=(placed, placed),
        out_specs=(placed,) * 3,
        check_vma=False,
    )
```

```python
import functools

import jax
import jax.numpy as jnp
import numpy as np
from jax import lax
from jax.experimental import pallas as pl
from jax.experimental.pallas import tpu as pltpu
from jax.sharding import PartitionSpec as P

FIRST_ALPHA = 1.0 / 3.0
FIRST_A = 14.0 / 9.0
FIRST_B = 1.0 / 9.0
SECOND_ALPHA = 2.0 / 11.0
SECOND_A = 12.0 / 11.0
SECOND_B = 3.0 / 11.0
MESH = pl.DeviceIdType.MESH
LIMIT = 28 * 1024 * 1024
STRIP = 24
SHORT = 16
REACH = 32
FULL = 128
RUN = 8


class Line:
    def __init__(self, alpha, taps):
        root = np.sqrt(1.0 - 4.0 * alpha * alpha)
        self.rho = (root - 1.0) / (2.0 * alpha)
        self.root, self.taps = root, taps
        self.ahead = sum(c * self.rho**m for m, c in taps.items()) / root
        self.behind = sum(c * self.rho**-m for m, c in taps.items()) / root

    def weight(self, n):
        n = np.asarray(n)
        return sum(c * self.rho ** np.abs(n + m) for m, c in self.taps.items()) / self.root

    def local(self, cells):
        i = np.arange(cells)
        table = self.weight(i[:, None] - i[None, :])
        table[:, cells - 1] = 0.0
        return table

    def low_sum(self, reach):
        power = self.rho ** np.arange(reach - 1)
        weights = np.zeros(reach)
        weights[1:] += power
        weights[:-1] -= power
        return weights


FIRST = Line(
    FIRST_ALPHA,
    {
        1: 0.25 * FIRST_B,
        0: 0.5 * FIRST_A + 0.25 * FIRST_B,
        -1: 0.5 * FIRST_A + 0.25 * FIRST_B,
        -2: 0.25 * FIRST_B,
    },
)
SECOND = Line(
    SECOND_ALPHA,
    {
        1: 0.25 * SECOND_B,
        0: SECOND_A + 0.25 * SECOND_B,
        -1: -SECOND_A - 0.25 * SECOND_B,
        -2: -0.25 * SECOND_B,
    },
)


def halves(table):
    high = np.asarray(table, np.float32).astype(jnp.bfloat16)
    low = (table - high.astype(np.float64)).astype(np.float32).astype(jnp.bfloat16)
    return high, low


def stacked(columns):
    table = np.zeros((len(columns), 32, 128), np.float32)
    for place, column in enumerate(columns):
        table[place, : len(column)] = column[:, None]
    return table


def sum_columns(reach, short):
    low = [FIRST.low_sum(reach), SECOND.low_sum(short)]
    return [-row[::-1] for row in low] + low


def high_end_columns():
    r = np.arange(STRIP)[::-1]
    columns = [(line.behind * line.rho**r) for line in (FIRST, SECOND)]
    for line in (FIRST, SECOND):
        column = np.zeros(8)
        column[7] = line.weight(0) - line.behind
        columns.append(column)
    return columns


def low_end_columns():
    r = np.arange(STRIP)
    columns = [(line.ahead * line.rho ** (r + 1)) for line in (FIRST, SECOND)]
    for line in (FIRST, SECOND):
        column = np.zeros(8)
        column[0] = line.weight(1) - line.ahead * line.rho
        columns.append(column)
    return columns


def x_table(cells):
    rows = []
    for line in (FIRST, SECOND):
        for half in halves(line.local(cells)):
            rows.append(np.concatenate([half, half], axis=1))
    return np.concatenate(rows, axis=0)


def y_table(cells):
    rows = []
    for line in (FIRST, SECOND):
        high, low = halves(line.local(cells).T)
        rows += [high, high, low]
    return np.concatenate(rows, axis=0)


def y_end_table(cells):
    i = np.arange(cells)
    blocks = []
    for line, sum_row, edge_row in ((FIRST, 0, 2), (SECOND, 1, 2), (FIRST, 3, 4)):
        table = np.zeros((16, cells))
        table[sum_row] = line.ahead * line.rho ** (i + 2)
        table[edge_row] = line.weight(i + 1)
        table[8 + sum_row] = line.behind * line.rho ** (cells - i)
        table[8 + edge_row] = line.weight(i - cells + 1)
        high, low = halves(table)
        blank = np.zeros((FULL - 48, cells), high.dtype)
        blocks += [high, high, low, blank]
    return np.concatenate(blocks, axis=0)


def split(values):
    high = values.astype(jnp.bfloat16)
    low = (values - high.astype(jnp.float32)).astype(jnp.bfloat16)
    return high, low


def matmul(left, right):
    return jnp.dot(left, right, preferred_element_type=jnp.float32)


def twice(tile):
    return jnp.concatenate([tile, tile], axis=1)


def ends_applied(side, grad, kgrad, part, kappa, columns, values):
    decay, decay_second, end, end_second = columns
    first, second, jump, kfirst, kjump = values
    grads, parts = [], []
    for tile in range(STRIP // 8):
        r = slice(8 * tile, 8 * tile + 8)
        g = grad[r] + decay[r] * first
        k = kgrad[r] + decay[r] * kfirst
        distance = tile if side == 0 else STRIP // 8 - 1 - tile
        d = part[r]
        if distance < 2:
            bend = decay_second[r] * second
            if distance == 0:
                g = g + end * jump
                k = k + end * kjump
                bend = bend + end_second * jump
            d = d + kappa[r] * bend
        grads.append(g)
        parts.append(d + k * g)
    return jnp.concatenate(grads, axis=0), jnp.concatenate(parts, axis=0)


def exchange_kernel(
    counts,
    f_hbm,
    k_hbm,
    tab_hbm,
    mats_hbm,
    gx,
    gy,
    dif,
    kx,
    kap,
    xc,
    low_tab,
    fld,
    tab,
    mats,
    curv,
    ky,
    xs,
    xr,
    ys,
    yr,
    xh,
    in_sem,
    send_sem,
    recv_sem,
    left_ready,
    above_ready,
):
    planes, cells_x, cells_y = fld.shape
    top = cells_x - STRIP
    other_rows = pl.ds(0, top)
    end_rows, next_rows = pl.ds(cells_x - 8, 8), pl.ds(top, STRIP - 8)

    def load(place, source, target):
        copy = pltpu.make_async_copy(source, target, in_sem.at[place])
        copy.start()
        return copy

    f_end_load = load(0, f_hbm.at[:, end_rows, :], fld.at[:, end_rows, :])
    k_end_load = load(3, k_hbm.at[:, end_rows, :], kap.at[:, end_rows, :])
    weights_load = load(2, tab_hbm.at[0:2], tab.at[0:2])
    f_high_load = load(1, f_hbm.at[:, next_rows, :], fld.at[:, next_rows, :])
    k_high_load = load(6, k_hbm.at[:, next_rows, :], kap.at[:, next_rows, :])
    table_rest = load(7, tab_hbm.at[2:12], tab.at[2:12])
    other_loads = [
        table_rest,
        load(4, f_hbm.at[:, other_rows, :], fld.at[:, other_rows, :]),
        load(5, k_hbm.at[:, other_rows, :], kap.at[:, other_rows, :]),
    ]
    table_load = load(8, mats_hbm, mats)

    ix, iy = lax.axis_index("gx"), lax.axis_index("gy")
    nx, ny = counts
    left = (jnp.where(ix == 0, nx - 1, ix - 1), iy)
    right = (jnp.where(ix == nx - 1, 0, ix + 1), iy)
    below = (ix, jnp.where(iy == 0, ny - 1, iy - 1))
    above = (ix, jnp.where(iy == ny - 1, 0, iy + 1))
    barrier = pltpu.get_barrier_semaphore()
    for neighbour in (left, above):
        pl.semaphore_signal(barrier, inc=1, device_id=neighbour, device_id_type=MESH)

    def tell(semaphore, neighbour):
        pl.semaphore_signal(semaphore, inc=1, device_id=neighbour, device_id_type=MESH)

    def message(place, source, target, device):
        return pltpu.make_async_remote_copy(
            src_ref=source,
            dst_ref=target,
            send_sem=send_sem.at[place],
            recv_sem=recv_sem.at[place],
            device_id=device,
            device_id_type=MESH,
        )

    def send(*what):
        copy = message(*what)
        copy.start()
        return copy

    def sums(side, place, field, start, reach, weights):
        with_weights = twice(tab[weights, 0:reach])
        for p in range(planes):
            rows = field[p, start : start + reach, :]
            xs[side, place, p : p + 1, :] = jnp.sum(rows * with_weights, axis=0, keepdims=True)

    def take_edge(side, place, field, edge):
        for p in range(planes):
            xs[side, place, p : p + 1, :] = field[p, edge : edge + 1, :]

    def send_right(place):
        send(1, xs.at[1, place : place + 1], xr.at[0, place : place + 1], right)

    f_end_load.wait()
    take_edge(1, 0, fld, cells_x - 1)
    pl.semaphore_wait(barrier, 2)
    tell(left_ready, right)
    send_right(0)
    k_end_load.wait()
    take_edge(1, 1, kap, cells_x - 1)
    send_right(1)
    weights_load.wait()
    f_high_load.wait()
    sums(1, 2, fld, top, STRIP, 0)
    send_right(2)
    low_load = load(1, tab_hbm.at[12:16], low_tab)
    sums(1, 3, fld, cells_x - SHORT, SHORT, 1)
    send_right(3)
    k_high_load.wait()
    sums(1, 4, kap, top, STRIP, 0)
    send_right(4)
    to_right = message(1, xs.at[1], xr.at[0], right)
    tell(above_ready, below)
    for copy in other_loads:
        copy.wait()
    take_edge(0, 0, fld, 0)
    take_edge(0, 1, kap, 0)
    sums(0, 2, fld, 0, STRIP, 2)
    sums(0, 3, fld, 0, SHORT, 3)
    sums(0, 4, kap, 0, STRIP, 2)

    ys[:, :, 5:8, :] = jnp.zeros((2, planes, 3, 128), jnp.float32)
    lane = lax.broadcasted_iota(jnp.int32, (cells_x, 128), 1)
    for p in range(planes):
        f_low, f_high = fld[p, :, 0:128], fld[p, :, cells_y - 128 : cells_y]
        k_low, k_high = kap[p, :, 0:128], kap[p, :, cells_y - 128 : cells_y]
        packed = jnp.where(
            lane < REACH,
            f_low,
            jnp.where(
                lane < 2 * REACH,
                pltpu.roll(k_low, REACH, 1),
                jnp.where(lane < 3 * REACH, pltpu.roll(k_high, 128 - REACH, 1), f_high),
            ),
        )
        turned = packed.T
        for side, place, f_part, k_part, f_edge, k_edge in (
            (0, 6, turned[0:32], turned[32:64], turned[0:1], turned[32:33]),
            (1, 4, turned[96:128], turned[64:96], turned[127:128], turned[95:96]),
        ):
            with_first, with_second = tab[place], tab[place + 1]
            ys[side, p, 0:1, :] = jnp.sum(f_part * with_first, axis=0, keepdims=True)
            ys[side, p, 1:2, :] = jnp.sum(f_part * with_second, axis=0, keepdims=True)
            ys[side, p, 2:3, :] = f_edge
            ys[side, p, 3:4, :] = jnp.sum(k_part * with_first, axis=0, keepdims=True)
            ys[side, p, 4:5, :] = k_edge
    to_below = send(2, ys.at[0], yr.at[1], below)
    pl.semaphore_wait(above_ready, 1)
    to_above = send(3, ys.at[1], yr.at[0], above)

    to_left = message(0, xs.at[0], xr.at[1], left)
    run_begins = lax.rem(ix, RUN) == 0

    def send_left():
        pl.semaphore_wait(left_ready, 1)
        to_left.start()

    pl.when(jnp.logical_not(run_begins))(send_left)

    table_load.wait()
    low_load.wait()
    x_rows = 4 * cells_x
    y_first = slice(x_rows, x_rows + 3 * cells_y)
    y_second = slice(x_rows + 3 * cells_y, x_rows + 6 * cells_y)
    ends_from = x_rows + 6 * cells_y

    def local_pair(pair, carry):
        tall, ktall = [], []
        for q in range(2):
            p = 2 * pair + q
            f, k = fld[p], kap[p]
            high, low = split(pltpu.roll(f, cells_x - 1, 0) - f)
            along = matmul(mats[0:x_rows, :], jnp.concatenate([high, low], axis=0))
            gx[p] = along[0:cells_x] + along[cells_x : 2 * cells_x]
            curv[p] = along[2 * cells_x : 3 * cells_x] + along[3 * cells_x : 4 * cells_x]
            high, low = split(pltpu.roll(k, cells_x - 1, 0) - k)
            along = matmul(mats[0 : 2 * cells_x, :], jnp.concatenate([high, low], axis=0))
            kx[p] = along[0:cells_x] + along[cells_x : 2 * cells_x]
            high, low = split(pltpu.roll(f, cells_y - 1, 1) - f)
            tall.append(jnp.concatenate([high, low, high], axis=1))
            high, low = split(pltpu.roll(k, cells_y - 1, 1) - k)
            ktall.append(jnp.concatenate([high, low, high], axis=1))
        across = matmul(jnp.concatenate(tall + ktall, axis=0), mats[y_first, :])
        bend = matmul(jnp.concatenate(tall, axis=0), mats[y_second, :])
        for q in range(2):
            p = 2 * pair + q
            gy[p] = across[q * cells_x : (q + 1) * cells_x]
            ky[p] = across[(q + 2) * cells_x : (q + 3) * cells_x]
            curv[p] = curv[p] + bend[q * cells_x : (q + 1) * cells_x]
        return carry

    lax.fori_loop(0, planes // 2, local_pair, 0)

    to_below.wait_recv()
    to_above.wait_recv()
    row = lax.broadcasted_iota(jnp.int32, (8, 128), 0)
    is_edge = (row == 2) | (row == 4)

    def finish_pair(pair, carry):
        stacks = []
        for q in range(2):
            p = 2 * pair + q
            from_below, from_above = yr[0, p], yr[1, p]
            from_below = jnp.where(is_edge, ys[0, p] - from_below, from_below)
            from_above = jnp.where(is_edge, from_above - ys[1, p], from_above)
            ends = jnp.concatenate([from_below, from_above], axis=0)
            high = ends.astype(jnp.bfloat16).astype(jnp.float32)
            blank = jnp.zeros((FULL - 48, cells_x), jnp.float32)
            stacks.append(jnp.concatenate([high, ends - high, high, blank], axis=0).T)
        turned = jnp.concatenate(stacks, axis=0).astype(jnp.bfloat16)
        reach = [
            matmul(turned, mats[ends_from + n * FULL : ends_from + (n + 1) * FULL, :]) for n in range(3)
        ]
        for q in range(2):
            p = 2 * pair + q
            rows = slice(q * cells_x, (q + 1) * cells_x)
            grad = gy[p] + reach[0][rows]
            gy[p] = grad
            part = kap[p] * (curv[p] + reach[1][rows]) + (ky[p] + reach[2][rows]) * grad
            inner = slice(STRIP, top)
            dif[p, 0:STRIP, :] = part[0:STRIP]
            dif[p, inner, :] = part[inner] + kx[p, inner, :] * gx[p, inner, :]
            dif[p, top:, :] = part[top:]
        return carry

    lax.fori_loop(0, planes // 2, finish_pair, 0)
    pl.when(run_begins)(send_left)

    def combine(side, out):
        sign = 1.0 if side == 0 else -1.0
        jump = sign * (xs[side, 0] - xr[side, 0])
        kjump = sign * (xs[side, 1] - xr[side, 1])
        out[0] = FIRST.rho * xr[side, 2] + jump
        out[1] = SECOND.rho * xr[side, 3] + jump
        out[2] = jump
        out[3] = FIRST.rho * xr[side, 4] + kjump
        out[4] = kjump

    to_left.wait_recv()
    combine(1, xh)
    columns = [twice(tab[n, 0:STRIP]) for n in (8, 9)] + [twice(tab[n, 0:8]) for n in (10, 11)]
    for p in range(planes):
        gx[p, top:, :], dif[p, top:, :] = ends_applied(
            1,
            gx[p, top:, :],
            kx[p, top:, :],
            dif[p, top:, :],
            kap[p, top:, :],
            columns,
            [xh[n, p : p + 1, :] for n in range(5)],
        )
    for copy in (to_left, to_below, to_above, to_right):
        copy.wait_send()
    to_right.wait_recv()
    combine(0, xc)


def finish_kernel(gx, gy, dif, kx, kap, xc, tab, gx_out, gy_out, dif_out, gs, ds, sem):
    planes, cells_x, cells_y = gx.shape
    copies = []

    def store(source, target):
        copy = pltpu.make_async_copy(source, target, sem.at[len(copies)])
        copy.start()
        copies.append(copy)

    rest = pl.ds(STRIP, cells_x - STRIP)
    store(gy, gy_out)
    store(gx.at[:, rest, :], gx_out.at[:, rest, :])
    store(dif.at[:, rest, :], dif_out.at[:, rest, :])
    columns = [twice(tab[n, 0:STRIP]) for n in (0, 1)] + [twice(tab[n, 0:8]) for n in (2, 3)]
    for p in range(planes):
        gs[p], ds[p] = ends_applied(
            0,
            gx[p, 0:STRIP, :],
            kx[p, 0:STRIP, :],
            dif[p, 0:STRIP, :],
            kap[p, 0:STRIP, :],
            columns,
            [xc[n, p : p + 1, :] for n in range(5)],
        )
    store(gs, gx_out.at[:, pl.ds(0, STRIP), :])
    store(ds, dif_out.at[:, pl.ds(0, STRIP), :])
    for copy in copies:
        copy.wait()


def local(counts, scalar, diffusivity):
    block = scalar.shape
    planes, cells_x, cells_y = block
    columns = sum_columns(STRIP, SHORT) + sum_columns(REACH, REACH)
    columns += high_end_columns() + low_end_columns()
    tables = (
        jnp.asarray(stacked(columns)),
        jnp.asarray(
            np.concatenate([x_table(cells_x), y_table(cells_y), y_end_table(cells_y)], axis=0)
        ),
    )
    vmem, hbm = pl.BlockSpec(memory_space=pltpu.VMEM), pl.BlockSpec(memory_space=pltpu.HBM)
    field = jax.ShapeDtypeStruct(block, jnp.float32)
    field_buffer = pltpu.VMEM(block, jnp.float32)
    ends_shape = (5, planes, cells_y)
    operands = [
        pltpu.with_memory_space_constraint(array, pltpu.HBM)
        for array in (scalar, diffusivity) + tables
    ]
    parts = pl.pallas_call(
        functools.partial(exchange_kernel, counts),
        out_shape=(field,) * 5 + (jax.ShapeDtypeStruct(ends_shape, jnp.float32), jax.ShapeDtypeStruct((4, 32, 128), jnp.float32)),
        in_specs=[hbm] * 4,
        out_specs=(vmem,) * 7,
        scratch_shapes=[field_buffer]
        + [pltpu.VMEM(table.shape, table.dtype) for table in tables]
        + [field_buffer, field_buffer]
        + [pltpu.VMEM((2,) + ends_shape, jnp.float32)] * 2
        + [pltpu.VMEM((2, planes, 8, cells_x), jnp.float32)] * 2
        + [
            pltpu.VMEM(ends_shape, jnp.float32),
            pltpu.SemaphoreType.DMA((9,)),
            pltpu.SemaphoreType.DMA((4,)),
            pltpu.SemaphoreType.DMA((4,)),
            pltpu.SemaphoreType.REGULAR,
            pltpu.SemaphoreType.REGULAR,
        ],
        compiler_params=pltpu.CompilerParams(
            collective_id=0, has_side_effects=True, vmem_limit_bytes=LIMIT
        ),
        name="exchange",
    )(*operands)
    strip_buffer = pltpu.VMEM((planes, STRIP, cells_y), jnp.float32)
    return pl.pallas_call(
        finish_kernel,
        out_shape=(field,) * 3,
        in_specs=[vmem] * 7,
        out_specs=(hbm,) * 3,
        scratch_shapes=[strip_buffer, strip_buffer, pltpu.SemaphoreType.DMA((5,))],
        compiler_params=pltpu.CompilerParams(vmem_limit_bytes=LIMIT),
        name="finish",
    )(*parts)


def solution(mesh):
    placed = P(None, "gx", "gy")
    return jax.shard_map(
        functools.partial(local, (mesh.shape["gx"], mesh.shape["gy"])),
        mesh=mesh,
        in_specs=(placed, placed),
        out_specs=(placed,) * 3,
        check_vma=False,
    )
```

```python
import functools

import jax
import jax.numpy as jnp
import numpy as np
from jax import lax
from jax.experimental import pallas as pl
from jax.experimental.pallas import tpu as pltpu
from jax.sharding import PartitionSpec as P

FIRST_ALPHA = 1.0 / 3.0
FIRST_A = 14.0 / 9.0
FIRST_B = 1.0 / 9.0
SECOND_ALPHA = 2.0 / 11.0
SECOND_A = 12.0 / 11.0
SECOND_B = 3.0 / 11.0
MESH = pl.DeviceIdType.MESH
LIMIT = 28 * 1024 * 1024
STRIP = 24
SHORT = 16
REACH = 32
FULL = 128
RUN = 8


class Line:
    def __init__(self, alpha, taps):
        root = np.sqrt(1.0 - 4.0 * alpha * alpha)
        self.rho = (root - 1.0) / (2.0 * alpha)
        self.root, self.taps = root, taps
        self.ahead = sum(c * self.rho**m for m, c in taps.items()) / root
        self.behind = sum(c * self.rho**-m for m, c in taps.items()) / root

    def weight(self, n):
        n = np.asarray(n)
        return sum(c * self.rho ** np.abs(n + m) for m, c in self.taps.items()) / self.root

    def local(self, cells):
        i = np.arange(cells)
        table = self.weight(i[:, None] - i[None, :])
        table[:, cells - 1] = 0.0
        return table

    def low_sum(self, reach):
        power = self.rho ** np.arange(reach - 1)
        weights = np.zeros(reach)
        weights[1:] += power
        weights[:-1] -= power
        return weights


FIRST = Line(
    FIRST_ALPHA,
    {
        1: 0.25 * FIRST_B,
        0: 0.5 * FIRST_A + 0.25 * FIRST_B,
        -1: 0.5 * FIRST_A + 0.25 * FIRST_B,
        -2: 0.25 * FIRST_B,
    },
)
SECOND = Line(
    SECOND_ALPHA,
    {
        1: 0.25 * SECOND_B,
        0: SECOND_A + 0.25 * SECOND_B,
        -1: -SECOND_A - 0.25 * SECOND_B,
        -2: -0.25 * SECOND_B,
    },
)


def halves(table):
    high = np.asarray(table, np.float32).astype(jnp.bfloat16)
    low = (table - high.astype(np.float64)).astype(np.float32).astype(jnp.bfloat16)
    return high, low


def stacked(columns):
    table = np.zeros((len(columns), 32, 128), np.float32)
    for place, column in enumerate(columns):
        table[place, : len(column)] = column[:, None]
    return table


def sum_columns(reach, short):
    low = [FIRST.low_sum(reach), SECOND.low_sum(short)]
    return [-row[::-1] for row in low] + low


def high_end_columns():
    r = np.arange(STRIP)[::-1]
    columns = [(line.behind * line.rho**r) for line in (FIRST, SECOND)]
    for line in (FIRST, SECOND):
        column = np.zeros(8)
        column[7] = line.weight(0) - line.behind
        columns.append(column)
    return columns


def low_end_columns():
    r = np.arange(STRIP)
    columns = [(line.ahead * line.rho ** (r + 1)) for line in (FIRST, SECOND)]
    for line in (FIRST, SECOND):
        column = np.zeros(8)
        column[0] = line.weight(1) - line.ahead * line.rho
        columns.append(column)
    return columns


def x_table(cells):
    rows = []
    for line in (FIRST, SECOND):
        for half in halves(line.local(cells)):
            rows.append(np.concatenate([half, half], axis=1))
    return np.concatenate(rows, axis=0)


def y_table(cells):
    rows = []
    for line in (FIRST, SECOND):
        high, low = halves(line.local(cells).T)
        rows += [high, high, low]
    return np.concatenate(rows, axis=0)


def y_end_table(cells):
    i = np.arange(cells)
    blocks = []
    for line, sum_row, edge_row in ((FIRST, 0, 2), (SECOND, 1, 2), (FIRST, 3, 4)):
        table = np.zeros((16, cells))
        table[sum_row] = line.ahead * line.rho ** (i + 2)
        table[edge_row] = line.weight(i + 1)
        table[8 + sum_row] = line.behind * line.rho ** (cells - i)
        table[8 + edge_row] = line.weight(i - cells + 1)
        high, low = halves(table)
        blank = np.zeros((FULL - 48, cells), high.dtype)
        blocks += [high, high, low, blank]
    return np.concatenate(blocks, axis=0)


def split(values):
    high = values.astype(jnp.bfloat16)
    low = (values - high.astype(jnp.float32)).astype(jnp.bfloat16)
    return high, low


def matmul(left, right):
    return jnp.dot(left, right, preferred_element_type=jnp.float32)


def twice(tile):
    return jnp.concatenate([tile, tile], axis=1)


def ends_applied(side, grad, kgrad, part, kappa, columns, values):
    decay, decay_second, end, end_second = columns
    first, second, jump, kfirst, kjump = values
    grads, parts = [], []
    for tile in range(STRIP // 8):
        r = slice(8 * tile, 8 * tile + 8)
        g = grad[r] + decay[r] * first
        k = kgrad[r] + decay[r] * kfirst
        distance = tile if side == 0 else STRIP // 8 - 1 - tile
        d = part[r]
        if distance < 2:
            bend = decay_second[r] * second
            if distance == 0:
                g = g + end * jump
                k = k + end * kjump
                bend = bend + end_second * jump
            d = d + kappa[r] * bend
        grads.append(g)
        parts.append(d + k * g)
    return jnp.concatenate(grads, axis=0), jnp.concatenate(parts, axis=0)


def exchange_kernel(
    counts,
    f_hbm,
    k_hbm,
    tab_hbm,
    mats_hbm,
    gx,
    gy,
    dif,
    kx,
    kap,
    xc,
    low_tab,
    fld,
    tab,
    mats,
    curv,
    ky,
    xs,
    xr,
    ys,
    yr,
    xh,
    in_sem,
    send_sem,
    recv_sem,
    left_ready,
    above_ready,
    below_ready,
):
    planes, cells_x, cells_y = fld.shape
    top = cells_x - STRIP
    other_rows = pl.ds(0, top)
    end_rows, next_rows = pl.ds(cells_x - 8, 8), pl.ds(top, STRIP - 8)

    def load(place, source, target):
        copy = pltpu.make_async_copy(source, target, in_sem.at[place])
        copy.start()
        return copy

    f_end_load = load(0, f_hbm.at[:, end_rows, :], fld.at[:, end_rows, :])
    k_end_load = load(3, k_hbm.at[:, end_rows, :], kap.at[:, end_rows, :])
    weights_load = load(2, tab_hbm.at[0:2], tab.at[0:2])
    f_high_load = load(1, f_hbm.at[:, next_rows, :], fld.at[:, next_rows, :])
    k_high_load = load(6, k_hbm.at[:, next_rows, :], kap.at[:, next_rows, :])
    table_rest = load(7, tab_hbm.at[2:12], tab.at[2:12])
    other_loads = [
        table_rest,
        load(4, f_hbm.at[:, other_rows, :], fld.at[:, other_rows, :]),
        load(5, k_hbm.at[:, other_rows, :], kap.at[:, other_rows, :]),
    ]
    table_load = load(8, mats_hbm, mats)

    ix, iy = lax.axis_index("gx"), lax.axis_index("gy")
    nx, ny = counts
    left = (jnp.where(ix == 0, nx - 1, ix - 1), iy)
    right = (jnp.where(ix == nx - 1, 0, ix + 1), iy)
    below = (ix, jnp.where(iy == 0, ny - 1, iy - 1))
    above = (ix, jnp.where(iy == ny - 1, 0, iy + 1))
    first_y, last_y, odd = iy == 0, iy == ny - 1, lax.rem(iy, 2) == 1
    later_y, even = jnp.logical_not(first_y), jnp.logical_not(odd)
    barrier = pltpu.get_barrier_semaphore()

    def tell(semaphore, neighbour, when=None):
        def signal():
            pl.semaphore_signal(semaphore, inc=1, device_id=neighbour, device_id_type=MESH)

        signal() if when is None else pl.when(when)(signal)

    tell(barrier, left)
    tell(barrier, below, odd | first_y)
    tell(barrier, above, odd & jnp.logical_not(last_y))
    heard = 1 + jnp.where(odd, jnp.where(last_y, 1, 0), jnp.where(first_y, 1, 2))

    def message(place, source, target, device):
        return pltpu.make_async_remote_copy(
            src_ref=source,
            dst_ref=target,
            send_sem=send_sem.at[place],
            recv_sem=recv_sem.at[place],
            device_id=device,
            device_id_type=MESH,
        )

    def send(*what):
        copy = message(*what)
        copy.start()
        return copy

    def sums(side, place, field, start, reach, weights):
        with_weights = twice(tab[weights, 0:reach])
        for p in range(planes):
            rows = field[p, start : start + reach, :]
            xs[side, place, p : p + 1, :] = jnp.sum(rows * with_weights, axis=0, keepdims=True)

    def take_edge(side, place, field, edge):
        for p in range(planes):
            xs[side, place, p : p + 1, :] = field[p, edge : edge + 1, :]

    def send_right(place):
        send(1, xs.at[1, place : place + 1], xr.at[0, place : place + 1], right)

    f_end_load.wait()
    take_edge(1, 0, fld, cells_x - 1)
    pl.semaphore_wait(barrier, heard)
    tell(left_ready, right)
    send_right(0)
    k_end_load.wait()
    take_edge(1, 1, kap, cells_x - 1)
    send_right(1)
    weights_load.wait()
    f_high_load.wait()
    sums(1, 2, fld, top, STRIP, 0)
    send_right(2)
    low_load = load(1, tab_hbm.at[12:16], low_tab)
    sums(1, 3, fld, cells_x - SHORT, SHORT, 1)
    send_right(3)
    k_high_load.wait()
    sums(1, 4, kap, top, STRIP, 0)
    send_right(4)
    to_right = message(1, xs.at[1], xr.at[0], right)
    tell(below_ready, above, even | last_y)
    tell(above_ready, below, even & later_y)
    for copy in other_loads:
        copy.wait()
    take_edge(0, 0, fld, 0)
    take_edge(0, 1, kap, 0)
    sums(0, 2, fld, 0, STRIP, 2)
    sums(0, 3, fld, 0, SHORT, 3)
    sums(0, 4, kap, 0, STRIP, 2)

    ys[:, :, 5:8, :] = jnp.zeros((2, planes, 3, 128), jnp.float32)
    lane = lax.broadcasted_iota(jnp.int32, (cells_x, 128), 1)
    for p in range(planes):
        f_low, f_high = fld[p, :, 0:128], fld[p, :, cells_y - 128 : cells_y]
        k_low, k_high = kap[p, :, 0:128], kap[p, :, cells_y - 128 : cells_y]
        packed = jnp.where(
            lane < REACH,
            f_low,
            jnp.where(
                lane < 2 * REACH,
                pltpu.roll(k_low, REACH, 1),
                jnp.where(lane < 3 * REACH, pltpu.roll(k_high, 128 - REACH, 1), f_high),
            ),
        )
        turned = packed.T
        for side, place, f_part, k_part, f_edge, k_edge in (
            (0, 6, turned[0:32], turned[32:64], turned[0:1], turned[32:33]),
            (1, 4, turned[96:128], turned[64:96], turned[127:128], turned[95:96]),
        ):
            with_first, with_second = tab[place], tab[place + 1]
            ys[side, p, 0:1, :] = jnp.sum(f_part * with_first, axis=0, keepdims=True)
            ys[side, p, 1:2, :] = jnp.sum(f_part * with_second, axis=0, keepdims=True)
            ys[side, p, 2:3, :] = f_edge
            ys[side, p, 3:4, :] = jnp.sum(k_part * with_first, axis=0, keepdims=True)
            ys[side, p, 4:5, :] = k_edge
    to_below = message(2, ys.at[0], yr.at[1], below)
    to_above = message(3, ys.at[1], yr.at[0], above)

    def send_below():
        pl.when(odd | first_y)(lambda: pl.semaphore_wait(below_ready, 1))
        to_below.start()

    pl.when(later_y)(send_below)
    pl.when(odd & jnp.logical_not(last_y))(lambda: pl.semaphore_wait(above_ready, 1))
    to_above.start()

    to_left = message(0, xs.at[0], xr.at[1], left)
    run_begins = lax.rem(ix, RUN) == 0

    def send_left():
        pl.semaphore_wait(left_ready, 1)
        to_left.start()

    pl.when(jnp.logical_not(run_begins))(send_left)

    table_load.wait()
    low_load.wait()
    x_rows = 4 * cells_x
    y_first = slice(x_rows, x_rows + 3 * cells_y)
    y_second = slice(x_rows + 3 * cells_y, x_rows + 6 * cells_y)
    ends_from = x_rows + 6 * cells_y

    def local_pair(pair, carry):
        tall, ktall = [], []
        for q in range(2):
            p = 2 * pair + q
            f, k = fld[p], kap[p]
            high, low = split(pltpu.roll(f, cells_x - 1, 0) - f)
            along = matmul(mats[0:x_rows, :], jnp.concatenate([high, low], axis=0))
            gx[p] = along[0:cells_x] + along[cells_x : 2 * cells_x]
            curv[p] = along[2 * cells_x : 3 * cells_x] + along[3 * cells_x : 4 * cells_x]
            high, low = split(pltpu.roll(k, cells_x - 1, 0) - k)
            along = matmul(mats[0 : 2 * cells_x, :], jnp.concatenate([high, low], axis=0))
            kx[p] = along[0:cells_x] + along[cells_x : 2 * cells_x]
            high, low = split(pltpu.roll(f, cells_y - 1, 1) - f)
            tall.append(jnp.concatenate([high, low, high], axis=1))
            high, low = split(pltpu.roll(k, cells_y - 1, 1) - k)
            ktall.append(jnp.concatenate([high, low, high], axis=1))
        across = matmul(jnp.concatenate(tall + ktall, axis=0), mats[y_first, :])
        bend = matmul(jnp.concatenate(tall, axis=0), mats[y_second, :])
        for q in range(2):
            p = 2 * pair + q
            gy[p] = across[q * cells_x : (q + 1) * cells_x]
            ky[p] = across[(q + 2) * cells_x : (q + 3) * cells_x]
            curv[p] = curv[p] + bend[q * cells_x : (q + 1) * cells_x]
        return carry

    lax.fori_loop(0, planes // 2 - 1, local_pair, 0)
    pl.when(first_y)(send_below)
    lax.fori_loop(planes // 2 - 1, planes // 2, local_pair, 0)

    to_below.wait_recv()
    to_above.wait_recv()
    row = lax.broadcasted_iota(jnp.int32, (8, 128), 0)
    is_edge = (row == 2) | (row == 4)

    def finish_pair(pair, carry):
        stacks = []
        for q in range(2):
            p = 2 * pair + q
            from_below, from_above = yr[0, p], yr[1, p]
            from_below = jnp.where(is_edge, ys[0, p] - from_below, from_below)
            from_above = jnp.where(is_edge, from_above - ys[1, p], from_above)
            ends = jnp.concatenate([from_below, from_above], axis=0)
            high = ends.astype(jnp.bfloat16).astype(jnp.float32)
            blank = jnp.zeros((FULL - 48, cells_x), jnp.float32)
            stacks.append(jnp.concatenate([high, ends - high, high, blank], axis=0).T)
        turned = jnp.concatenate(stacks, axis=0).astype(jnp.bfloat16)
        reach = [
            matmul(turned, mats[ends_from + n * FULL : ends_from + (n + 1) * FULL, :]) for n in range(3)
        ]
        for q in range(2):
            p = 2 * pair + q
            rows = slice(q * cells_x, (q + 1) * cells_x)
            grad = gy[p] + reach[0][rows]
            gy[p] = grad
            part = kap[p] * (curv[p] + reach[1][rows]) + (ky[p] + reach[2][rows]) * grad
            inner = slice(STRIP, top)
            dif[p, 0:STRIP, :] = part[0:STRIP]
            dif[p, inner, :] = part[inner] + kx[p, inner, :] * gx[p, inner, :]
            dif[p, top:, :] = part[top:]
        return carry

    lax.fori_loop(0, planes // 2, finish_pair, 0)
    pl.when(run_begins)(send_left)

    def combine(side, out):
        sign = 1.0 if side == 0 else -1.0
        jump = sign * (xs[side, 0] - xr[side, 0])
        kjump = sign * (xs[side, 1] - xr[side, 1])
        out[0] = FIRST.rho * xr[side, 2] + jump
        out[1] = SECOND.rho * xr[side, 3] + jump
        out[2] = jump
        out[3] = FIRST.rho * xr[side, 4] + kjump
        out[4] = kjump

    to_left.wait_recv()
    combine(1, xh)
    columns = [twice(tab[n, 0:STRIP]) for n in (8, 9)] + [twice(tab[n, 0:8]) for n in (10, 11)]
    for p in range(planes):
        gx[p, top:, :], dif[p, top:, :] = ends_applied(
            1,
            gx[p, top:, :],
            kx[p, top:, :],
            dif[p, top:, :],
            kap[p, top:, :],
            columns,
            [xh[n, p : p + 1, :] for n in range(5)],
        )
    for copy in (to_left, to_below, to_above, to_right):
        copy.wait_send()
    to_right.wait_recv()
    combine(0, xc)


def finish_kernel(gx, gy, dif, kx, kap, xc, tab, gx_out, gy_out, dif_out, gs, ds, sem):
    planes, cells_x, cells_y = gx.shape
    copies = []

    def store(source, target):
        copy = pltpu.make_async_copy(source, target, sem.at[len(copies)])
        copy.start()
        copies.append(copy)

    rest = pl.ds(STRIP, cells_x - STRIP)
    store(gy, gy_out)
    store(gx.at[:, rest, :], gx_out.at[:, rest, :])
    store(dif.at[:, rest, :], dif_out.at[:, rest, :])
    columns = [twice(tab[n, 0:STRIP]) for n in (0, 1)] + [twice(tab[n, 0:8]) for n in (2, 3)]
    for p in range(planes):
        gs[p], ds[p] = ends_applied(
            0,
            gx[p, 0:STRIP, :],
            kx[p, 0:STRIP, :],
            dif[p, 0:STRIP, :],
            kap[p, 0:STRIP, :],
            columns,
            [xc[n, p : p + 1, :] for n in range(5)],
        )
    store(gs, gx_out.at[:, pl.ds(0, STRIP), :])
    store(ds, dif_out.at[:, pl.ds(0, STRIP), :])
    for copy in copies:
        copy.wait()


def local(counts, scalar, diffusivity):
    block = scalar.shape
    planes, cells_x, cells_y = block
    columns = sum_columns(STRIP, SHORT) + sum_columns(REACH, REACH)
    columns += high_end_columns() + low_end_columns()
    tables = (
        jnp.asarray(stacked(columns)),
        jnp.asarray(
            np.concatenate([x_table(cells_x), y_table(cells_y), y_end_table(cells_y)], axis=0)
        ),
    )
    vmem, hbm = pl.BlockSpec(memory_space=pltpu.VMEM), pl.BlockSpec(memory_space=pltpu.HBM)
    field = jax.ShapeDtypeStruct(block, jnp.float32)
    field_buffer = pltpu.VMEM(block, jnp.float32)
    ends_shape = (5, planes, cells_y)
    operands = [
        pltpu.with_memory_space_constraint(array, pltpu.HBM)
        for array in (scalar, diffusivity) + tables
    ]
    parts = pl.pallas_call(
        functools.partial(exchange_kernel, counts),
        out_shape=(field,) * 5 + (jax.ShapeDtypeStruct(ends_shape, jnp.float32), jax.ShapeDtypeStruct((4, 32, 128), jnp.float32)),
        in_specs=[hbm] * 4,
        out_specs=(vmem,) * 7,
        scratch_shapes=[field_buffer]
        + [pltpu.VMEM(table.shape, table.dtype) for table in tables]
        + [field_buffer, field_buffer]
        + [pltpu.VMEM((2,) + ends_shape, jnp.float32)] * 2
        + [pltpu.VMEM((2, planes, 8, cells_x), jnp.float32)] * 2
        + [
            pltpu.VMEM(ends_shape, jnp.float32),
            pltpu.SemaphoreType.DMA((9,)),
            pltpu.SemaphoreType.DMA((4,)),
            pltpu.SemaphoreType.DMA((4,)),
            pltpu.SemaphoreType.REGULAR,
            pltpu.SemaphoreType.REGULAR,
            pltpu.SemaphoreType.REGULAR,
        ],
        compiler_params=pltpu.CompilerParams(
            collective_id=0, has_side_effects=True, vmem_limit_bytes=LIMIT
        ),
        name="exchange",
    )(*operands)
    strip_buffer = pltpu.VMEM((planes, STRIP, cells_y), jnp.float32)
    return pl.pallas_call(
        finish_kernel,
        out_shape=(field,) * 3,
        in_specs=[vmem] * 7,
        out_specs=(hbm,) * 3,
        scratch_shapes=[strip_buffer, strip_buffer, pltpu.SemaphoreType.DMA((5,))],
        compiler_params=pltpu.CompilerParams(vmem_limit_bytes=LIMIT),
        name="finish",
    )(*parts)


def solution(mesh):
    placed = P(None, "gx", "gy")
    return jax.shard_map(
        functools.partial(local, (mesh.shape["gx"], mesh.shape["gy"])),
        mesh=mesh,
        in_specs=(placed, placed),
        out_specs=(placed,) * 3,
        check_vma=False,
    )
```

```python
import functools

import jax
import jax.numpy as jnp
import numpy as np
from jax import lax
from jax.experimental import pallas as pl
from jax.experimental.pallas import tpu as pltpu
from jax.sharding import PartitionSpec as P

FIRST_ALPHA = 1.0 / 3.0
FIRST_A = 14.0 / 9.0
FIRST_B = 1.0 / 9.0
SECOND_ALPHA = 2.0 / 11.0
SECOND_A = 12.0 / 11.0
SECOND_B = 3.0 / 11.0
MESH = pl.DeviceIdType.MESH
LIMIT = 28 * 1024 * 1024
STRIP = 24
SHORT = 16
REACH = 32
FULL = 128
RUN = 8


class Line:
    def __init__(self, alpha, taps):
        root = np.sqrt(1.0 - 4.0 * alpha * alpha)
        self.rho = (root - 1.0) / (2.0 * alpha)
        self.root, self.taps = root, taps
        self.ahead = sum(c * self.rho**m for m, c in taps.items()) / root
        self.behind = sum(c * self.rho**-m for m, c in taps.items()) / root

    def weight(self, n):
        n = np.asarray(n)
        return sum(c * self.rho ** np.abs(n + m) for m, c in self.taps.items()) / self.root

    def local(self, cells):
        i = np.arange(cells)
        table = self.weight(i[:, None] - i[None, :])
        table[:, cells - 1] = 0.0
        return table

    def low_sum(self, reach):
        power = self.rho ** np.arange(reach - 1)
        weights = np.zeros(reach)
        weights[1:] += power
        weights[:-1] -= power
        return weights


FIRST = Line(
    FIRST_ALPHA,
    {
        1: 0.25 * FIRST_B,
        0: 0.5 * FIRST_A + 0.25 * FIRST_B,
        -1: 0.5 * FIRST_A + 0.25 * FIRST_B,
        -2: 0.25 * FIRST_B,
    },
)
SECOND = Line(
    SECOND_ALPHA,
    {
        1: 0.25 * SECOND_B,
        0: SECOND_A + 0.25 * SECOND_B,
        -1: -SECOND_A - 0.25 * SECOND_B,
        -2: -0.25 * SECOND_B,
    },
)


def halves(table):
    high = np.asarray(table, np.float32).astype(jnp.bfloat16)
    low = (table - high.astype(np.float64)).astype(np.float32).astype(jnp.bfloat16)
    return high, low


def stacked(columns):
    table = np.zeros((len(columns), 32, 128), np.float32)
    for place, column in enumerate(columns):
        table[place, : len(column)] = column[:, None]
    return table


def sum_columns(reach, short):
    low = [FIRST.low_sum(reach), SECOND.low_sum(short)]
    return [-row[::-1] for row in low] + low


def high_end_columns():
    r = np.arange(STRIP)[::-1]
    columns = [(line.behind * line.rho**r) for line in (FIRST, SECOND)]
    for line in (FIRST, SECOND):
        column = np.zeros(8)
        column[7] = line.weight(0) - line.behind
        columns.append(column)
    return columns


def low_end_columns():
    r = np.arange(STRIP)
    columns = [(line.ahead * line.rho ** (r + 1)) for line in (FIRST, SECOND)]
    for line in (FIRST, SECOND):
        column = np.zeros(8)
        column[0] = line.weight(1) - line.ahead * line.rho
        columns.append(column)
    return columns


def x_table(cells):
    rows = []
    for line in (FIRST, SECOND):
        for half in halves(line.local(cells)):
            rows.append(np.concatenate([half, half], axis=1))
    return np.concatenate(rows, axis=0)


def y_table(cells):
    rows = []
    for line in (FIRST, SECOND):
        high, low = halves(line.local(cells).T)
        rows += [high, high, low]
    return np.concatenate(rows, axis=0)


def y_end_table(cells):
    i = np.arange(cells)
    blocks = []
    for line, sum_row, edge_row in ((FIRST, 0, 2), (SECOND, 1, 2), (FIRST, 3, 4)):
        table = np.zeros((16, cells))
        table[sum_row] = line.ahead * line.rho ** (i + 2)
        table[edge_row] = line.weight(i + 1)
        table[8 + sum_row] = line.behind * line.rho ** (cells - i)
        table[8 + edge_row] = line.weight(i - cells + 1)
        high, low = halves(table)
        blank = np.zeros((FULL - 48, cells), high.dtype)
        blocks += [high, high, low, blank]
    return np.concatenate(blocks, axis=0)


def split(values):
    high = values.astype(jnp.bfloat16)
    low = (values - high.astype(jnp.float32)).astype(jnp.bfloat16)
    return high, low


def matmul(left, right):
    return jnp.dot(left, right, preferred_element_type=jnp.float32)


def twice(tile):
    return jnp.concatenate([tile, tile], axis=1)


def ends_applied(side, grad, kgrad, part, kappa, columns, values):
    decay, decay_second, end, end_second = columns
    first, second, jump, kfirst, kjump = values
    grads, parts = [], []
    for tile in range(STRIP // 8):
        r = slice(8 * tile, 8 * tile + 8)
        g = grad[r] + decay[r] * first
        k = kgrad[r] + decay[r] * kfirst
        distance = tile if side == 0 else STRIP // 8 - 1 - tile
        d = part[r]
        if distance < 2:
            bend = decay_second[r] * second
            if distance == 0:
                g = g + end * jump
                k = k + end * kjump
                bend = bend + end_second * jump
            d = d + kappa[r] * bend
        grads.append(g)
        parts.append(d + k * g)
    return jnp.concatenate(grads, axis=0), jnp.concatenate(parts, axis=0)


def exchange_kernel(
    counts,
    f_hbm,
    k_hbm,
    tab_hbm,
    mats_hbm,
    gx,
    gy,
    dif,
    kx,
    kap,
    xc,
    low_tab,
    fld,
    tab,
    mats,
    curv,
    ky,
    xs,
    xr,
    ys,
    yr,
    er,
    xh,
    in_sem,
    send_sem,
    recv_sem,
    left_ready,
    above_ready,
    below_ready,
):
    planes, cells_x, cells_y = fld.shape
    top = cells_x - STRIP
    other_rows = pl.ds(0, top)
    end_rows, next_rows = pl.ds(cells_x - 8, 8), pl.ds(top, STRIP - 8)

    def load(place, source, target):
        copy = pltpu.make_async_copy(source, target, in_sem.at[place])
        copy.start()
        return copy

    f_end_load = load(0, f_hbm.at[:, end_rows, :], fld.at[:, end_rows, :])
    k_end_load = load(3, k_hbm.at[:, end_rows, :], kap.at[:, end_rows, :])
    weights_load = load(2, tab_hbm.at[0:2], tab.at[0:2])
    f_high_load = load(1, f_hbm.at[:, next_rows, :], fld.at[:, next_rows, :])
    k_high_load = load(6, k_hbm.at[:, next_rows, :], kap.at[:, next_rows, :])
    table_rest = load(7, tab_hbm.at[2:12], tab.at[2:12])
    other_loads = [
        table_rest,
        load(4, f_hbm.at[:, other_rows, :], fld.at[:, other_rows, :]),
        load(5, k_hbm.at[:, other_rows, :], kap.at[:, other_rows, :]),
    ]
    table_load = load(8, mats_hbm, mats)

    ix, iy = lax.axis_index("gx"), lax.axis_index("gy")
    nx, ny = counts
    left = (jnp.where(ix == 0, nx - 1, ix - 1), iy)
    right = (jnp.where(ix == nx - 1, 0, ix + 1), iy)
    below = (ix, jnp.where(iy == 0, ny - 1, iy - 1))
    above = (ix, jnp.where(iy == ny - 1, 0, iy + 1))
    first_y, last_y, odd = iy == 0, iy == ny - 1, lax.rem(iy, 2) == 1
    later_y, even = jnp.logical_not(first_y), jnp.logical_not(odd)
    barrier = pltpu.get_barrier_semaphore()

    def tell(semaphore, neighbour, when=None):
        def signal():
            pl.semaphore_signal(semaphore, inc=1, device_id=neighbour, device_id_type=MESH)

        signal() if when is None else pl.when(when)(signal)

    tell(barrier, left)
    tell(barrier, below, odd | first_y)
    tell(barrier, above, odd & jnp.logical_not(last_y))
    heard = 1 + jnp.where(odd, jnp.where(last_y, 1, 0), jnp.where(first_y, 1, 2))

    def message(place, source, target, device):
        return pltpu.make_async_remote_copy(
            src_ref=source,
            dst_ref=target,
            send_sem=send_sem.at[place],
            recv_sem=recv_sem.at[place],
            device_id=device,
            device_id_type=MESH,
        )

    def send(*what):
        copy = message(*what)
        copy.start()
        return copy

    def sums(side, place, field, start, reach, weights):
        with_weights = twice(tab[weights, 0:reach])
        for p in range(planes):
            rows = field[p, start : start + reach, :]
            xs[side, place, p : p + 1, :] = jnp.sum(rows * with_weights, axis=0, keepdims=True)

    def take_edge(side, place, field, edge):
        for p in range(planes):
            xs[side, place, p : p + 1, :] = field[p, edge : edge + 1, :]

    def send_right(place):
        send(1, xs.at[1, place : place + 1], xr.at[0, place : place + 1], right)

    pl.semaphore_wait(barrier, heard)
    edge_row = pl.ds(cells_x - 1, 1)
    for place, field in enumerate((f_hbm, k_hbm)):
        send(4, field.at[:, edge_row, :], er.at[place, :, pl.ds(7, 1), :], right)
    tell(left_ready, right)
    weights_load.wait()
    f_end_load.wait()
    f_high_load.wait()
    sums(1, 2, fld, top, STRIP, 0)
    send_right(2)
    low_load = load(1, tab_hbm.at[12:16], low_tab)
    sums(1, 3, fld, cells_x - SHORT, SHORT, 1)
    send_right(3)
    k_end_load.wait()
    k_high_load.wait()
    sums(1, 4, kap, top, STRIP, 0)
    send_right(4)
    to_right = message(1, xs.at[1, 2:5], xr.at[0, 2:5], right)
    both_rows = er.at[:, :, pl.ds(7, 1), :]
    to_right_edges = message(4, both_rows, both_rows, right)
    take_edge(1, 0, fld, cells_x - 1)
    take_edge(1, 1, kap, cells_x - 1)
    tell(below_ready, above, even | last_y)
    tell(above_ready, below, even & later_y)
    for copy in other_loads:
        copy.wait()
    take_edge(0, 0, fld, 0)
    take_edge(0, 1, kap, 0)
    sums(0, 2, fld, 0, STRIP, 2)
    sums(0, 3, fld, 0, SHORT, 3)
    sums(0, 4, kap, 0, STRIP, 2)

    ys[:, :, 5:8, :] = jnp.zeros((2, planes, 3, 128), jnp.float32)
    lane = lax.broadcasted_iota(jnp.int32, (cells_x, 128), 1)
    for p in range(planes):
        f_low, f_high = fld[p, :, 0:128], fld[p, :, cells_y - 128 : cells_y]
        k_low, k_high = kap[p, :, 0:128], kap[p, :, cells_y - 128 : cells_y]
        packed = jnp.where(
            lane < REACH,
            f_low,
            jnp.where(
                lane < 2 * REACH,
                pltpu.roll(k_low, REACH, 1),
                jnp.where(lane < 3 * REACH, pltpu.roll(k_high, 128 - REACH, 1), f_high),
            ),
        )
        turned = packed.T
        for side, place, f_part, k_part, f_edge, k_edge in (
            (0, 6, turned[0:32], turned[32:64], turned[0:1], turned[32:33]),
            (1, 4, turned[96:128], turned[64:96], turned[127:128], turned[95:96]),
        ):
            with_first, with_second = tab[place], tab[place + 1]
            ys[side, p, 0:1, :] = jnp.sum(f_part * with_first, axis=0, keepdims=True)
            ys[side, p, 1:2, :] = jnp.sum(f_part * with_second, axis=0, keepdims=True)
            ys[side, p, 2:3, :] = f_edge
            ys[side, p, 3:4, :] = jnp.sum(k_part * with_first, axis=0, keepdims=True)
            ys[side, p, 4:5, :] = k_edge
    to_below = message(2, ys.at[0], yr.at[1], below)
    to_above = message(3, ys.at[1], yr.at[0], above)

    def send_below():
        pl.when(odd | first_y)(lambda: pl.semaphore_wait(below_ready, 1))
        to_below.start()

    pl.when(later_y)(send_below)
    pl.when(odd & jnp.logical_not(last_y))(lambda: pl.semaphore_wait(above_ready, 1))
    to_above.start()

    to_left = message(0, xs.at[0], xr.at[1], left)
    run_begins = lax.rem(ix, RUN) == 0

    def send_left():
        pl.semaphore_wait(left_ready, 1)
        to_left.start()

    pl.when(jnp.logical_not(run_begins))(send_left)

    table_load.wait()
    low_load.wait()
    x_rows = 4 * cells_x
    y_first = slice(x_rows, x_rows + 3 * cells_y)
    y_second = slice(x_rows + 3 * cells_y, x_rows + 6 * cells_y)
    ends_from = x_rows + 6 * cells_y

    def local_pair(pair, carry):
        tall, ktall = [], []
        for q in range(2):
            p = 2 * pair + q
            f, k = fld[p], kap[p]
            high, low = split(pltpu.roll(f, cells_x - 1, 0) - f)
            along = matmul(mats[0:x_rows, :], jnp.concatenate([high, low], axis=0))
            gx[p] = along[0:cells_x] + along[cells_x : 2 * cells_x]
            curv[p] = along[2 * cells_x : 3 * cells_x] + along[3 * cells_x : 4 * cells_x]
            high, low = split(pltpu.roll(k, cells_x - 1, 0) - k)
            along = matmul(mats[0 : 2 * cells_x, :], jnp.concatenate([high, low], axis=0))
            kx[p] = along[0:cells_x] + along[cells_x : 2 * cells_x]
            high, low = split(pltpu.roll(f, cells_y - 1, 1) - f)
            tall.append(jnp.concatenate([high, low, high], axis=1))
            high, low = split(pltpu.roll(k, cells_y - 1, 1) - k)
            ktall.append(jnp.concatenate([high, low, high], axis=1))
        across = matmul(jnp.concatenate(tall + ktall, axis=0), mats[y_first, :])
        bend = matmul(jnp.concatenate(tall, axis=0), mats[y_second, :])
        for q in range(2):
            p = 2 * pair + q
            gy[p] = across[q * cells_x : (q + 1) * cells_x]
            ky[p] = across[(q + 2) * cells_x : (q + 3) * cells_x]
            curv[p] = curv[p] + bend[q * cells_x : (q + 1) * cells_x]
        return carry

    lax.fori_loop(0, planes // 2 - 1, local_pair, 0)
    pl.when(first_y)(send_below)
    lax.fori_loop(planes // 2 - 1, planes // 2, local_pair, 0)

    to_below.wait_recv()
    to_above.wait_recv()
    row = lax.broadcasted_iota(jnp.int32, (8, 128), 0)
    is_edge = (row == 2) | (row == 4)

    def finish_pair(pair, carry):
        stacks = []
        for q in range(2):
            p = 2 * pair + q
            from_below, from_above = yr[0, p], yr[1, p]
            from_below = jnp.where(is_edge, ys[0, p] - from_below, from_below)
            from_above = jnp.where(is_edge, from_above - ys[1, p], from_above)
            ends = jnp.concatenate([from_below, from_above], axis=0)
            high = ends.astype(jnp.bfloat16).astype(jnp.float32)
            blank = jnp.zeros((FULL - 48, cells_x), jnp.float32)
            stacks.append(jnp.concatenate([high, ends - high, high, blank], axis=0).T)
        turned = jnp.concatenate(stacks, axis=0).astype(jnp.bfloat16)
        reach = [
            matmul(turned, mats[ends_from + n * FULL : ends_from + (n + 1) * FULL, :]) for n in range(3)
        ]
        for q in range(2):
            p = 2 * pair + q
            rows = slice(q * cells_x, (q + 1) * cells_x)
            grad = gy[p] + reach[0][rows]
            gy[p] = grad
            part = kap[p] * (curv[p] + reach[1][rows]) + (ky[p] + reach[2][rows]) * grad
            inner = slice(STRIP, top)
            dif[p, 0:STRIP, :] = part[0:STRIP]
            dif[p, inner, :] = part[inner] + kx[p, inner, :] * gx[p, inner, :]
            dif[p, top:, :] = part[top:]
        return carry

    lax.fori_loop(0, planes // 2, finish_pair, 0)
    pl.when(run_begins)(send_left)

    def combine(side, out):
        sign = 1.0 if side == 0 else -1.0
        came, kcame = (er[0, :, 7, :], er[1, :, 7, :]) if side == 0 else (xr[1, 0], xr[1, 1])
        jump = sign * (xs[side, 0] - came)
        kjump = sign * (xs[side, 1] - kcame)
        out[0] = FIRST.rho * xr[side, 2] + jump
        out[1] = SECOND.rho * xr[side, 3] + jump
        out[2] = jump
        out[3] = FIRST.rho * xr[side, 4] + kjump
        out[4] = kjump

    to_left.wait_recv()
    combine(1, xh)
    columns = [twice(tab[n, 0:STRIP]) for n in (8, 9)] + [twice(tab[n, 0:8]) for n in (10, 11)]
    for p in range(planes):
        gx[p, top:, :], dif[p, top:, :] = ends_applied(
            1,
            gx[p, top:, :],
            kx[p, top:, :],
            dif[p, top:, :],
            kap[p, top:, :],
            columns,
            [xh[n, p : p + 1, :] for n in range(5)],
        )
    for copy in (to_left, to_below, to_above, to_right, to_right_edges):
        copy.wait_send()
    to_right_edges.wait_recv()
    to_right.wait_recv()
    combine(0, xc)


def finish_kernel(gx, gy, dif, kx, kap, xc, tab, gx_out, gy_out, dif_out, gs, ds, sem):
    planes, cells_x, cells_y = gx.shape
    copies = []

    def store(source, target):
        copy = pltpu.make_async_copy(source, target, sem.at[len(copies)])
        copy.start()
        copies.append(copy)

    rest = pl.ds(STRIP, cells_x - STRIP)
    store(gy, gy_out)
    store(gx.at[:, rest, :], gx_out.at[:, rest, :])
    store(dif.at[:, rest, :], dif_out.at[:, rest, :])
    columns = [twice(tab[n, 0:STRIP]) for n in (0, 1)] + [twice(tab[n, 0:8]) for n in (2, 3)]
    for p in range(planes):
        gs[p], ds[p] = ends_applied(
            0,
            gx[p, 0:STRIP, :],
            kx[p, 0:STRIP, :],
            dif[p, 0:STRIP, :],
            kap[p, 0:STRIP, :],
            columns,
            [xc[n, p : p + 1, :] for n in range(5)],
        )
    store(gs, gx_out.at[:, pl.ds(0, STRIP), :])
    store(ds, dif_out.at[:, pl.ds(0, STRIP), :])
    for copy in copies:
        copy.wait()


def local(counts, scalar, diffusivity):
    block = scalar.shape
    planes, cells_x, cells_y = block
    columns = sum_columns(STRIP, SHORT) + sum_columns(REACH, REACH)
    columns += high_end_columns() + low_end_columns()
    tables = (
        jnp.asarray(stacked(columns)),
        jnp.asarray(
            np.concatenate([x_table(cells_x), y_table(cells_y), y_end_table(cells_y)], axis=0)
        ),
    )
    vmem, hbm = pl.BlockSpec(memory_space=pltpu.VMEM), pl.BlockSpec(memory_space=pltpu.HBM)
    field = jax.ShapeDtypeStruct(block, jnp.float32)
    field_buffer = pltpu.VMEM(block, jnp.float32)
    ends_shape = (5, planes, cells_y)
    operands = [
        pltpu.with_memory_space_constraint(array, pltpu.HBM)
        for array in (scalar, diffusivity) + tables
    ]
    parts = pl.pallas_call(
        functools.partial(exchange_kernel, counts),
        out_shape=(field,) * 5 + (jax.ShapeDtypeStruct(ends_shape, jnp.float32), jax.ShapeDtypeStruct((4, 32, 128), jnp.float32)),
        in_specs=[hbm] * 4,
        out_specs=(vmem,) * 7,
        scratch_shapes=[field_buffer]
        + [pltpu.VMEM(table.shape, table.dtype) for table in tables]
        + [field_buffer, field_buffer]
        + [pltpu.VMEM((2,) + ends_shape, jnp.float32)] * 2
        + [pltpu.VMEM((2, planes, 8, cells_x), jnp.float32)] * 2
        + [
            pltpu.VMEM((2, planes, 8, cells_y), jnp.float32),
            pltpu.VMEM(ends_shape, jnp.float32),
            pltpu.SemaphoreType.DMA((9,)),
            pltpu.SemaphoreType.DMA((5,)),
            pltpu.SemaphoreType.DMA((5,)),
            pltpu.SemaphoreType.REGULAR,
            pltpu.SemaphoreType.REGULAR,
            pltpu.SemaphoreType.REGULAR,
        ],
        compiler_params=pltpu.CompilerParams(
            collective_id=0, has_side_effects=True, vmem_limit_bytes=LIMIT
        ),
        name="exchange",
    )(*operands)
    strip_buffer = pltpu.VMEM((planes, STRIP, cells_y), jnp.float32)
    return pl.pallas_call(
        finish_kernel,
        out_shape=(field,) * 3,
        in_specs=[vmem] * 7,
        out_specs=(hbm,) * 3,
        scratch_shapes=[strip_buffer, strip_buffer, pltpu.SemaphoreType.DMA((5,))],
        compiler_params=pltpu.CompilerParams(vmem_limit_bytes=LIMIT),
        name="finish",
    )(*parts)


def solution(mesh):
    placed = P(None, "gx", "gy")
    return jax.shard_map(
        functools.partial(local, (mesh.shape["gx"], mesh.shape["gy"])),
        mesh=mesh,
        in_specs=(placed, placed),
        out_specs=(placed,) * 3,
        check_vma=False,
    )
```

```python
import functools

import jax
import jax.numpy as jnp
import numpy as np
from jax import lax
from jax.experimental import pallas as pl
from jax.experimental.pallas import tpu as pltpu
from jax.sharding import PartitionSpec as P

FIRST_ALPHA = 1.0 / 3.0
FIRST_A = 14.0 / 9.0
FIRST_B = 1.0 / 9.0
SECOND_ALPHA = 2.0 / 11.0
SECOND_A = 12.0 / 11.0
SECOND_B = 3.0 / 11.0
MESH = pl.DeviceIdType.MESH
LIMIT = 28 * 1024 * 1024
STRIP = 24
SHORT = 16
REACH = 32
FULL = 128
RUN = 8


class Line:
    def __init__(self, alpha, taps):
        root = np.sqrt(1.0 - 4.0 * alpha * alpha)
        self.rho = (root - 1.0) / (2.0 * alpha)
        self.root, self.taps = root, taps
        self.ahead = sum(c * self.rho**m for m, c in taps.items()) / root
        self.behind = sum(c * self.rho**-m for m, c in taps.items()) / root

    def weight(self, n):
        n = np.asarray(n)
        return sum(c * self.rho ** np.abs(n + m) for m, c in self.taps.items()) / self.root

    def local(self, cells):
        i = np.arange(cells)
        table = self.weight(i[:, None] - i[None, :])
        table[:, cells - 1] = 0.0
        return table

    def low_sum(self, reach):
        power = self.rho ** np.arange(reach - 1)
        weights = np.zeros(reach)
        weights[1:] += power
        weights[:-1] -= power
        return weights


FIRST = Line(
    FIRST_ALPHA,
    {
        1: 0.25 * FIRST_B,
        0: 0.5 * FIRST_A + 0.25 * FIRST_B,
        -1: 0.5 * FIRST_A + 0.25 * FIRST_B,
        -2: 0.25 * FIRST_B,
    },
)
SECOND = Line(
    SECOND_ALPHA,
    {
        1: 0.25 * SECOND_B,
        0: SECOND_A + 0.25 * SECOND_B,
        -1: -SECOND_A - 0.25 * SECOND_B,
        -2: -0.25 * SECOND_B,
    },
)


def halves(table):
    high = np.asarray(table, np.float32).astype(jnp.bfloat16)
    low = (table - high.astype(np.float64)).astype(np.float32).astype(jnp.bfloat16)
    return high, low


def stacked(columns):
    table = np.zeros((len(columns), 32, 128), np.float32)
    for place, column in enumerate(columns):
        table[place, : len(column)] = column[:, None]
    return table


def sum_columns(reach, short):
    low = [FIRST.low_sum(reach), SECOND.low_sum(short)]
    return [-row[::-1] for row in low] + low


def high_end_columns():
    r = np.arange(STRIP)[::-1]
    columns = [(line.behind * line.rho**r) for line in (FIRST, SECOND)]
    for line in (FIRST, SECOND):
        column = np.zeros(8)
        column[7] = line.weight(0) - line.behind
        columns.append(column)
    return columns


def low_end_columns():
    r = np.arange(STRIP)
    columns = [(line.ahead * line.rho ** (r + 1)) for line in (FIRST, SECOND)]
    for line in (FIRST, SECOND):
        column = np.zeros(8)
        column[0] = line.weight(1) - line.ahead * line.rho
        columns.append(column)
    return columns


def x_table(cells):
    rows = []
    for line in (FIRST, SECOND):
        for half in halves(line.local(cells)):
            rows.append(np.concatenate([half, half], axis=1))
    return np.concatenate(rows, axis=0)


def y_table(cells):
    rows = []
    for line in (FIRST, SECOND):
        high, low = halves(line.local(cells).T)
        rows += [high, high, low]
    return np.concatenate(rows, axis=0)


def y_end_table(cells):
    i = np.arange(cells)
    blocks = []
    for line, sum_row, edge_row in ((FIRST, 0, 2), (SECOND, 1, 2), (FIRST, 3, 4)):
        table = np.zeros((16, cells))
        table[sum_row] = line.ahead * line.rho ** (i + 2)
        table[edge_row] = line.weight(i + 1)
        table[8 + sum_row] = line.behind * line.rho ** (cells - i)
        table[8 + edge_row] = line.weight(i - cells + 1)
        high, low = halves(table)
        blank = np.zeros((FULL - 48, cells), high.dtype)
        blocks += [high, high, low, blank]
    return np.concatenate(blocks, axis=0)


def split(values):
    high = values.astype(jnp.bfloat16)
    low = (values - high.astype(jnp.float32)).astype(jnp.bfloat16)
    return high, low


def matmul(left, right):
    return jnp.dot(left, right, preferred_element_type=jnp.float32)


def twice(tile):
    return jnp.concatenate([tile, tile], axis=1)


def ends_applied(side, grad, kgrad, part, kappa, columns, values):
    decay, decay_second, end, end_second = columns
    first, second, jump, kfirst, kjump = values
    grads, parts = [], []
    for tile in range(STRIP // 8):
        r = slice(8 * tile, 8 * tile + 8)
        g = grad[r] + decay[r] * first
        k = kgrad[r] + decay[r] * kfirst
        distance = tile if side == 0 else STRIP // 8 - 1 - tile
        d = part[r]
        if distance < 2:
            bend = decay_second[r] * second
            if distance == 0:
                g = g + end * jump
                k = k + end * kjump
                bend = bend + end_second * jump
            d = d + kappa[r] * bend
        grads.append(g)
        parts.append(d + k * g)
    return jnp.concatenate(grads, axis=0), jnp.concatenate(parts, axis=0)


def exchange_kernel(
    counts,
    f_hbm,
    k_hbm,
    tab_hbm,
    mats_hbm,
    gx,
    gy,
    dif,
    kx,
    kap,
    xc,
    low_tab,
    fld,
    tab,
    mats,
    curv,
    ky,
    xs,
    xr,
    ys,
    yr,
    xh,
    in_sem,
    send_sem,
    recv_sem,
    left_ready,
    above_ready,
    below_ready,
):
    planes, cells_x, cells_y = fld.shape
    top = cells_x - STRIP
    other_rows = pl.ds(0, top)
    end_rows, next_rows = pl.ds(cells_x - 8, 8), pl.ds(top, STRIP - 8)

    def load(place, source, target, priority=0):
        copy = pltpu.make_async_copy(source, target, in_sem.at[place])
        copy.start(priority=priority)
        return copy

    f_end_load = load(0, f_hbm.at[:, end_rows, :], fld.at[:, end_rows, :], 1)
    k_end_load = load(3, k_hbm.at[:, end_rows, :], kap.at[:, end_rows, :], 1)
    weights_load = load(2, tab_hbm.at[0:2], tab.at[0:2], 1)
    f_high_load = load(1, f_hbm.at[:, next_rows, :], fld.at[:, next_rows, :], 1)
    k_high_load = load(6, k_hbm.at[:, next_rows, :], kap.at[:, next_rows, :], 1)
    table_rest = load(7, tab_hbm.at[2:12], tab.at[2:12])
    other_loads = [
        table_rest,
        load(4, f_hbm.at[:, other_rows, :], fld.at[:, other_rows, :]),
        load(5, k_hbm.at[:, other_rows, :], kap.at[:, other_rows, :]),
    ]
    table_load = load(8, mats_hbm, mats)

    ix, iy = lax.axis_index("gx"), lax.axis_index("gy")
    nx, ny = counts
    left = (jnp.where(ix == 0, nx - 1, ix - 1), iy)
    right = (jnp.where(ix == nx - 1, 0, ix + 1), iy)
    below = (ix, jnp.where(iy == 0, ny - 1, iy - 1))
    above = (ix, jnp.where(iy == ny - 1, 0, iy + 1))
    first_y, last_y, odd = iy == 0, iy == ny - 1, lax.rem(iy, 2) == 1
    later_y, even = jnp.logical_not(first_y), jnp.logical_not(odd)
    barrier = pltpu.get_barrier_semaphore()

    def tell(semaphore, neighbour, when=None):
        def signal():
            pl.semaphore_signal(semaphore, inc=1, device_id=neighbour, device_id_type=MESH)

        signal() if when is None else pl.when(when)(signal)

    tell(barrier, left)
    tell(barrier, below, odd | first_y)
    tell(barrier, above, odd & jnp.logical_not(last_y))
    heard = 1 + jnp.where(odd, jnp.where(last_y, 1, 0), jnp.where(first_y, 1, 2))

    def message(place, source, target, device):
        return pltpu.make_async_remote_copy(
            src_ref=source,
            dst_ref=target,
            send_sem=send_sem.at[place],
            recv_sem=recv_sem.at[place],
            device_id=device,
            device_id_type=MESH,
        )

    def send(*what):
        copy = message(*what)
        copy.start()
        return copy

    def sums(side, place, field, start, reach, weights):
        with_weights = twice(tab[weights, 0:reach])
        for p in range(planes):
            rows = field[p, start : start + reach, :]
            xs[side, place, p : p + 1, :] = jnp.sum(rows * with_weights, axis=0, keepdims=True)

    def take_edge(side, place, field, edge):
        for p in range(planes):
            xs[side, place, p : p + 1, :] = field[p, edge : edge + 1, :]

    def send_right(place):
        send(1, xs.at[1, place : place + 1], xr.at[0, place : place + 1], right)

    f_end_load.wait()
    take_edge(1, 0, fld, cells_x - 1)
    pl.semaphore_wait(barrier, heard)
    tell(left_ready, right)
    send_right(0)
    k_end_load.wait()
    take_edge(1, 1, kap, cells_x - 1)
    send_right(1)
    weights_load.wait()
    f_high_load.wait()
    sums(1, 2, fld, top, STRIP, 0)
    send_right(2)
    low_load = load(1, tab_hbm.at[12:16], low_tab)
    sums(1, 3, fld, cells_x - SHORT, SHORT, 1)
    send_right(3)
    k_high_load.wait()
    sums(1, 4, kap, top, STRIP, 0)
    send_right(4)
    to_right = message(1, xs.at[1], xr.at[0], right)
    tell(below_ready, above, even | last_y)
    tell(above_ready, below, even & later_y)
    for copy in other_loads:
        copy.wait()
    take_edge(0, 0, fld, 0)
    take_edge(0, 1, kap, 0)
    sums(0, 2, fld, 0, STRIP, 2)
    sums(0, 3, fld, 0, SHORT, 3)
    sums(0, 4, kap, 0, STRIP, 2)

    ys[:, :, 5:8, :] = jnp.zeros((2, planes, 3, 128), jnp.float32)
    lane = lax.broadcasted_iota(jnp.int32, (cells_x, 128), 1)
    for p in range(planes):
        f_low, f_high = fld[p, :, 0:128], fld[p, :, cells_y - 128 : cells_y]
        k_low, k_high = kap[p, :, 0:128], kap[p, :, cells_y - 128 : cells_y]
        packed = jnp.where(
            lane < REACH,
            f_low,
            jnp.where(
                lane < 2 * REACH,
                pltpu.roll(k_low, REACH, 1),
                jnp.where(lane < 3 * REACH, pltpu.roll(k_high, 128 - REACH, 1), f_high),
            ),
        )
        turned = packed.T
        for side, place, f_part, k_part, f_edge, k_edge in (
            (0, 6, turned[0:32], turned[32:64], turned[0:1], turned[32:33]),
            (1, 4, turned[96:128], turned[64:96], turned[127:128], turned[95:96]),
        ):
            with_first, with_second = tab[place], tab[place + 1]
            ys[side, p, 0:1, :] = jnp.sum(f_part * with_first, axis=0, keepdims=True)
            ys[side, p, 1:2, :] = jnp.sum(f_part * with_second, axis=0, keepdims=True)
            ys[side, p, 2:3, :] = f_edge
            ys[side, p, 3:4, :] = jnp.sum(k_part * with_first, axis=0, keepdims=True)
            ys[side, p, 4:5, :] = k_edge
    to_below = message(2, ys.at[0], yr.at[1], below)
    to_above = message(3, ys.at[1], yr.at[0], above)

    def send_below():
        pl.when(odd | first_y)(lambda: pl.semaphore_wait(below_ready, 1))
        to_below.start()

    pl.when(later_y)(send_below)
    pl.when(odd & jnp.logical_not(last_y))(lambda: pl.semaphore_wait(above_ready, 1))
    to_above.start()

    to_left = message(0, xs.at[0], xr.at[1], left)
    run_begins = lax.rem(ix, RUN) == 0

    def send_left():
        pl.semaphore_wait(left_ready, 1)
        to_left.start()

    pl.when(jnp.logical_not(run_begins))(send_left)

    table_load.wait()
    low_load.wait()
    x_rows = 4 * cells_x
    y_first = slice(x_rows, x_rows + 3 * cells_y)
    y_second = slice(x_rows + 3 * cells_y, x_rows + 6 * cells_y)
    ends_from = x_rows + 6 * cells_y

    def local_pair(pair, carry):
        tall, ktall = [], []
        for q in range(2):
            p = 2 * pair + q
            f, k = fld[p], kap[p]
            high, low = split(pltpu.roll(f, cells_x - 1, 0) - f)
            along = matmul(mats[0:x_rows, :], jnp.concatenate([high, low], axis=0))
            gx[p] = along[0:cells_x] + along[cells_x : 2 * cells_x]
            curv[p] = along[2 * cells_x : 3 * cells_x] + along[3 * cells_x : 4 * cells_x]
            high, low = split(pltpu.roll(k, cells_x - 1, 0) - k)
            along = matmul(mats[0 : 2 * cells_x, :], jnp.concatenate([high, low], axis=0))
            kx[p] = along[0:cells_x] + along[cells_x : 2 * cells_x]
            high, low = split(pltpu.roll(f, cells_y - 1, 1) - f)
            tall.append(jnp.concatenate([high, low, high], axis=1))
            high, low = split(pltpu.roll(k, cells_y - 1, 1) - k)
            ktall.append(jnp.concatenate([high, low, high], axis=1))
        across = matmul(jnp.concatenate(tall + ktall, axis=0), mats[y_first, :])
        bend = matmul(jnp.concatenate(tall, axis=0), mats[y_second, :])
        for q in range(2):
            p = 2 * pair + q
            gy[p] = across[q * cells_x : (q + 1) * cells_x]
            ky[p] = across[(q + 2) * cells_x : (q + 3) * cells_x]
            curv[p] = curv[p] + bend[q * cells_x : (q + 1) * cells_x]
        return carry

    lax.fori_loop(0, planes // 2 - 1, local_pair, 0)
    pl.when(first_y)(send_below)
    lax.fori_loop(planes // 2 - 1, planes // 2, local_pair, 0)

    to_below.wait_recv()
    to_above.wait_recv()
    row = lax.broadcasted_iota(jnp.int32, (8, 128), 0)
    is_edge = (row == 2) | (row == 4)

    def finish_pair(pair, carry):
        stacks = []
        for q in range(2):
            p = 2 * pair + q
            from_below, from_above = yr[0, p], yr[1, p]
            from_below = jnp.where(is_edge, ys[0, p] - from_below, from_below)
            from_above = jnp.where(is_edge, from_above - ys[1, p], from_above)
            ends = jnp.concatenate([from_below, from_above], axis=0)
            high = ends.astype(jnp.bfloat16).astype(jnp.float32)
            blank = jnp.zeros((FULL - 48, cells_x), jnp.float32)
            stacks.append(jnp.concatenate([high, ends - high, high, blank], axis=0).T)
        turned = jnp.concatenate(stacks, axis=0).astype(jnp.bfloat16)
        reach = [
            matmul(turned, mats[ends_from + n * FULL : ends_from + (n + 1) * FULL, :]) for n in range(3)
        ]
        for q in range(2):
            p = 2 * pair + q
            rows = slice(q * cells_x, (q + 1) * cells_x)
            grad = gy[p] + reach[0][rows]
            gy[p] = grad
            part = kap[p] * (curv[p] + reach[1][rows]) + (ky[p] + reach[2][rows]) * grad
            inner = slice(STRIP, top)
            dif[p, 0:STRIP, :] = part[0:STRIP]
            dif[p, inner, :] = part[inner] + kx[p, inner, :] * gx[p, inner, :]
            dif[p, top:, :] = part[top:]
        return carry

    lax.fori_loop(0, planes // 2, finish_pair, 0)
    pl.when(run_begins)(send_left)

    def combine(side, out):
        sign = 1.0 if side == 0 else -1.0
        jump = sign * (xs[side, 0] - xr[side, 0])
        kjump = sign * (xs[side, 1] - xr[side, 1])
        out[0] = FIRST.rho * xr[side, 2] + jump
        out[1] = SECOND.rho * xr[side, 3] + jump
        out[2] = jump
        out[3] = FIRST.rho * xr[side, 4] + kjump
        out[4] = kjump

    to_left.wait_recv()
    combine(1, xh)
    columns = [twice(tab[n, 0:STRIP]) for n in (8, 9)] + [twice(tab[n, 0:8]) for n in (10, 11)]
    for p in range(planes):
        gx[p, top:, :], dif[p, top:, :] = ends_applied(
            1,
            gx[p, top:, :],
            kx[p, top:, :],
            dif[p, top:, :],
            kap[p, top:, :],
            columns,
            [xh[n, p : p + 1, :] for n in range(5)],
        )
    for copy in (to_left, to_below, to_above, to_right):
        copy.wait_send()
    to_right.wait_recv()
    combine(0, xc)


def finish_kernel(gx, gy, dif, kx, kap, xc, tab, gx_out, gy_out, dif_out, gs, ds, sem):
    planes, cells_x, cells_y = gx.shape
    copies = []

    def store(source, target):
        copy = pltpu.make_async_copy(source, target, sem.at[len(copies)])
        copy.start()
        copies.append(copy)

    rest = pl.ds(STRIP, cells_x - STRIP)
    store(gy, gy_out)
    store(gx.at[:, rest, :], gx_out.at[:, rest, :])
    store(dif.at[:, rest, :], dif_out.at[:, rest, :])
    columns = [twice(tab[n, 0:STRIP]) for n in (0, 1)] + [twice(tab[n, 0:8]) for n in (2, 3)]
    for p in range(planes):
        gs[p], ds[p] = ends_applied(
            0,
            gx[p, 0:STRIP, :],
            kx[p, 0:STRIP, :],
            dif[p, 0:STRIP, :],
            kap[p, 0:STRIP, :],
            columns,
            [xc[n, p : p + 1, :] for n in range(5)],
        )
    store(gs, gx_out.at[:, pl.ds(0, STRIP), :])
    store(ds, dif_out.at[:, pl.ds(0, STRIP), :])
    for copy in copies:
        copy.wait()


def local(counts, scalar, diffusivity):
    block = scalar.shape
    planes, cells_x, cells_y = block
    columns = sum_columns(STRIP, SHORT) + sum_columns(REACH, REACH)
    columns += high_end_columns() + low_end_columns()
    tables = (
        jnp.asarray(stacked(columns)),
        jnp.asarray(
            np.concatenate([x_table(cells_x), y_table(cells_y), y_end_table(cells_y)], axis=0)
        ),
    )
    vmem, hbm = pl.BlockSpec(memory_space=pltpu.VMEM), pl.BlockSpec(memory_space=pltpu.HBM)
    field = jax.ShapeDtypeStruct(block, jnp.float32)
    field_buffer = pltpu.VMEM(block, jnp.float32)
    ends_shape = (5, planes, cells_y)
    operands = [
        pltpu.with_memory_space_constraint(array, pltpu.HBM)
        for array in (scalar, diffusivity) + tables
    ]
    parts = pl.pallas_call(
        functools.partial(exchange_kernel, counts),
        out_shape=(field,) * 5 + (jax.ShapeDtypeStruct(ends_shape, jnp.float32), jax.ShapeDtypeStruct((4, 32, 128), jnp.float32)),
        in_specs=[hbm] * 4,
        out_specs=(vmem,) * 7,
        scratch_shapes=[field_buffer]
        + [pltpu.VMEM(table.shape, table.dtype) for table in tables]
        + [field_buffer, field_buffer]
        + [pltpu.VMEM((2,) + ends_shape, jnp.float32)] * 2
        + [pltpu.VMEM((2, planes, 8, cells_x), jnp.float32)] * 2
        + [
            pltpu.VMEM(ends_shape, jnp.float32),
            pltpu.SemaphoreType.DMA((9,)),
            pltpu.SemaphoreType.DMA((4,)),
            pltpu.SemaphoreType.DMA((4,)),
            pltpu.SemaphoreType.REGULAR,
            pltpu.SemaphoreType.REGULAR,
            pltpu.SemaphoreType.REGULAR,
        ],
        compiler_params=pltpu.CompilerParams(
            collective_id=0, has_side_effects=True, vmem_limit_bytes=LIMIT
        ),
        name="exchange",
    )(*operands)
    strip_buffer = pltpu.VMEM((planes, STRIP, cells_y), jnp.float32)
    return pl.pallas_call(
        finish_kernel,
        out_shape=(field,) * 3,
        in_specs=[vmem] * 7,
        out_specs=(hbm,) * 3,
        scratch_shapes=[strip_buffer, strip_buffer, pltpu.SemaphoreType.DMA((5,))],
        compiler_params=pltpu.CompilerParams(vmem_limit_bytes=LIMIT),
        name="finish",
    )(*parts)


def solution(mesh):
    placed = P(None, "gx", "gy")
    return jax.shard_map(
        functools.partial(local, (mesh.shape["gx"], mesh.shape["gy"])),
        mesh=mesh,
        in_specs=(placed, placed),
        out_specs=(placed,) * 3,
        check_vma=False,
    )
```

```python
import functools

import jax
import jax.numpy as jnp
import numpy as np
from jax import lax
from jax.experimental import pallas as pl
from jax.experimental.pallas import tpu as pltpu
from jax.sharding import PartitionSpec as P

FIRST_ALPHA = 1.0 / 3.0
FIRST_A = 14.0 / 9.0
FIRST_B = 1.0 / 9.0
SECOND_ALPHA = 2.0 / 11.0
SECOND_A = 12.0 / 11.0
SECOND_B = 3.0 / 11.0
MESH = pl.DeviceIdType.MESH
LIMIT = 28 * 1024 * 1024
STRIP = 24
SHORT = 16
REACH = 32
FULL = 128
RUN = 8


class Line:
    def __init__(self, alpha, taps):
        root = np.sqrt(1.0 - 4.0 * alpha * alpha)
        self.rho = (root - 1.0) / (2.0 * alpha)
        self.root, self.taps = root, taps
        self.ahead = sum(c * self.rho**m for m, c in taps.items()) / root
        self.behind = sum(c * self.rho**-m for m, c in taps.items()) / root

    def weight(self, n):
        n = np.asarray(n)
        return sum(c * self.rho ** np.abs(n + m) for m, c in self.taps.items()) / self.root

    def local(self, cells):
        i = np.arange(cells)
        table = self.weight(i[:, None] - i[None, :])
        table[:, cells - 1] = 0.0
        return table

    def low_sum(self, reach):
        power = self.rho ** np.arange(reach - 1)
        weights = np.zeros(reach)
        weights[1:] += power
        weights[:-1] -= power
        return weights


FIRST = Line(
    FIRST_ALPHA,
    {
        1: 0.25 * FIRST_B,
        0: 0.5 * FIRST_A + 0.25 * FIRST_B,
        -1: 0.5 * FIRST_A + 0.25 * FIRST_B,
        -2: 0.25 * FIRST_B,
    },
)
SECOND = Line(
    SECOND_ALPHA,
    {
        1: 0.25 * SECOND_B,
        0: SECOND_A + 0.25 * SECOND_B,
        -1: -SECOND_A - 0.25 * SECOND_B,
        -2: -0.25 * SECOND_B,
    },
)


def halves(table):
    high = np.asarray(table, np.float32).astype(jnp.bfloat16)
    low = (table - high.astype(np.float64)).astype(np.float32).astype(jnp.bfloat16)
    return high, low


def stacked(columns):
    table = np.zeros((len(columns), 32, 128), np.float32)
    for place, column in enumerate(columns):
        table[place, : len(column)] = column[:, None]
    return table


def sum_columns(reach, short):
    low = [FIRST.low_sum(reach), SECOND.low_sum(short)]
    return [-row[::-1] for row in low] + low


def high_end_columns():
    r = np.arange(STRIP)[::-1]
    columns = [(line.behind * line.rho**r) for line in (FIRST, SECOND)]
    for line in (FIRST, SECOND):
        column = np.zeros(8)
        column[7] = line.weight(0) - line.behind
        columns.append(column)
    return columns


def low_end_columns():
    r = np.arange(STRIP)
    columns = [(line.ahead * line.rho ** (r + 1)) for line in (FIRST, SECOND)]
    for line in (FIRST, SECOND):
        column = np.zeros(8)
        column[0] = line.weight(1) - line.ahead * line.rho
        columns.append(column)
    return columns


def x_table(cells):
    rows = []
    for line in (FIRST, SECOND):
        for half in halves(line.local(cells)):
            rows.append(np.concatenate([half, half], axis=1))
    return np.concatenate(rows, axis=0)


def y_table(cells):
    rows = []
    for line in (FIRST, SECOND):
        high, low = halves(line.local(cells).T)
        rows += [high, high, low]
    return np.concatenate(rows, axis=0)


def y_end_table(cells):
    i = np.arange(cells)
    blocks = []
    for line, sum_row, edge_row in ((FIRST, 0, 2), (SECOND, 1, 2), (FIRST, 3, 4)):
        table = np.zeros((16, cells))
        table[sum_row] = line.ahead * line.rho ** (i + 2)
        table[edge_row] = line.weight(i + 1)
        table[8 + sum_row] = line.behind * line.rho ** (cells - i)
        table[8 + edge_row] = line.weight(i - cells + 1)
        high, low = halves(table)
        blank = np.zeros((FULL - 48, cells), high.dtype)
        blocks += [high, high, low, blank]
    return np.concatenate(blocks, axis=0)


def split(values):
    high = values.astype(jnp.bfloat16)
    low = (values - high.astype(jnp.float32)).astype(jnp.bfloat16)
    return high, low


def matmul(left, right):
    return jnp.dot(left, right, preferred_element_type=jnp.float32)


def twice(tile):
    return jnp.concatenate([tile, tile], axis=1)


def ends_applied(side, grad, kgrad, part, kappa, columns, values):
    decay, decay_second, end, end_second = columns
    first, second, jump, kfirst, kjump = values
    grads, parts = [], []
    for tile in range(STRIP // 8):
        r = slice(8 * tile, 8 * tile + 8)
        g = grad[r] + decay[r] * first
        k = kgrad[r] + decay[r] * kfirst
        distance = tile if side == 0 else STRIP // 8 - 1 - tile
        d = part[r]
        if distance < 2:
            bend = decay_second[r] * second
            if distance == 0:
                g = g + end * jump
                k = k + end * kjump
                bend = bend + end_second * jump
            d = d + kappa[r] * bend
        grads.append(g)
        parts.append(d + k * g)
    return jnp.concatenate(grads, axis=0), jnp.concatenate(parts, axis=0)


def exchange_kernel(
    counts,
    f_hbm,
    k_hbm,
    tab_hbm,
    mats_hbm,
    gx,
    gy,
    dif,
    kx,
    kap,
    xc,
    low_tab,
    fld,
    tab,
    mats,
    curv,
    ky,
    xs,
    xr,
    ys,
    yr,
    xh,
    in_sem,
    send_sem,
    recv_sem,
    left_ready,
    above_ready,
    below_ready,
):
    planes, cells_x, cells_y = fld.shape
    top = cells_x - STRIP
    other_rows = pl.ds(0, top)
    end_rows, next_rows = pl.ds(cells_x - 8, 8), pl.ds(top, STRIP - 8)

    def load(place, source, target):
        copy = pltpu.make_async_copy(source, target, in_sem.at[place])
        copy.start()
        return copy

    f_end_load = load(0, f_hbm.at[:, end_rows, :], fld.at[:, end_rows, :])
    k_end_load = load(3, k_hbm.at[:, end_rows, :], kap.at[:, end_rows, :])
    weights_load = load(2, tab_hbm.at[0:2], tab.at[0:2])
    f_high_load = load(1, f_hbm.at[:, next_rows, :], fld.at[:, next_rows, :])
    k_high_load = load(6, k_hbm.at[:, next_rows, :], kap.at[:, next_rows, :])
    table_rest = load(7, tab_hbm.at[2:12], tab.at[2:12])
    other_loads = [
        table_rest,
        load(4, f_hbm.at[:, other_rows, :], fld.at[:, other_rows, :]),
        load(5, k_hbm.at[:, other_rows, :], kap.at[:, other_rows, :]),
    ]
    table_load = load(8, mats_hbm, mats)

    ix, iy = lax.axis_index("gx"), lax.axis_index("gy")
    nx, ny = counts
    left = (jnp.where(ix == 0, nx - 1, ix - 1), iy)
    right = (jnp.where(ix == nx - 1, 0, ix + 1), iy)
    below = (ix, jnp.where(iy == 0, ny - 1, iy - 1))
    above = (ix, jnp.where(iy == ny - 1, 0, iy + 1))
    first_y, last_y, odd = iy == 0, iy == ny - 1, lax.rem(iy, 2) == 1
    later_y, even = jnp.logical_not(first_y), jnp.logical_not(odd)
    barrier = pltpu.get_barrier_semaphore()

    def tell(semaphore, neighbour, when=None):
        def signal():
            pl.semaphore_signal(semaphore, inc=1, device_id=neighbour, device_id_type=MESH)

        signal() if when is None else pl.when(when)(signal)

    tell(barrier, left)
    tell(barrier, below, odd | first_y)
    tell(barrier, above, odd & jnp.logical_not(last_y))
    heard = 1 + jnp.where(odd, jnp.where(last_y, 1, 0), jnp.where(first_y, 1, 2))

    def message(place, source, target, device):
        return pltpu.make_async_remote_copy(
            src_ref=source,
            dst_ref=target,
            send_sem=send_sem.at[place],
            recv_sem=recv_sem.at[place],
            device_id=device,
            device_id_type=MESH,
        )

    def send(*what):
        copy = message(*what)
        copy.start()
        return copy

    def sums(side, place, field, start, reach, weights):
        with_weights = twice(tab[weights, 0:reach])
        for p in range(planes):
            rows = field[p, start : start + reach, :]
            xs[side, place, p : p + 1, :] = jnp.sum(rows * with_weights, axis=0, keepdims=True)

    def take_edge(side, place, field, edge):
        for p in range(planes):
            xs[side, place, p : p + 1, :] = field[p, edge : edge + 1, :]

    def send_right(place):
        send(1, xs.at[1, place : place + 1], xr.at[0, place : place + 1], right)

    f_end_load.wait()
    take_edge(1, 0, fld, cells_x - 1)
    pl.semaphore_wait(barrier, heard)
    send_right(0)
    tell(left_ready, right)
    k_end_load.wait()
    take_edge(1, 1, kap, cells_x - 1)
    send_right(1)
    weights_load.wait()
    f_high_load.wait()
    sums(1, 2, fld, top, STRIP, 0)
    send_right(2)
    low_load = load(1, tab_hbm.at[12:16], low_tab)
    sums(1, 3, fld, cells_x - SHORT, SHORT, 1)
    send_right(3)
    k_high_load.wait()
    sums(1, 4, kap, top, STRIP, 0)
    send_right(4)
    to_right = message(1, xs.at[1], xr.at[0], right)
    tell(below_ready, above, even | last_y)
    tell(above_ready, below, even & later_y)
    for copy in other_loads:
        copy.wait()
    take_edge(0, 0, fld, 0)
    take_edge(0, 1, kap, 0)
    sums(0, 2, fld, 0, STRIP, 2)
    sums(0, 3, fld, 0, SHORT, 3)
    sums(0, 4, kap, 0, STRIP, 2)

    ys[:, :, 5:8, :] = jnp.zeros((2, planes, 3, 128), jnp.float32)
    lane = lax.broadcasted_iota(jnp.int32, (cells_x, 128), 1)
    for p in range(planes):
        f_low, f_high = fld[p, :, 0:128], fld[p, :, cells_y - 128 : cells_y]
        k_low, k_high = kap[p, :, 0:128], kap[p, :, cells_y - 128 : cells_y]
        packed = jnp.where(
            lane < REACH,
            f_low,
            jnp.where(
                lane < 2 * REACH,
                pltpu.roll(k_low, REACH, 1),
                jnp.where(lane < 3 * REACH, pltpu.roll(k_high, 128 - REACH, 1), f_high),
            ),
        )
        turned = packed.T
        for side, place, f_part, k_part, f_edge, k_edge in (
            (0, 6, turned[0:32], turned[32:64], turned[0:1], turned[32:33]),
            (1, 4, turned[96:128], turned[64:96], turned[127:128], turned[95:96]),
        ):
            with_first, with_second = tab[place], tab[place + 1]
            ys[side, p, 0:1, :] = jnp.sum(f_part * with_first, axis=0, keepdims=True)
            ys[side, p, 1:2, :] = jnp.sum(f_part * with_second, axis=0, keepdims=True)
            ys[side, p, 2:3, :] = f_edge
            ys[side, p, 3:4, :] = jnp.sum(k_part * with_first, axis=0, keepdims=True)
            ys[side, p, 4:5, :] = k_edge
    to_below = message(2, ys.at[0], yr.at[1], below)
    to_above = message(3, ys.at[1], yr.at[0], above)

    def send_below():
        pl.when(odd | first_y)(lambda: pl.semaphore_wait(below_ready, 1))
        to_below.start()

    pl.when(later_y)(send_below)
    pl.when(odd & jnp.logical_not(last_y))(lambda: pl.semaphore_wait(above_ready, 1))
    to_above.start()

    to_left = message(0, xs.at[0], xr.at[1], left)
    run_begins = lax.rem(ix, RUN) == 0

    def send_left():
        pl.semaphore_wait(left_ready, 1)
        to_left.start()

    pl.when(jnp.logical_not(run_begins))(send_left)

    table_load.wait()
    low_load.wait()
    x_rows = 4 * cells_x
    y_first = slice(x_rows, x_rows + 3 * cells_y)
    y_second = slice(x_rows + 3 * cells_y, x_rows + 6 * cells_y)
    ends_from = x_rows + 6 * cells_y

    def local_pair(pair, carry):
        tall, ktall = [], []
        for q in range(2):
            p = 2 * pair + q
            f, k = fld[p], kap[p]
            high, low = split(pltpu.roll(f, cells_x - 1, 0) - f)
            along = matmul(mats[0:x_rows, :], jnp.concatenate([high, low], axis=0))
            gx[p] = along[0:cells_x] + along[cells_x : 2 * cells_x]
            curv[p] = along[2 * cells_x : 3 * cells_x] + along[3 * cells_x : 4 * cells_x]
            high, low = split(pltpu.roll(k, cells_x - 1, 0) - k)
            along = matmul(mats[0 : 2 * cells_x, :], jnp.concatenate([high, low], axis=0))
            kx[p] = along[0:cells_x] + along[cells_x : 2 * cells_x]
            high, low = split(pltpu.roll(f, cells_y - 1, 1) - f)
            tall.append(jnp.concatenate([high, low, high], axis=1))
            high, low = split(pltpu.roll(k, cells_y - 1, 1) - k)
            ktall.append(jnp.concatenate([high, low, high], axis=1))
        across = matmul(jnp.concatenate(tall + ktall, axis=0), mats[y_first, :])
        bend = matmul(jnp.concatenate(tall, axis=0), mats[y_second, :])
        for q in range(2):
            p = 2 * pair + q
            gy[p] = across[q * cells_x : (q + 1) * cells_x]
            ky[p] = across[(q + 2) * cells_x : (q + 3) * cells_x]
            curv[p] = curv[p] + bend[q * cells_x : (q + 1) * cells_x]
        return carry

    lax.fori_loop(0, planes // 2 - 1, local_pair, 0)
    pl.when(first_y)(send_below)
    lax.fori_loop(planes // 2 - 1, planes // 2, local_pair, 0)

    to_below.wait_recv()
    to_above.wait_recv()
    row = lax.broadcasted_iota(jnp.int32, (8, 128), 0)
    is_edge = (row == 2) | (row == 4)

    def finish_pair(pair, carry):
        stacks = []
        for q in range(2):
            p = 2 * pair + q
            from_below, from_above = yr[0, p], yr[1, p]
            from_below = jnp.where(is_edge, ys[0, p] - from_below, from_below)
            from_above = jnp.where(is_edge, from_above - ys[1, p], from_above)
            ends = jnp.concatenate([from_below, from_above], axis=0)
            high = ends.astype(jnp.bfloat16).astype(jnp.float32)
            blank = jnp.zeros((FULL - 48, cells_x), jnp.float32)
            stacks.append(jnp.concatenate([high, ends - high, high, blank], axis=0).T)
        turned = jnp.concatenate(stacks, axis=0).astype(jnp.bfloat16)
        reach = [
            matmul(turned, mats[ends_from + n * FULL : ends_from + (n + 1) * FULL, :]) for n in range(3)
        ]
        for q in range(2):
            p = 2 * pair + q
            rows = slice(q * cells_x, (q + 1) * cells_x)
            grad = gy[p] + reach[0][rows]
            gy[p] = grad
            part = kap[p] * (curv[p] + reach[1][rows]) + (ky[p] + reach[2][rows]) * grad
            inner = slice(STRIP, top)
            dif[p, 0:STRIP, :] = part[0:STRIP]
            dif[p, inner, :] = part[inner] + kx[p, inner, :] * gx[p, inner, :]
            dif[p, top:, :] = part[top:]
        return carry

    lax.fori_loop(0, planes // 2, finish_pair, 0)
    pl.when(run_begins)(send_left)

    def combine(side, out):
        sign = 1.0 if side == 0 else -1.0
        jump = sign * (xs[side, 0] - xr[side, 0])
        kjump = sign * (xs[side, 1] - xr[side, 1])
        out[0] = FIRST.rho * xr[side, 2] + jump
        out[1] = SECOND.rho * xr[side, 3] + jump
        out[2] = jump
        out[3] = FIRST.rho * xr[side, 4] + kjump
        out[4] = kjump

    to_left.wait_recv()
    combine(1, xh)
    columns = [twice(tab[n, 0:STRIP]) for n in (8, 9)] + [twice(tab[n, 0:8]) for n in (10, 11)]
    for p in range(planes):
        gx[p, top:, :], dif[p, top:, :] = ends_applied(
            1,
            gx[p, top:, :],
            kx[p, top:, :],
            dif[p, top:, :],
            kap[p, top:, :],
            columns,
            [xh[n, p : p + 1, :] for n in range(5)],
        )
    for copy in (to_left, to_below, to_above, to_right):
        copy.wait_send()
    to_right.wait_recv()
    combine(0, xc)


def finish_kernel(gx, gy, dif, kx, kap, xc, tab, gx_out, gy_out, dif_out, gs, ds, sem):
    planes, cells_x, cells_y = gx.shape
    copies = []

    def store(source, target):
        copy = pltpu.make_async_copy(source, target, sem.at[len(copies)])
        copy.start()
        copies.append(copy)

    rest = pl.ds(STRIP, cells_x - STRIP)
    store(gy, gy_out)
    store(gx.at[:, rest, :], gx_out.at[:, rest, :])
    store(dif.at[:, rest, :], dif_out.at[:, rest, :])
    columns = [twice(tab[n, 0:STRIP]) for n in (0, 1)] + [twice(tab[n, 0:8]) for n in (2, 3)]
    for p in range(planes):
        gs[p], ds[p] = ends_applied(
            0,
            gx[p, 0:STRIP, :],
            kx[p, 0:STRIP, :],
            dif[p, 0:STRIP, :],
            kap[p, 0:STRIP, :],
            columns,
            [xc[n, p : p + 1, :] for n in range(5)],
        )
    store(gs, gx_out.at[:, pl.ds(0, STRIP), :])
    store(ds, dif_out.at[:, pl.ds(0, STRIP), :])
    for copy in copies:
        copy.wait()


def local(counts, scalar, diffusivity):
    block = scalar.shape
    planes, cells_x, cells_y = block
    columns = sum_columns(STRIP, SHORT) + sum_columns(REACH, REACH)
    columns += high_end_columns() + low_end_columns()
    tables = (
        jnp.asarray(stacked(columns)),
        jnp.asarray(
            np.concatenate([x_table(cells_x), y_table(cells_y), y_end_table(cells_y)], axis=0)
        ),
    )
    vmem, hbm = pl.BlockSpec(memory_space=pltpu.VMEM), pl.BlockSpec(memory_space=pltpu.HBM)
    field = jax.ShapeDtypeStruct(block, jnp.float32)
    field_buffer = pltpu.VMEM(block, jnp.float32)
    ends_shape = (5, planes, cells_y)
    operands = [
        pltpu.with_memory_space_constraint(array, pltpu.HBM)
        for array in (scalar, diffusivity) + tables
    ]
    parts = pl.pallas_call(
        functools.partial(exchange_kernel, counts),
        out_shape=(field,) * 5 + (jax.ShapeDtypeStruct(ends_shape, jnp.float32), jax.ShapeDtypeStruct((4, 32, 128), jnp.float32)),
        in_specs=[hbm] * 4,
        out_specs=(vmem,) * 7,
        scratch_shapes=[field_buffer]
        + [pltpu.VMEM(table.shape, table.dtype) for table in tables]
        + [field_buffer, field_buffer]
        + [pltpu.VMEM((2,) + ends_shape, jnp.float32)] * 2
        + [pltpu.VMEM((2, planes, 8, cells_x), jnp.float32)] * 2
        + [
            pltpu.VMEM(ends_shape, jnp.float32),
            pltpu.SemaphoreType.DMA((9,)),
            pltpu.SemaphoreType.DMA((4,)),
            pltpu.SemaphoreType.DMA((4,)),
            pltpu.SemaphoreType.REGULAR,
            pltpu.SemaphoreType.REGULAR,
            pltpu.SemaphoreType.REGULAR,
        ],
        compiler_params=pltpu.CompilerParams(
            collective_id=0, has_side_effects=True, vmem_limit_bytes=LIMIT
        ),
        name="exchange",
    )(*operands)
    strip_buffer = pltpu.VMEM((planes, STRIP, cells_y), jnp.float32)
    return pl.pallas_call(
        finish_kernel,
        out_shape=(field,) * 3,
        in_specs=[vmem] * 7,
        out_specs=(hbm,) * 3,
        scratch_shapes=[strip_buffer, strip_buffer, pltpu.SemaphoreType.DMA((5,))],
        compiler_params=pltpu.CompilerParams(vmem_limit_bytes=LIMIT),
        name="finish",
    )(*parts)


def solution(mesh):
    placed = P(None, "gx", "gy")
    return jax.shard_map(
        functools.partial(local, (mesh.shape["gx"], mesh.shape["gy"])),
        mesh=mesh,
        in_specs=(placed, placed),
        out_specs=(placed,) * 3,
        check_vma=False,
    )
```
